32 devices in a mesh: group: 2 (over y), seq: 4 (over z), req: 2 (over x), sub: 2 (over core).
Axes of the slice: x: 2, y: 2, z: 4, core: 2. Of those that a mesh axis runs over, the one named last changes fastest.
Arguments:
- latent_codes: bfloat16 [2, 16, 2048, 512], P(None, ('group', 'req', 'sub'), 'seq'), parts along dimension 1, may hold values from -6 to 6
- latent_scales: bfloat16 [2, 16, 2048, 4], P(None, ('group', 'req', 'sub'), 'seq'), parts along dimension 1, may hold values from 0.34 to 3.5
- rope_keys: bfloat16 [2, 16, 2048, 64], P(None, ('group', 'req', 'sub'), 'seq'), parts along dimension 1, may hold values from -6 to 6
- lengths: int32 [16], P(('group', 'req', 'sub')), parts along dimension 0, may hold values from 256 to 2048, as said below
- query_latent: bfloat16 [2, 16, 4, 128, 512], P(None, ('group', 'req', 'sub'), None, 'seq'), parts along dimension 1, may hold values from -64 to 64
- query_rope: bfloat16 [2, 16, 4, 128, 64], P(None, ('group', 'req', 'sub'), None, 'seq'), parts along dimension 1, may hold values from -8 to 8
- new_latent: bfloat16 [2, 16, 4, 512], P(None, ('group', 'req', 'sub')), parts along dimension 1, may hold values from -9 to 9
- new_rope: bfloat16 [2, 16, 4, 64], P(None, ('group', 'req', 'sub')), parts along dimension 1, may hold values from -6 to 6
Outputs:
- attended: bfloat16 [2, 16, 4, 128, 512], P(None, ('group', 'req', 'sub'), None, 'seq'), parts along dimension 1
- cache_codes: bfloat16 [2, 16, 512, 4, 512], P(None, ('group', 'req', 'sub'), None, 'seq'), parts along dimension 1
- cache_scales: bfloat16 [2, 16, 512, 4, 4], P(None, ('group', 'req', 'sub'), None, 'seq'), parts along dimension 1
- cache_rope: bfloat16 [2, 16, 512, 4, 64], P(None, ('group', 'req', 'sub'), None, 'seq'), parts along dimension 1
The draws below stay inside these ranges and needn't reach their ends.
There are 2 independent parts, one for each index of `group`. The reference program is written for one: setup_inputs(seed, part) draws one part's arguments, and reference() takes and returns one part's arrays. A program takes and returns all parts, laid end to end along the dimension named above; each array names one. Nothing has to cross between parts.
Inputs may be any that keep to these rules, and one draw needn't show every extreme that they name: `lengths`: one request is exactly 2048 long.
All inputs are finite; a program needn't handle non-finite values.
Results may differ from the reference program's by a relative error of at most 0.013.
Values may be sent and summed in bfloat16 or wider, within the bound.
A program may use at most 64 MiB of HBM per device.

```python
import jax
import jax.numpy as jnp
from jax import lax

LAT = 512
ROPE = 64
HEADS = 128
BLK = 128
LAYERS = 2
DEC = 4
REQS = 8
S_MAX = 2048
N_SEQ = 4


def head_positions(key):
    codes_head = jax.random.normal(jax.random.fold_in(key, 101), (LAYERS, REQS, 2, LAT), jnp.float32)
    codes_head = jnp.clip(codes_head, -6.0, 6.0)
    scales_head = jnp.exp(jax.random.uniform(jax.random.fold_in(key, 103), (LAYERS, REQS, 2, LAT // BLK), jnp.float32, jnp.log(0.35), jnp.log(3.5)))
    return (codes_head, scales_head)


def new_keys_of(key):
    values = 1.5 * jax.random.normal(jax.random.fold_in(key, 106), (LAYERS, REQS, DEC, LAT), jnp.float32)
    return jnp.clip(values, -9.0, 9.0)


def draw_latent_codes(key, part):
    codes_head, scales_head = head_positions(key)
    rest = jax.random.normal(jax.random.fold_in(key, 104), (LAYERS, REQS, S_MAX - 2, LAT), jnp.float32)
    whole = jnp.concatenate([codes_head, jnp.clip(rest, -6.0, 6.0)], axis=2)
    return whole.astype(jnp.bfloat16)


def draw_latent_scales(key, part):
    codes_head, scales_head = head_positions(key)
    rest = jnp.exp(jax.random.uniform(jax.random.fold_in(key, 105), (LAYERS, REQS, S_MAX - 2, LAT // BLK), jnp.float32, jnp.log(0.35), jnp.log(3.5)))
    whole = jnp.concatenate([scales_head, rest], axis=2)
    return jnp.clip(whole, 0.35, 3.5).astype(jnp.bfloat16)


def draw_new_latent(key, part):
    return new_keys_of(key).astype(jnp.bfloat16)


def draw_query_latent(key, part):
    noise = 1.3 * jax.random.normal(jax.random.fold_in(key, 107), (LAYERS, REQS, DEC, HEADS, LAT), jnp.float32)
    values = noise + 0.2 * new_keys_of(key)[:, :, :, None, :]
    return jnp.clip(values, -64.0, 64.0).astype(jnp.bfloat16)


def draw_lengths(key, part):
    values = jax.random.randint(jax.random.fold_in(key, 109), (REQS,), S_MAX // 8, S_MAX + 1)
    longest = jax.random.randint(jax.random.fold_in(key, 110), (), 0, REQS)
    return jnp.where(jnp.arange(REQS, dtype=jnp.int32) == longest, S_MAX, values).astype(jnp.int32)


def levels(key, shape, cuts, smallest, high):
    def one(dim, shards_of):
        draws = jax.random.uniform(jax.random.fold_in(jax.random.fold_in(key, 6), dim), (shards_of,), jnp.float32, smallest / len(cuts), high / len(cuts))
        return jnp.repeat(jnp.exp(draws), shape[dim] // shards_of).reshape((-1,) + (1,) * (len(shape) - dim - 1))

    gain = one(*cuts[0])
    for cut in cuts[1:]:
        gain = gain * one(*cut)
    return gain


def normal_values(key, dims, spread, reach, cuts=(), held_as=jnp.bfloat16):
    result = jax.random.normal(key, dims, jnp.float32) * spread
    if len(cuts) > 0:
        result = levels(key, dims, cuts, -0.22, 0.18) * result
    return jnp.clip(result, min=-reach, max=reach).astype(held_as)


def setup_inputs(seed: int = 0, part: int = 0) -> dict:
    streams_of = jax.random.split(jax.random.key(seed), 9)
    part_keys = jax.random.split(jax.random.fold_in(streams_of[8], part), 9)
    return {
        "latent_codes": draw_latent_codes(jax.random.fold_in(jax.random.fold_in(streams_of[8], part), 71), part),
        "latent_scales": draw_latent_scales(jax.random.fold_in(jax.random.fold_in(streams_of[8], part), 71), part),
        "rope_keys": normal_values(part_keys[2], (LAYERS, REQS, S_MAX, ROPE), 1.0, 6.0, ((1, 4), (2, 4))),
        "lengths": draw_lengths(jax.random.fold_in(jax.random.fold_in(streams_of[8], part), 71), part),
        "query_latent": draw_query_latent(jax.random.fold_in(jax.random.fold_in(streams_of[8], part), 71), part),
        "query_rope": normal_values(part_keys[5], (LAYERS, REQS, DEC, HEADS, ROPE), 1.3, 8.0, ((1, 4), (3, 4))),
        "new_latent": draw_new_latent(jax.random.fold_in(jax.random.fold_in(streams_of[8], part), 71), part),
        "new_rope": normal_values(part_keys[7], (LAYERS, REQS, DEC, ROPE), 1.0, 6.0, ((1, 4),)),
    }


softmax_gain = 192.0 ** -0.5
masked_score = -1.0e30


def dequantize(code_values, scale_values):
    blocks = scale_values.shape[-1]
    latent_width = code_values.shape[-1]
    shaped = code_values.astype(jnp.float32).reshape(code_values.shape[:-1] + (blocks, latent_width // blocks))
    scaled = shaped * scale_values.astype(jnp.float32)[..., None]
    return scaled.reshape(code_values.shape).astype(jnp.bfloat16)


def shard_partial(lat_query, rope_query, key_rows, rope_rows, usable, new_keys, new_rope_rows, holds_new):
    tokens_new, head_count, latent_width = lat_query.shape
    query_rows = lat_query.reshape(tokens_new * head_count, latent_width)
    query_pos = rope_query.reshape(tokens_new * head_count, rope_query.shape[-1])
    scores = jnp.dot(query_rows, key_rows.T, preferred_element_type=jnp.float32)
    scores = (scores + jnp.dot(query_pos, rope_rows.T, preferred_element_type=jnp.float32)) * softmax_gain
    fresh_scores = jnp.dot(query_rows, new_keys.T, preferred_element_type=jnp.float32)
    fresh_scores = (fresh_scores + jnp.dot(query_pos, new_rope_rows.T, preferred_element_type=jnp.float32)) * softmax_gain
    token_of_row = jnp.arange(tokens_new * head_count, dtype=jnp.int32) // head_count
    causal = (jnp.arange(tokens_new, dtype=jnp.int32)[None, :] <= token_of_row[:, None]) & holds_new
    scores = jnp.where(usable[None, :], scores, masked_score)
    fresh_scores = jnp.where(causal, fresh_scores, masked_score)
    group_peak = jnp.maximum(jnp.max(scores, 1), jnp.max(fresh_scores, 1)).astype(jnp.bfloat16)
    peak_float = group_peak.astype(jnp.float32)[:, None]
    weights = jnp.where(usable[None, :], jnp.exp(scores - peak_float), 0.0).astype(jnp.bfloat16)
    fresh_weights = jnp.where(causal, jnp.exp(fresh_scores - peak_float), 0.0).astype(jnp.bfloat16)
    group_total = jnp.sum(weights.astype(jnp.float32), 1) + jnp.sum(fresh_weights.astype(jnp.float32), 1)
    group_sum = jnp.dot(weights, key_rows, preferred_element_type=jnp.float32)
    group_sum = group_sum + jnp.dot(fresh_weights, new_keys, preferred_element_type=jnp.float32)
    return (group_sum.astype(jnp.bfloat16).reshape(tokens_new, head_count, latent_width),
            group_peak.reshape(tokens_new, head_count),
            group_total.astype(jnp.bfloat16).reshape(tokens_new, head_count))


def merge_groups(pieces):
    group_sum, group_peak, group_total = pieces
    peak_float = group_peak.astype(jnp.float32)
    overall = jnp.max(peak_float, 0)
    factor = jnp.exp(peak_float - overall)
    numerator = jnp.sum(factor[..., None] * group_sum.astype(jnp.float32), 0)
    denominator = jnp.sum(factor * group_total.astype(jnp.float32), 0)
    return (numerator / denominator[..., None]).astype(jnp.bfloat16)


def reference(latent_codes, latent_scales, rope_keys, lengths, query_latent, query_rope, new_latent, new_rope):
    shard_count = N_SEQ
    layer_count, request_count, full_length, latent_width = latent_codes.shape
    span = full_length // shard_count

    def regroup_rows(values):
        return values.reshape(layer_count, request_count, span, shard_count, values.shape[-1])

    cache_codes = regroup_rows(latent_codes)
    cache_scales = regroup_rows(latent_scales)
    cache_rope = regroup_rows(rope_keys)
    pair_count = layer_count * request_count

    def flatten_pairs(values):
        return values.reshape((pair_count,) + values.shape[2:])

    pair_lengths = jnp.tile(lengths, layer_count)
    groups = jnp.arange(shard_count, dtype=jnp.int32)
    offsets = jnp.arange(span, dtype=jnp.int32)
    positions = offsets[None, :] * shard_count + groups[:, None]
    holds_new = groups == 0

    def per_pair(inputs):
        codes_pair, scales_pair, rope_pair, length_pair, lat_query, rope_query, new_keys, new_rope_pair = inputs
        key_rows = jnp.swapaxes(dequantize(codes_pair, scales_pair), 0, 1)
        rope_rows = jnp.swapaxes(rope_pair, 0, 1)
        usable = positions < length_pair

        def per_group(group_inputs):
            key_group, rope_group, usable_group, holds_group = group_inputs
            return shard_partial(lat_query, rope_query, key_group, rope_group, usable_group, new_keys, new_rope_pair, holds_group)

        partial_sums = lax.map(per_group, (key_rows, rope_rows, usable, holds_new))
        return merge_groups(partial_sums)

    attended = lax.map(per_pair, (flatten_pairs(cache_codes), flatten_pairs(cache_scales), flatten_pairs(cache_rope),
                                  pair_lengths, flatten_pairs(query_latent), flatten_pairs(query_rope),
                                  flatten_pairs(new_latent), flatten_pairs(new_rope)))
    attended = attended.reshape(query_latent.shape)
    return (attended, cache_codes, cache_scales, cache_rope)
```

```python
import jax
import jax.numpy as jnp
from jax import lax
from jax.experimental import pallas as pl
from jax.experimental.pallas import tpu as pltpu
from jax.sharding import PartitionSpec as P

softmax_gain = 192.0 ** (-0.5)
masked_score = -1e30


def dequantize(code_values, scale_values):
    blocks = scale_values.shape[-1]
    latent_width = code_values.shape[-1]
    shaped = code_values.astype(jnp.float32).reshape(
        code_values.shape[:-1] + (blocks, latent_width // blocks)
    )
    scaled = shaped * scale_values.astype(jnp.float32)[..., None]
    return scaled.reshape(code_values.shape).astype(jnp.bfloat16)


def shard_partial(
    lat_query, rope_query, key_rows, rope_rows, usable, new_keys, new_rope_rows, holds_new
):
    tokens_new, head_count, latent_width = lat_query.shape
    query_rows = lat_query.reshape(tokens_new * head_count, latent_width)
    query_pos = rope_query.reshape(tokens_new * head_count, rope_query.shape[-1])
    scores = jnp.dot(query_rows, key_rows.T, preferred_element_type=jnp.float32)
    scores = (
        scores + jnp.dot(query_pos, rope_rows.T, preferred_element_type=jnp.float32)
    ) * softmax_gain
    fresh_scores = jnp.dot(query_rows, new_keys.T, preferred_element_type=jnp.float32)
    fresh_scores = (
        fresh_scores + jnp.dot(query_pos, new_rope_rows.T, preferred_element_type=jnp.float32)
    ) * softmax_gain
    token_of_row = jnp.arange(tokens_new * head_count, dtype=jnp.int32) // head_count
    causal = (jnp.arange(tokens_new, dtype=jnp.int32)[None, :] <= token_of_row[:, None]) & holds_new
    scores = jnp.where(usable[None, :], scores, masked_score)
    fresh_scores = jnp.where(causal, fresh_scores, masked_score)
    group_peak = jnp.maximum(jnp.max(scores, 1), jnp.max(fresh_scores, 1)).astype(jnp.bfloat16)
    peak_float = group_peak.astype(jnp.float32)[:, None]
    weights = jnp.where(usable[None, :], jnp.exp(scores - peak_float), 0.0).astype(jnp.bfloat16)
    fresh_weights = jnp.where(causal, jnp.exp(fresh_scores - peak_float), 0.0).astype(jnp.bfloat16)
    group_total = jnp.sum(weights.astype(jnp.float32), 1) + jnp.sum(
        fresh_weights.astype(jnp.float32), 1
    )
    group_sum = jnp.dot(weights, key_rows, preferred_element_type=jnp.float32)
    group_sum = group_sum + jnp.dot(fresh_weights, new_keys, preferred_element_type=jnp.float32)
    return (
        group_sum.astype(jnp.bfloat16).reshape(tokens_new, head_count, latent_width),
        group_peak.reshape(tokens_new, head_count),
        group_total.astype(jnp.bfloat16).reshape(tokens_new, head_count),
    )


def merge_groups(pieces):
    group_sum, group_peak, group_total = pieces
    peak_float = group_peak.astype(jnp.float32)
    overall = jnp.max(peak_float, 0)
    factor = jnp.exp(peak_float - overall)
    numerator = jnp.sum(factor[..., None] * group_sum.astype(jnp.float32), 0)
    denominator = jnp.sum(factor * group_total.astype(jnp.float32), 0)
    return (numerator / denominator[..., None]).astype(jnp.bfloat16)


def per_device(
    latent_codes, latent_scales, rope_keys, lengths, query_latent, query_rope, new_latent, new_rope
):
    shard_count = lax.axis_size("seq")
    seq_index = lax.axis_index("seq")
    layer_count, request_count, span, latent_width = latent_codes.shape
    lat_query, rope_query = (
        lax.all_gather(query_latent, "seq", axis=3, tiled=True),
        lax.all_gather(query_rope, "seq", axis=3, tiled=True),
    )

    def regroup_rows(values):
        return values.reshape(
            values.shape[0], values.shape[1], span // shard_count, shard_count, values.shape[-1]
        )

    codes_moved, scales_moved, rope_moved = (
        lax.all_to_all(regroup_rows(latent_codes), "seq", split_axis=3, concat_axis=2, tiled=True),
        lax.all_to_all(regroup_rows(latent_scales), "seq", split_axis=3, concat_axis=2, tiled=True),
        lax.all_to_all(regroup_rows(rope_keys), "seq", split_axis=3, concat_axis=2, tiled=True),
    )
    offsets = jnp.arange(span, dtype=jnp.int32)
    key_rows = dequantize(latent_codes, latent_scales)
    positions = seq_index * span + offsets
    usable = positions[None, :] < lengths[:, None]
    holds_new = seq_index == 0
    per_request = jax.vmap(shard_partial, in_axes=(0, 0, 0, 0, 0, 0, 0, None))
    per_layer = jax.vmap(per_request, in_axes=(0, 0, 0, 0, None, 0, 0, None))
    group_sum, group_peak, group_total = per_layer(
        lat_query, rope_query, key_rows, rope_keys, usable, new_latent, new_rope, holds_new
    )
    attended = merge_groups(
        (
            lax.all_to_all(group_sum[None], "seq", split_axis=4, concat_axis=0, tiled=True),
            lax.all_to_all(group_peak[None], "seq", split_axis=4, concat_axis=0, tiled=True),
            lax.all_to_all(group_total[None], "seq", split_axis=4, concat_axis=0, tiled=True),
        )
    )
    return (attended, codes_moved, scales_moved, rope_moved)


def _exchange_kernel(
    len_ref, codes_ref, rope_ref, scale_ref, q_ref, qr_ref, new_ref, newr_ref,
    att_ref, cache_ref, crope_ref, cscale_ref,
    perm, kbuf, abuf, scale_in, raw, rawr, raws, qbuf, qrbuf, nkbuf, nrbuf, keys, result,
    own_sum, own_stat, near_out, near_out_stat, near_in, near_in_stat,
    side_sum, side_stat, far_out, far_out_stat, part_in, part_in_stat, far_in, far_in_stat,
    load_sem, keep_sem, q_send, q_recv, f_send, f_recv, near_send, near_recv,
    far_send, far_recv, part_recv,
):
    pairs, span, width = codes_ref.shape
    groups = 4
    rows = span // groups
    half = q_ref.shape[1]
    rope = qr_ref.shape[2]
    blocks = scale_ref.shape[1]
    fresh = new_ref.shape[1]
    heads = half // fresh
    early = pairs // 2
    me = lax.axis_index("seq")
    inner = (me == 1) | (me == 2)
    outer = jnp.logical_not(inner)
    partner = jnp.where(me < 2, 1 - me, 5 - me)
    across = 3 - me
    far_outer = jnp.where(me < 2, 3, 0)
    f32, bf16 = jnp.float32, jnp.bfloat16

    def start(copies):
        for copy in copies:
            copy.start()

    def remote(src, dst, send, recv, target):
        return pltpu.make_async_remote_copy(
            src_ref=src, dst_ref=dst, send_sem=send, recv_sem=recv,
            device_id={"seq": target}, device_id_type=pl.DeviceIdType.MESH,
        )

    def load(c):
        return (
            pltpu.make_async_copy(codes_ref.at[c], raw.at[c], load_sem.at[0, c]),
            pltpu.make_async_copy(rope_ref.at[c], rawr.at[c], load_sem.at[1, c]),
            pltpu.make_async_copy(scale_ref.at[c], raws.at[c], load_sem.at[2, c]),
            pltpu.make_async_copy(q_ref.at[c], qbuf.at[c, 0], load_sem.at[3, c]),
            pltpu.make_async_copy(qr_ref.at[c], qrbuf.at[c, 0], load_sem.at[4, c]),
        )

    def queries(c, flow, src, dst, target):
        lat = q_ref.at[c] if src == 0 else qbuf.at[c, src]
        rot = qr_ref.at[c] if src == 0 else qrbuf.at[c, src]
        return (
            remote(lat, qbuf.at[c, dst], q_send.at[0, flow, c], q_recv.at[0, dst, c], target),
            remote(rot, qrbuf.at[c, dst], q_send.at[1, flow, c], q_recv.at[1, dst, c], target),
        )

    def to_partner(c):
        return queries(c, 0, 0, 1, partner)

    def own_across(c):
        return queries(c, 1, 0, 2, across)

    def partner_across(c):
        return queries(c, 2, 1, 3, across)

    def relay(c):
        return queries(c, 3, 2, 2, partner) + queries(c, 4, 3, 3, partner)

    def await_queries(c, slot):
        for copy in queries(c, 0, 0, slot, partner):
            copy.wait_recv()

    def handover(c, r):
        target = (me + r) % groups
        spot = pl.multiple_of(me * rows, rows)
        return (
            remote(kbuf.at[c, target], cache_ref.at[c, pl.ds(spot, rows)],
                   f_send.at[0, r - 1, c], f_recv.at[0, r - 1, c], target),
            remote(abuf.at[c, target, pl.ds(0, rope)], crope_ref.at[c, :, pl.ds(spot, rows)],
                   f_send.at[1, r - 1, c], f_recv.at[1, r - 1, c], target),
            remote(abuf.at[c, target, pl.ds(rope, 16)], scale_in.at[c, r - 1],
                   f_send.at[2, r - 1, c], f_recv.at[2, r - 1, c], target),
        )

    def handover_near(c):
        for r in range(1, groups):
            @pl.when((me + r) % groups == partner)
            def _():
                start(handover(c, r))

    def handover_far(c):
        for r in range(1, groups):
            @pl.when((me + r) % groups != partner)
            def _():
                start(handover(c, r))

    def keep(c):
        spot = pl.multiple_of(me * rows, rows)
        return (
            pltpu.make_async_copy(kbuf.at[c, me], cache_ref.at[c, pl.ds(spot, rows)], keep_sem.at[0, c]),
            pltpu.make_async_copy(
                abuf.at[c, me, pl.ds(0, rope)], crope_ref.at[c, :, pl.ds(spot, rows)], keep_sem.at[1, c]
            ),
        )

    def near_result(c):
        return (
            remote(near_out.at[c], near_in.at[c], near_send.at[0, c], near_recv.at[0, c], partner),
            remote(near_out_stat.at[c], near_in_stat.at[c], near_send.at[1, c], near_recv.at[1, c], partner),
        )

    def part_result(c, j):
        return (
            remote(far_out.at[c, j], part_in.at[c, j],
                   far_send.at[0, j, c], part_recv.at[0, j, c], partner),
            remote(far_out_stat.at[c, j], part_in_stat.at[c, j],
                   far_send.at[1, j, c], part_recv.at[1, j, c], partner),
        )

    def far_result(c, j):
        target = across if j == 0 else far_outer
        return (
            remote(far_out.at[c, j], far_in.at[c],
                   far_send.at[0, j, c], far_recv.at[0, c], target),
            remote(far_out_stat.at[c, j], far_in_stat.at[c],
                   far_send.at[1, j, c], far_recv.at[1, c], target),
        )

    def own_result(c):
        return pltpu.make_async_copy(result.at[c], att_ref.at[c], load_sem.at[5, c])

    for c in range(pairs):
        start(load(c))
    for r in range(1, groups):
        pl.semaphore_signal(
            pltpu.get_barrier_semaphore(), inc=1, device_id={"seq": (me + r) % groups},
            device_id_type=pl.DeviceIdType.MESH,
        )
    pl.semaphore_wait(pltpu.get_barrier_semaphore(), groups - 1)

    for c in range(pairs):
        @pl.when(inner)
        def _():
            start(own_across(c))

        start(to_partner(c))

    line = lax.broadcasted_iota(jnp.int32, (span, span), 0)
    place = lax.broadcasted_iota(jnp.int32, (span, span), 1)
    perm[...] = jnp.where(place == (line % rows) * groups + line // rows, 1.0, 0.0).astype(bf16)
    nkbuf[...] = jnp.zeros(nkbuf.shape, bf16)
    nrbuf[...] = jnp.zeros(nrbuf.shape, bf16)
    for c in range(pairs):
        nkbuf[c, 0:fresh, :] = new_ref[c]
        nrbuf[c, 0:fresh, :] = newr_ref[c]
    dims = (((1,), (1,)), ((), ()))

    @pl.loop(0, pairs)
    def _(c):
        for copy in load(c):
            copy.wait()
        sorted_codes = jnp.dot(perm[...], raw[c], preferred_element_type=f32)
        for k in range(groups):
            kbuf[c, k] = sorted_codes[k * rows:(k + 1) * rows].astype(bf16)
        extra = jnp.concatenate(
            [rawr[c].astype(f32), raws[c].astype(f32), jnp.zeros((16 - blocks, span), f32)], axis=0
        ).astype(bf16)
        sorted_extra = lax.dot_general(extra, perm[...], dims, preferred_element_type=f32)
        for k in range(groups):
            abuf[c, k] = sorted_extra[:, k * rows:(k + 1) * rows].astype(bf16)

        @pl.when(inner)
        def _():
            await_queries(c, 1)
            start(partner_across(c))

        handover_near(c)
        start(keep(c))
        mine = abuf[c, me, rope:rope + 16, :].astype(f32)[0:blocks]
        cscale_ref[c, :, pl.ds(pl.multiple_of(me * rows, rows), rows)] = mine.astype(bf16)

    def stats_of(m, d):
        lane = lax.broadcasted_iota(jnp.int32, (half, 128), 1)
        return jnp.where(lane == 0, m, d).T[0:8]

    def columns_of(stat):
        turned = stat.T
        return turned[:, 0:1], turned[:, 1:2]

    def partial(c, first):
        q = qbuf[c, first:first + 2].reshape(2 * half, width)
        qr = qrbuf[c, first:first + 2].reshape(2 * half, rope)
        s = lax.dot_general(q, keys[...], dims, preferred_element_type=f32)
        s = (s + jnp.dot(qr, rawr[c], preferred_element_type=f32)) * softmax_gain
        position = me * span + lax.broadcasted_iota(jnp.int32, (1, span), 1)
        s = jnp.where(position < len_ref[c % len_ref.shape[0]], s, masked_score)
        m = jnp.max(s, axis=1, keepdims=True)
        if first == 0:
            t = lax.dot_general(q, nkbuf[c], dims, preferred_element_type=f32)
            t = (t + lax.dot_general(qr, nrbuf[c], dims, preferred_element_type=f32)) * softmax_gain
            row = lax.broadcasted_iota(jnp.int32, t.shape, 0)
            column = lax.broadcasted_iota(jnp.int32, t.shape, 1)
            t = jnp.where((column <= row // heads) & (row < half), t, masked_score)
            m = jnp.maximum(m, jnp.max(t, axis=1, keepdims=True))
        w = jnp.exp(s - m).astype(bf16)
        d = jnp.sum(w.astype(f32), axis=1, keepdims=True)
        n = jnp.dot(w, keys[...], preferred_element_type=f32)
        if first == 0:
            v = jnp.exp(t - m).astype(bf16)
            d = d + jnp.sum(v.astype(f32), axis=1, keepdims=True)
            n = n + jnp.dot(v, nkbuf[c], preferred_element_type=f32)
        return [
            (n[j * half:(j + 1) * half], stats_of(m[j * half:(j + 1) * half], d[j * half:(j + 1) * half]))
            for j in range(2)
        ]

    def combine(c):
        for j in range(2):
            for copy in part_result(c, j):
                copy.wait_recv()
            m0, d0 = columns_of(side_stat[c, j])
            m1, d1 = columns_of(part_in_stat[c, j])
            m = jnp.maximum(m0, m1)
            f0, f1 = jnp.exp(m0 - m), jnp.exp(m1 - m)
            far_out[c, j] = (f0 * side_sum[c, j] + f1 * part_in[c, j].astype(f32)).astype(bf16)
            far_out_stat[c, j] = stats_of(m, f0 * d0 + f1 * d1)
            start(far_result(c, j))

    @pl.loop(0, pairs)
    def _(c):
        @pl.when(inner)
        def _():
            await_queries(c, 2)
            await_queries(c, 3)
            start(relay(c))

        @pl.when(outer)
        def _():
            await_queries(c, 1)

        scales = jnp.concatenate([raws[c].astype(f32), jnp.zeros((8 - blocks, span), f32)], axis=0).T
        for b in range(blocks):
            lanes = slice(b * (width // blocks), (b + 1) * (width // blocks))
            keys[:, lanes] = (raw[c, :, lanes].astype(f32) * scales[:, b:b + 1]).astype(bf16)

        own, near = partial(c, 0)
        near_out[c], near_out_stat[c] = near[0].astype(bf16), near[1]
        start(near_result(c))
        own_sum[c], own_stat[c] = own

        @pl.when(outer)
        def _():
            await_queries(c, 2)
            await_queries(c, 3)

        far = partial(c, 2)

        @pl.when(outer)
        def _():
            for j in range(2):
                far_out[c, j], far_out_stat[c, j] = far[j][0].astype(bf16), far[j][1]
                start(part_result(c, j))

        @pl.when(inner)
        def _():
            for j in range(2):
                side_sum[c, j], side_stat[c, j] = far[j]

        @pl.when(inner & (c >= 1))
        def _():
            combine(c - 1)

        @pl.when(c < early)
        def _():
            handover_far(c)

    @pl.when(inner)
    def _():
        combine(pairs - 1)

    @pl.loop(early, pairs)
    def _(c):
        handover_far(c)

    @pl.loop(0, pairs)
    def _(c):
        for copy in near_result(c) + far_result(c, 0):
            copy.wait_recv()
        m0, d0 = columns_of(own_stat[c])
        m1, d1 = columns_of(near_in_stat[c])
        m2, d2 = columns_of(far_in_stat[c])
        m = jnp.maximum(m0, jnp.maximum(m1, m2))
        f0, f1, f2 = jnp.exp(m0 - m), jnp.exp(m1 - m), jnp.exp(m2 - m)
        numerator = f0 * own_sum[c] + f1 * near_in[c].astype(f32) + f2 * far_in[c].astype(f32)
        result[c] = (numerator / (f0 * d0 + f1 * d1 + f2 * d2)).astype(bf16)
        own_result(c).start()

    @pl.loop(0, pairs)
    def _(c):
        for r in range(1, groups):
            for copy in handover(c, r):
                copy.wait()
            spot = pl.multiple_of((me + groups - r) % groups * rows, rows)
            got = scale_in[c, r - 1].astype(f32)[0:blocks]
            cscale_ref[c, :, pl.ds(spot, rows)] = got.astype(bf16)
        for copy in keep(c):
            copy.wait()
        own_result(c).wait()
        for copy in to_partner(c) + near_result(c):
            copy.wait_send()

        @pl.when(outer)
        def _():
            for copy in part_result(c, 0) + part_result(c, 1):
                copy.wait_send()

        @pl.when(inner)
        def _():
            for copy in own_across(c) + partner_across(c) + relay(c):
                copy.wait_send()
            for copy in far_result(c, 0) + far_result(c, 1):
                copy.wait_send()


def per_device_line(
    latent_codes, latent_scales, rope_keys, lengths, query_latent, query_rope, new_latent, new_rope
):
    layers, requests, span, width = latent_codes.shape
    pairs, rows = layers * requests, span // 4
    rope, blocks = rope_keys.shape[-1], latent_scales.shape[-1]
    tokens, heads = query_latent.shape[2:4]
    half = tokens * heads
    hbm_spec = pl.BlockSpec(memory_space=pltpu.HBM)
    any_spec = pl.BlockSpec(memory_space=pl.ANY)
    vmem_spec = pl.BlockSpec(memory_space=pltpu.VMEM)
    dma = pltpu.SemaphoreType.DMA
    bf16, f32 = jnp.bfloat16, jnp.float32
    att, cache, crope, cscale = pl.pallas_call(
        _exchange_kernel,
        out_shape=(
            jax.ShapeDtypeStruct((pairs, half, width), bf16),
            jax.ShapeDtypeStruct((pairs, span, width), bf16),
            jax.ShapeDtypeStruct((pairs, rope, span), bf16),
            jax.ShapeDtypeStruct((pairs, blocks, span), bf16),
        ),
        in_specs=[pl.BlockSpec(memory_space=pltpu.SMEM)] + [hbm_spec] * 5 + [vmem_spec] * 2,
        out_specs=(any_spec, any_spec, any_spec, vmem_spec),
        scratch_shapes=[
            pltpu.VMEM((span, span), bf16),
            pltpu.VMEM((pairs, 4, rows, width), bf16),
            pltpu.VMEM((pairs, 4, rope + 16, rows), bf16),
            pltpu.VMEM((pairs, 3, 16, rows), bf16),
            pltpu.VMEM((pairs, span, width), bf16),
            pltpu.VMEM((pairs, rope, span), bf16),
            pltpu.VMEM((pairs, blocks, span), bf16),
            pltpu.VMEM((pairs, 4, half, width), bf16),
            pltpu.VMEM((pairs, 4, half, rope), bf16),
            pltpu.VMEM((pairs, 128, width), bf16),
            pltpu.VMEM((pairs, 128, rope), bf16),
            pltpu.VMEM((span, width), bf16),
            pltpu.VMEM((pairs, half, width), bf16),
            pltpu.VMEM((pairs, half, width), f32),
            pltpu.VMEM((pairs, 8, 128), f32),
            pltpu.VMEM((pairs, half, width), bf16),
            pltpu.VMEM((pairs, 8, 128), f32),
            pltpu.VMEM((pairs, half, width), bf16),
            pltpu.VMEM((pairs, 8, 128), f32),
            pltpu.VMEM((pairs, 2, half, width), f32),
            pltpu.VMEM((pairs, 2, 8, 128), f32),
            pltpu.VMEM((pairs, 2, half, width), bf16),
            pltpu.VMEM((pairs, 2, 8, 128), f32),
            pltpu.VMEM((pairs, 2, half, width), bf16),
            pltpu.VMEM((pairs, 2, 8, 128), f32),
            pltpu.VMEM((pairs, half, width), bf16),
            pltpu.VMEM((pairs, 8, 128), f32),
            dma((6, pairs)), dma((2, pairs)), dma((2, 5, pairs)), dma((2, 4, pairs)),
            dma((3, 3, pairs)), dma((3, 3, pairs)), dma((2, pairs)), dma((2, pairs)),
            dma((2, 2, pairs)), dma((2, pairs)), dma((2, 2, pairs)),
        ],
        compiler_params=pltpu.CompilerParams(
            collective_id=0, has_side_effects=True, vmem_limit_bytes=60 << 20
        ),
    )(
        lengths, latent_codes.reshape(pairs, span, width),
        rope_keys.transpose(0, 1, 3, 2).reshape(pairs, rope, span),
        latent_scales.transpose(0, 1, 3, 2).reshape(pairs, blocks, span),
        query_latent.reshape(pairs, half, width), query_rope.reshape(pairs, half, rope),
        new_latent.reshape(pairs, tokens, width), new_rope.reshape(pairs, tokens, rope),
    )

    def as_cache(values):
        flipped = values.reshape(layers, requests, values.shape[1], span).transpose(0, 1, 3, 2)
        return flipped.reshape(layers, requests, span, 1, values.shape[1])

    return (
        att.reshape(query_latent.shape),
        cache.reshape(layers, requests, span, 1, width),
        as_cache(cscale),
        as_cache(crope),
    )


def solution(mesh):
    placed = (
        P(None, ("group", "req", "sub"), "seq", None),
        P(None, ("group", "req", "sub"), "seq", None),
        P(None, ("group", "req", "sub"), "seq", None),
        P(("group", "req", "sub")),
        P(None, ("group", "req", "sub"), None, "seq", None),
        P(None, ("group", "req", "sub"), None, "seq", None),
        P(None, ("group", "req", "sub"), None, None),
        P(None, ("group", "req", "sub"), None, None),
    )
    return jax.shard_map(
        per_device_line if mesh.shape["seq"] == 4 else per_device,
        mesh=mesh,
        in_specs=placed,
        out_specs=(
            P(None, ("group", "req", "sub"), None, "seq", None),
            P(None, ("group", "req", "sub"), None, "seq", None),
            P(None, ("group", "req", "sub"), None, "seq", None),
            P(None, ("group", "req", "sub"), None, "seq", None),
        ),
        check_vma=False,
    )
```

```python
import jax
import jax.numpy as jnp
from jax import lax
from jax.experimental import pallas as pl
from jax.experimental.pallas import tpu as pltpu
from jax.sharding import PartitionSpec as P

softmax_gain = 192.0 ** (-0.5)
masked_score = -1e30


def dequantize(code_values, scale_values):
    blocks = scale_values.shape[-1]
    latent_width = code_values.shape[-1]
    shaped = code_values.astype(jnp.float32).reshape(
        code_values.shape[:-1] + (blocks, latent_width // blocks)
    )
    scaled = shaped * scale_values.astype(jnp.float32)[..., None]
    return scaled.reshape(code_values.shape).astype(jnp.bfloat16)


def shard_partial(
    lat_query, rope_query, key_rows, rope_rows, usable, new_keys, new_rope_rows, holds_new
):
    tokens_new, head_count, latent_width = lat_query.shape
    query_rows = lat_query.reshape(tokens_new * head_count, latent_width)
    query_pos = rope_query.reshape(tokens_new * head_count, rope_query.shape[-1])
    scores = jnp.dot(query_rows, key_rows.T, preferred_element_type=jnp.float32)
    scores = (
        scores + jnp.dot(query_pos, rope_rows.T, preferred_element_type=jnp.float32)
    ) * softmax_gain
    fresh_scores = jnp.dot(query_rows, new_keys.T, preferred_element_type=jnp.float32)
    fresh_scores = (
        fresh_scores + jnp.dot(query_pos, new_rope_rows.T, preferred_element_type=jnp.float32)
    ) * softmax_gain
    token_of_row = jnp.arange(tokens_new * head_count, dtype=jnp.int32) // head_count
    causal = (jnp.arange(tokens_new, dtype=jnp.int32)[None, :] <= token_of_row[:, None]) & holds_new
    scores = jnp.where(usable[None, :], scores, masked_score)
    fresh_scores = jnp.where(causal, fresh_scores, masked_score)
    group_peak = jnp.maximum(jnp.max(scores, 1), jnp.max(fresh_scores, 1)).astype(jnp.bfloat16)
    peak_float = group_peak.astype(jnp.float32)[:, None]
    weights = jnp.where(usable[None, :], jnp.exp(scores - peak_float), 0.0).astype(jnp.bfloat16)
    fresh_weights = jnp.where(causal, jnp.exp(fresh_scores - peak_float), 0.0).astype(jnp.bfloat16)
    group_total = jnp.sum(weights.astype(jnp.float32), 1) + jnp.sum(
        fresh_weights.astype(jnp.float32), 1
    )
    group_sum = jnp.dot(weights, key_rows, preferred_element_type=jnp.float32)
    group_sum = group_sum + jnp.dot(fresh_weights, new_keys, preferred_element_type=jnp.float32)
    return (
        group_sum.astype(jnp.bfloat16).reshape(tokens_new, head_count, latent_width),
        group_peak.reshape(tokens_new, head_count),
        group_total.astype(jnp.bfloat16).reshape(tokens_new, head_count),
    )


def merge_groups(pieces):
    group_sum, group_peak, group_total = pieces
    peak_float = group_peak.astype(jnp.float32)
    overall = jnp.max(peak_float, 0)
    factor = jnp.exp(peak_float - overall)
    numerator = jnp.sum(factor[..., None] * group_sum.astype(jnp.float32), 0)
    denominator = jnp.sum(factor * group_total.astype(jnp.float32), 0)
    return (numerator / denominator[..., None]).astype(jnp.bfloat16)


def per_device(
    latent_codes, latent_scales, rope_keys, lengths, query_latent, query_rope, new_latent, new_rope
):
    shard_count = lax.axis_size("seq")
    seq_index = lax.axis_index("seq")
    layer_count, request_count, span, latent_width = latent_codes.shape
    lat_query, rope_query = (
        lax.all_gather(query_latent, "seq", axis=3, tiled=True),
        lax.all_gather(query_rope, "seq", axis=3, tiled=True),
    )

    def regroup_rows(values):
        return values.reshape(
            values.shape[0], values.shape[1], span // shard_count, shard_count, values.shape[-1]
        )

    codes_moved, scales_moved, rope_moved = (
        lax.all_to_all(regroup_rows(latent_codes), "seq", split_axis=3, concat_axis=2, tiled=True),
        lax.all_to_all(regroup_rows(latent_scales), "seq", split_axis=3, concat_axis=2, tiled=True),
        lax.all_to_all(regroup_rows(rope_keys), "seq", split_axis=3, concat_axis=2, tiled=True),
    )
    offsets = jnp.arange(span, dtype=jnp.int32)
    key_rows = dequantize(latent_codes, latent_scales)
    positions = seq_index * span + offsets
    usable = positions[None, :] < lengths[:, None]
    holds_new = seq_index == 0
    per_request = jax.vmap(shard_partial, in_axes=(0, 0, 0, 0, 0, 0, 0, None))
    per_layer = jax.vmap(per_request, in_axes=(0, 0, 0, 0, None, 0, 0, None))
    group_sum, group_peak, group_total = per_layer(
        lat_query, rope_query, key_rows, rope_keys, usable, new_latent, new_rope, holds_new
    )
    attended = merge_groups(
        (
            lax.all_to_all(group_sum[None], "seq", split_axis=4, concat_axis=0, tiled=True),
            lax.all_to_all(group_peak[None], "seq", split_axis=4, concat_axis=0, tiled=True),
            lax.all_to_all(group_total[None], "seq", split_axis=4, concat_axis=0, tiled=True),
        )
    )
    return (attended, codes_moved, scales_moved, rope_moved)


def _hub_kernel(
    len_ref, codes_ref, rope_ref, scale_ref, q_ref, qr_ref, new_ref, newr_ref,
    att_ref, cache_ref, crope_ref, cscale_ref,
    perm, kbuf, abuf, sbuf, scale_in, scale_rows, raw, rawr, raws, rawq, qbuf, qrbuf, nkbuf, nrbuf,
    keys, result, side_sum, side_stat, far_out, far_out_stat, far_in, far_in_stat,
    load_sem, keep_sem, q_send, q_recv, k_send, k_recv, f_send, f_recv, s_send, s_recv,
    far_send, far_recv, r_send, r_recv,
):
    pairs, span, width = codes_ref.shape
    groups = 4
    rows = span // groups
    half = q_ref.shape[1]
    rope = qr_ref.shape[2]
    blocks = scale_ref.shape[1]
    fresh = new_ref.shape[1]
    heads = half // fresh
    fold = half * rope // 128
    me = lax.axis_index("seq")
    is_hub = (me == 1) | (me == 2)
    is_edge = jnp.logical_not(is_hub)
    hub = 1 + me // 2
    edge = me // 2 * 3
    across = 3 - hub
    far_edge = 3 - edge
    f32, bf16 = jnp.float32, jnp.bfloat16

    def start(copies):
        for copy in copies:
            copy.start()

    def remote(src, dst, send, recv, target):
        return pltpu.make_async_remote_copy(
            src_ref=src, dst_ref=dst, send_sem=send, recv_sem=recv,
            device_id={"seq": target}, device_id_type=pl.DeviceIdType.MESH,
        )

    def greet(target):
        pl.semaphore_signal(
            pltpu.get_barrier_semaphore(), inc=1, device_id={"seq": target},
            device_id_type=pl.DeviceIdType.MESH,
        )

    def load(c):
        return (
            pltpu.make_async_copy(codes_ref.at[c], raw.at[c], load_sem.at[0, c]),
            pltpu.make_async_copy(rope_ref.at[c], rawr.at[c], load_sem.at[1, c]),
        )

    def load_scales(c):
        return pltpu.make_async_copy(scale_ref.at[c], raws.at[c], load_sem.at[2, c])

    def load_rotary(c):
        return pltpu.make_async_copy(qr_ref.at[c], rawq.at[c], load_sem.at[4, c])

    def load_query(c):
        return pltpu.make_async_copy(q_ref.at[c], qbuf.at[c, 0], load_sem.at[3, c])

    def query_latent(c, flow, src, dst, target):
        return remote(q_ref.at[c] if src == 0 else qbuf.at[c, src], qbuf.at[c, dst],
                      q_send.at[0, flow, c], q_recv.at[0, dst, c], target)

    def query_rotary(c, flow, src, dst, target):
        return remote(qrbuf.at[c, src], qrbuf.at[c, dst],
                      q_send.at[1, flow, c], q_recv.at[1, dst, c], target)

    def queries(c, flow, src, dst, target):
        return (query_latent(c, flow, src, dst, target), query_rotary(c, flow, src, dst, target))

    def await_queries(c, slot):
        for copy in queries(c, 0, 0, slot, across):
            copy.wait_recv()

    def shard(c):
        return (
            remote(abuf.at[0, c], abuf.at[1, c], k_send.at[0, c], k_recv.at[0, c], hub),
            remote(kbuf.at[0, c], kbuf.at[1, c], k_send.at[1, c], k_recv.at[1, c], hub),
        )

    def shard_scales():
        return remote(sbuf.at[0], sbuf.at[1], s_send.at[2, 0], s_recv.at[groups], hub)

    def place_of(slot):
        return hub if slot == 0 else edge

    def handover(slot, c, target, lane):
        place = place_of(slot)
        spot = pl.multiple_of(place * rows, rows)
        return (
            remote(kbuf.at[slot, c, target], cache_ref.at[c, pl.ds(spot, rows)],
                   f_send.at[0, slot, lane, c], f_recv.at[0, place, c], target),
            remote(abuf.at[slot, c, target], crope_ref.at[c, :, pl.ds(spot, rows)],
                   f_send.at[1, slot, lane, c], f_recv.at[1, place, c], target),
        )

    def handover_far(slot, c):
        return handover(slot, c, far_edge, 1) + handover(slot, c, across, 0)

    def handover_scales(slot, target, lane):
        return remote(sbuf.at[slot, target], scale_in.at[place_of(slot)],
                      s_send.at[slot, lane], s_recv.at[place_of(slot)], target)

    def await_handover(c, place):
        spot = pl.multiple_of(place * rows, rows)
        remote(kbuf.at[0, c, 0], cache_ref.at[c, pl.ds(spot, rows)],
               f_send.at[0, 0, 0, c], f_recv.at[0, place, c], across).wait_recv()
        remote(abuf.at[0, c, 0], crope_ref.at[c, :, pl.ds(spot, rows)],
               f_send.at[1, 0, 0, c], f_recv.at[1, place, c], across).wait_recv()

    def keep_scales(tile, place):
        values = tile.astype(f32)
        for c in range(pairs):
            cscale_ref[c, :, pl.ds(pl.multiple_of(place * rows, rows), rows)] = (
                values[c * blocks:(c + 1) * blocks].astype(bf16)
            )

    def await_scales(place):
        remote(sbuf.at[0, 0], scale_in.at[place], s_send.at[0, 0], s_recv.at[place], across).wait_recv()
        keep_scales(scale_in[place], place)

    def keep(slot, c, place):
        spot = pl.multiple_of(place * rows, rows)
        return (
            pltpu.make_async_copy(
                kbuf.at[slot, c, me], cache_ref.at[c, pl.ds(spot, rows)], keep_sem.at[0, slot, c]
            ),
            pltpu.make_async_copy(
                abuf.at[slot, c, me], crope_ref.at[c, :, pl.ds(spot, rows)], keep_sem.at[1, slot, c]
            ),
        )

    def sums(c):
        return (
            remote(far_out.at[c], far_in.at[c], far_send.at[0, c], far_recv.at[0, c], across),
            remote(far_out_stat.at[c], far_in_stat.at[c], far_send.at[1, c], far_recv.at[1, c], across),
        )

    def own_result(c):
        return pltpu.make_async_copy(result.at[c, 0], att_ref.at[c], load_sem.at[5, c])

    def edge_result(c):
        return remote(result.at[c, 1], att_ref.at[c], r_send.at[c], r_recv.at[c], edge)

    for c in range(pairs):
        load_rotary(c).start()
    for c in range(pairs):
        load_scales(c).start()
        start(load(c))

    @pl.when(is_hub)
    def _():
        for c in range(pairs):
            load_query(c).start()
        greet(across)
        greet(edge)
        pl.semaphore_wait(pltpu.get_barrier_semaphore(), 3)
        for c in range(pairs):
            query_latent(c, 1, 0, 2, across).start()

    @pl.when(is_edge)
    def _():
        greet(hub)
        greet(across)
        pl.semaphore_wait(pltpu.get_barrier_semaphore(), 1)
        for c in range(pairs):
            query_latent(c, 0, 0, 1, hub).start()

    for c in range(pairs):
        load_rotary(c).wait()
        qrbuf[c, 0] = jnp.concatenate(
            [rawq[c, i * fold:(i + 1) * fold, :] for i in range(half // fold)], axis=1
        )

    @pl.when(is_hub)
    def _():
        for c in range(pairs):
            query_rotary(c, 1, 0, 2, across).start()

    @pl.when(is_edge)
    def _():
        for c in range(pairs):
            query_rotary(c, 0, 0, 1, hub).start()

    line = lax.broadcasted_iota(jnp.int32, (span, span), 0)
    column = lax.broadcasted_iota(jnp.int32, (span, span), 1)
    perm[...] = jnp.where(column == (line % rows) * groups + line // rows, 1.0, 0.0).astype(bf16)
    dims = (((1,), (1,)), ((), ()))

    tile_rows = sbuf.shape[2]
    for c in range(pairs):
        load_scales(c).wait()
    stacked = [raws[c].astype(f32) for c in range(pairs)]
    if tile_rows > pairs * blocks:
        stacked.append(jnp.zeros((tile_rows - pairs * blocks, span), f32))
    stacked = jnp.concatenate(stacked, axis=0).astype(bf16)
    sorted_scales = lax.dot_general(stacked, perm[...], dims, preferred_element_type=f32)
    for k in range(groups):
        sbuf[0, k] = sorted_scales[:, k * rows:(k + 1) * rows].astype(bf16)
    keep_scales(sbuf[0, me], me)

    def spread_scales(slot):
        scale_rows[slot] = jnp.zeros(scale_rows.shape[1:], f32)
        for k in range(groups):
            values = sbuf[slot, k].astype(f32)
            for c in range(pairs):
                scale_rows[slot, c, 0:blocks, k * rows:(k + 1) * rows] = (
                    values[c * blocks:(c + 1) * blocks]
                )

    def prepare(c):
        for copy in load(c):
            copy.wait()
        sorted_codes = jnp.dot(perm[...], raw[c], preferred_element_type=f32)
        for k in range(groups):
            kbuf[0, c, k] = sorted_codes[k * rows:(k + 1) * rows].astype(bf16)
        sorted_rope = lax.dot_general(rawr[c], perm[...], dims, preferred_element_type=f32)
        for k in range(groups):
            abuf[0, c, k] = sorted_rope[:, k * rows:(k + 1) * rows].astype(bf16)

    def stats_of(m, d):
        lane = lax.broadcasted_iota(jnp.int32, (half, 128), 1)
        return jnp.where(lane == 0, m, d).T[0:8]

    def columns_of(stat):
        turned = stat.T
        return turned[:, 0:1], turned[:, 1:2]

    def dequantize_keys(c):
        for slot in range(2):
            scales = scale_rows[slot, c].T
            for k in range(groups):
                for b in range(blocks):
                    lanes = slice(b * (width // blocks), (b + 1) * (width // blocks))
                    keys[slot * span + k * rows:slot * span + (k + 1) * rows, lanes] = (
                        kbuf[slot, c, k, :, lanes].astype(f32)
                        * scales[k * rows:(k + 1) * rows, b:b + 1]
                    ).astype(bf16)

    def partial(c, first):
        q = qbuf[c, first:first + 2].reshape(2 * half, width)
        qr = jnp.concatenate(
            [qrbuf[c, first + j, :, i * rope:(i + 1) * rope] for j in range(2) for i in range(half // fold)],
            axis=0,
        )
        ropes = jnp.concatenate(
            [abuf[slot, c, k] for slot in range(2) for k in range(groups)], axis=1
        )
        s = lax.dot_general(q, keys[...], dims, preferred_element_type=f32)
        s = (s + jnp.dot(qr, ropes, preferred_element_type=f32)) * softmax_gain
        column = lax.broadcasted_iota(jnp.int32, (1, 2 * span), 1)
        local = column % span
        position = jnp.where(column < span, hub, edge) * span + local % rows * groups + local // rows
        s = jnp.where(position < len_ref[c % len_ref.shape[0]], s, masked_score)
        m = jnp.max(s, axis=1, keepdims=True)
        if first == 0:
            t = lax.dot_general(q, nkbuf[c], dims, preferred_element_type=f32)
            t = (t + lax.dot_general(qr, nrbuf[c], dims, preferred_element_type=f32)) * softmax_gain
            token = lax.broadcasted_iota(jnp.int32, t.shape, 0) % half // heads
            t = jnp.where(lax.broadcasted_iota(jnp.int32, t.shape, 1) <= token, t, masked_score)
            m = jnp.maximum(m, jnp.max(t, axis=1, keepdims=True))
        w = jnp.exp(s - m).astype(bf16)
        d = jnp.sum(w.astype(f32), axis=1, keepdims=True)
        n = jnp.dot(w, keys[...], preferred_element_type=f32)
        if first == 0:
            v = jnp.exp(t - m).astype(bf16)
            d = d + jnp.sum(v.astype(f32), axis=1, keepdims=True)
            n = n + jnp.dot(v, nkbuf[c], preferred_element_type=f32)
        return [
            (n[j * half:(j + 1) * half], stats_of(m[j * half:(j + 1) * half], d[j * half:(j + 1) * half]))
            for j in range(2)
        ]

    def merge(c):
        for copy in sums(c):
            copy.wait_recv()
        for j in (1, 0):
            m0, d0 = columns_of(side_stat[c, j])
            m1, d1 = columns_of(far_in_stat[c, j])
            m = jnp.maximum(m0, m1)
            f0, f1 = jnp.exp(m0 - m), jnp.exp(m1 - m)
            numerator = f0 * side_sum[c, j] + f1 * far_in[c, j].astype(f32)
            result[c, j] = (numerator / (f0 * d0 + f1 * d1)).astype(bf16)
            if j == 1:
                edge_result(c).start()
        own_result(c).start()

    @pl.when(is_edge)
    def _():
        shard_scales().start()

        @pl.loop(0, pairs)
        def _(c):
            prepare(c)

            @pl.when(c >= 1)
            def _():
                for copy in shard(c - 1):
                    copy.wait_send()

            start(shard(c))
            start(keep(0, c, me))

        for copy in shard(pairs - 1):
            copy.wait_send()
        for place in (hub, across, far_edge):
            await_scales(place)

        @pl.loop(0, pairs)
        def _(c):
            for place in (hub, across, far_edge):
                await_handover(c, place)
            edge_result(c).wait_recv()
            for copy in keep(0, c, me):
                copy.wait()
            for copy in queries(c, 0, 0, 1, hub):
                copy.wait_send()

        shard_scales().wait_send()

    @pl.when(is_hub)
    def _():
        handover_scales(0, edge, 2).start()

        @pl.loop(0, pairs)
        def _(c):
            prepare(c)
            await_queries(c, 1)
            start(queries(c, 2, 1, 3, across))
            start(handover(0, c, edge, 2))
            start(keep(0, c, me))

        for lane, target in ((0, across), (1, far_edge)):
            handover_scales(0, target, lane).start()
        start(handover_far(0, 0))
        start(handover_far(0, 1))
        nkbuf[...] = jnp.zeros(nkbuf.shape, bf16)
        nrbuf[...] = jnp.zeros(nrbuf.shape, bf16)
        for c in range(pairs):
            nkbuf[c, 0:fresh, :] = new_ref[c]
            nrbuf[c, 0:fresh, :] = newr_ref[c]
            load_query(c).wait()
        spread_scales(0)
        shard_scales().wait_recv()
        for lane, target in ((0, across), (1, far_edge)):
            handover_scales(1, target, lane).start()
        keep_scales(sbuf[1, me], edge)
        spread_scales(1)

        @pl.loop(0, pairs)
        def _(c):
            for copy in shard(c):
                copy.wait_recv()
            start(handover_far(1, c))
            start(keep(1, c, edge))

            @pl.when((c >= 2) & (c < pairs - 1))
            def _():
                start(handover_far(0, c))

            await_queries(c, 2)
            await_queries(c, 3)
            dequantize_keys(c)
            far = partial(c, 2)
            for j in range(2):
                far_out[c, j], far_out_stat[c, j] = far[j][0].astype(bf16), far[j][1]
            start(sums(c))
            near = partial(c, 0)
            for j in range(2):
                side_sum[c, j], side_stat[c, j] = near[j]

            @pl.when(c >= 1)
            def _():
                merge(c - 1)

        start(handover_far(0, pairs - 1))
        merge(pairs - 1)
        for place in (across, far_edge):
            await_scales(place)

        @pl.loop(0, pairs)
        def _(c):
            for place in (across, far_edge):
                await_handover(c, place)
            for copy in keep(0, c, me) + keep(1, c, edge):
                copy.wait()
            own_result(c).wait()
            for copy in handover(0, c, edge, 2) + handover_far(0, c) + handover_far(1, c):
                copy.wait_send()
            for copy in queries(c, 1, 0, 2, across) + queries(c, 2, 1, 3, across) + sums(c):
                copy.wait_send()
            edge_result(c).wait_send()

        handover_scales(0, edge, 2).wait_send()
        for lane, target in ((0, across), (1, far_edge)):
            handover_scales(0, target, lane).wait_send()
            handover_scales(1, target, lane).wait_send()


def per_device_line(
    latent_codes, latent_scales, rope_keys, lengths, query_latent, query_rope, new_latent, new_rope
):
    layers, requests, span, width = latent_codes.shape
    pairs, rows = layers * requests, span // 4
    rope, blocks = rope_keys.shape[-1], latent_scales.shape[-1]
    tokens, heads = query_latent.shape[2:4]
    half = tokens * heads
    tile_rows = -(-pairs * blocks // 16) * 16
    hbm_spec = pl.BlockSpec(memory_space=pltpu.HBM)
    any_spec = pl.BlockSpec(memory_space=pl.ANY)
    vmem_spec = pl.BlockSpec(memory_space=pltpu.VMEM)
    dma = pltpu.SemaphoreType.DMA
    bf16, f32 = jnp.bfloat16, jnp.float32
    att, cache, crope, cscale = pl.pallas_call(
        _hub_kernel,
        out_shape=(
            jax.ShapeDtypeStruct((pairs, half, width), bf16),
            jax.ShapeDtypeStruct((pairs, span, width), bf16),
            jax.ShapeDtypeStruct((pairs, rope, span), bf16),
            jax.ShapeDtypeStruct((pairs, blocks, span), bf16),
        ),
        in_specs=[pl.BlockSpec(memory_space=pltpu.SMEM)] + [hbm_spec] * 5 + [vmem_spec] * 2,
        out_specs=(any_spec, any_spec, any_spec, vmem_spec),
        scratch_shapes=[
            pltpu.VMEM((span, span), bf16),
            pltpu.VMEM((2, pairs, 4, rows, width), bf16),
            pltpu.VMEM((2, pairs, 4, rope, rows), bf16),
            pltpu.VMEM((2, 4, tile_rows, rows), bf16),
            pltpu.VMEM((4, tile_rows, rows), bf16),
            pltpu.VMEM((2, pairs, 8, span), f32),
            pltpu.VMEM((pairs, span, width), bf16),
            pltpu.VMEM((pairs, rope, span), bf16),
            pltpu.VMEM((pairs, blocks, span), bf16),
            pltpu.VMEM((pairs, half, rope), bf16),
            pltpu.VMEM((pairs, 4, half, width), bf16),
            pltpu.VMEM((pairs, 4, half * rope // 128, 128), bf16),
            pltpu.VMEM((pairs, 128, width), bf16),
            pltpu.VMEM((pairs, 128, rope), bf16),
            pltpu.VMEM((2 * span, width), bf16),
            pltpu.VMEM((pairs, 2, half, width), bf16),
            pltpu.VMEM((pairs, 2, half, width), f32),
            pltpu.VMEM((pairs, 2, 8, 128), f32),
            pltpu.VMEM((pairs, 2, half, width), bf16),
            pltpu.VMEM((pairs, 2, 8, 128), f32),
            pltpu.VMEM((pairs, 2, half, width), bf16),
            pltpu.VMEM((pairs, 2, 8, 128), f32),
            dma((6, pairs)), dma((2, 2, pairs)), dma((2, 3, pairs)), dma((2, 4, pairs)),
            dma((2, pairs)), dma((2, pairs)), dma((2, 2, 3, pairs)), dma((2, 4, pairs)),
            dma((3, 3)), dma((5,)), dma((2, pairs)), dma((2, pairs)), dma((pairs,)), dma((pairs,)),
        ],
        compiler_params=pltpu.CompilerParams(
            collective_id=0, has_side_effects=True, vmem_limit_bytes=60 << 20
        ),
    )(
        lengths, latent_codes.reshape(pairs, span, width),
        rope_keys.transpose(0, 1, 3, 2).reshape(pairs, rope, span),
        latent_scales.transpose(0, 1, 3, 2).reshape(pairs, blocks, span),
        query_latent.reshape(pairs, half, width), query_rope.reshape(pairs, half, rope),
        new_latent.reshape(pairs, tokens, width), new_rope.reshape(pairs, tokens, rope),
    )

    def as_cache(values):
        flipped = values.reshape(layers, requests, values.shape[1], span).transpose(0, 1, 3, 2)
        return flipped.reshape(layers, requests, span, 1, values.shape[1])

    return (
        att.reshape(query_latent.shape),
        cache.reshape(layers, requests, span, 1, width),
        as_cache(cscale),
        as_cache(crope),
    )


def solution(mesh):
    placed = (
        P(None, ("group", "req", "sub"), "seq", None),
        P(None, ("group", "req", "sub"), "seq", None),
        P(None, ("group", "req", "sub"), "seq", None),
        P(("group", "req", "sub")),
        P(None, ("group", "req", "sub"), None, "seq", None),
        P(None, ("group", "req", "sub"), None, "seq", None),
        P(None, ("group", "req", "sub"), None, None),
        P(None, ("group", "req", "sub"), None, None),
    )
    return jax.shard_map(
        per_device_line if mesh.shape["seq"] == 4 else per_device,
        mesh=mesh,
        in_specs=placed,
        out_specs=(
            P(None, ("group", "req", "sub"), None, "seq", None),
            P(None, ("group", "req", "sub"), None, "seq", None),
            P(None, ("group", "req", "sub"), None, "seq", None),
            P(None, ("group", "req", "sub"), None, "seq", None),
        ),
        check_vma=False,
    )
```

```python
import jax
import jax.numpy as jnp
from jax import lax
from jax.experimental import pallas as pl
from jax.experimental.pallas import tpu as pltpu
from jax.sharding import PartitionSpec as P

softmax_gain = 192.0 ** (-0.5)
masked_score = -1e30


def dequantize(code_values, scale_values):
    blocks = scale_values.shape[-1]
    latent_width = code_values.shape[-1]
    shaped = code_values.astype(jnp.float32).reshape(
        code_values.shape[:-1] + (blocks, latent_width // blocks)
    )
    scaled = shaped * scale_values.astype(jnp.float32)[..., None]
    return scaled.reshape(code_values.shape).astype(jnp.bfloat16)


def shard_partial(
    lat_query, rope_query, key_rows, rope_rows, usable, new_keys, new_rope_rows, holds_new
):
    tokens_new, head_count, latent_width = lat_query.shape
    query_rows = lat_query.reshape(tokens_new * head_count, latent_width)
    query_pos = rope_query.reshape(tokens_new * head_count, rope_query.shape[-1])
    scores = jnp.dot(query_rows, key_rows.T, preferred_element_type=jnp.float32)
    scores = (
        scores + jnp.dot(query_pos, rope_rows.T, preferred_element_type=jnp.float32)
    ) * softmax_gain
    fresh_scores = jnp.dot(query_rows, new_keys.T, preferred_element_type=jnp.float32)
    fresh_scores = (
        fresh_scores + jnp.dot(query_pos, new_rope_rows.T, preferred_element_type=jnp.float32)
    ) * softmax_gain
    token_of_row = jnp.arange(tokens_new * head_count, dtype=jnp.int32) // head_count
    causal = (jnp.arange(tokens_new, dtype=jnp.int32)[None, :] <= token_of_row[:, None]) & holds_new
    scores = jnp.where(usable[None, :], scores, masked_score)
    fresh_scores = jnp.where(causal, fresh_scores, masked_score)
    group_peak = jnp.maximum(jnp.max(scores, 1), jnp.max(fresh_scores, 1)).astype(jnp.bfloat16)
    peak_float = group_peak.astype(jnp.float32)[:, None]
    weights = jnp.where(usable[None, :], jnp.exp(scores - peak_float), 0.0).astype(jnp.bfloat16)
    fresh_weights = jnp.where(causal, jnp.exp(fresh_scores - peak_float), 0.0).astype(jnp.bfloat16)
    group_total = jnp.sum(weights.astype(jnp.float32), 1) + jnp.sum(
        fresh_weights.astype(jnp.float32), 1
    )
    group_sum = jnp.dot(weights, key_rows, preferred_element_type=jnp.float32)
    group_sum = group_sum + jnp.dot(fresh_weights, new_keys, preferred_element_type=jnp.float32)
    return (
        group_sum.astype(jnp.bfloat16).reshape(tokens_new, head_count, latent_width),
        group_peak.reshape(tokens_new, head_count),
        group_total.astype(jnp.bfloat16).reshape(tokens_new, head_count),
    )


def merge_groups(pieces):
    group_sum, group_peak, group_total = pieces
    peak_float = group_peak.astype(jnp.float32)
    overall = jnp.max(peak_float, 0)
    factor = jnp.exp(peak_float - overall)
    numerator = jnp.sum(factor[..., None] * group_sum.astype(jnp.float32), 0)
    denominator = jnp.sum(factor * group_total.astype(jnp.float32), 0)
    return (numerator / denominator[..., None]).astype(jnp.bfloat16)


def per_device(
    latent_codes, latent_scales, rope_keys, lengths, query_latent, query_rope, new_latent, new_rope
):
    shard_count = lax.axis_size("seq")
    seq_index = lax.axis_index("seq")
    layer_count, request_count, span, latent_width = latent_codes.shape
    lat_query, rope_query = (
        lax.all_gather(query_latent, "seq", axis=3, tiled=True),
        lax.all_gather(query_rope, "seq", axis=3, tiled=True),
    )

    def regroup_rows(values):
        return values.reshape(
            values.shape[0], values.shape[1], span // shard_count, shard_count, values.shape[-1]
        )

    codes_moved, scales_moved, rope_moved = (
        lax.all_to_all(regroup_rows(latent_codes), "seq", split_axis=3, concat_axis=2, tiled=True),
        lax.all_to_all(regroup_rows(latent_scales), "seq", split_axis=3, concat_axis=2, tiled=True),
        lax.all_to_all(regroup_rows(rope_keys), "seq", split_axis=3, concat_axis=2, tiled=True),
    )
    offsets = jnp.arange(span, dtype=jnp.int32)
    key_rows = dequantize(latent_codes, latent_scales)
    positions = seq_index * span + offsets
    usable = positions[None, :] < lengths[:, None]
    holds_new = seq_index == 0
    per_request = jax.vmap(shard_partial, in_axes=(0, 0, 0, 0, 0, 0, 0, None))
    per_layer = jax.vmap(per_request, in_axes=(0, 0, 0, 0, None, 0, 0, None))
    group_sum, group_peak, group_total = per_layer(
        lat_query, rope_query, key_rows, rope_keys, usable, new_latent, new_rope, holds_new
    )
    attended = merge_groups(
        (
            lax.all_to_all(group_sum[None], "seq", split_axis=4, concat_axis=0, tiled=True),
            lax.all_to_all(group_peak[None], "seq", split_axis=4, concat_axis=0, tiled=True),
            lax.all_to_all(group_total[None], "seq", split_axis=4, concat_axis=0, tiled=True),
        )
    )
    return (attended, codes_moved, scales_moved, rope_moved)


def _hub_kernel(
    len_ref, codes_ref, rope_ref, scale_ref, q_ref, qr_ref, new_ref, newr_ref,
    att_ref, cache_ref, crope_ref, cscale_ref,
    perm, kbuf, abuf, sbuf, scale_in, scale_rows, raw, rawr, raws, rawq, qbuf, qrbuf, nkbuf, nrbuf,
    keys, result, side_sum, side_stat, far_out, far_out_stat, far_in, far_in_stat,
    load_sem, keep_sem, q_send, q_recv, k_send, k_recv, f_send, f_recv, s_send, s_recv,
    far_send, far_recv, r_send, r_recv,
):
    pairs, span, width = codes_ref.shape
    groups = 4
    rows = span // groups
    half = q_ref.shape[1]
    rope = qr_ref.shape[2]
    blocks = scale_ref.shape[1]
    fresh = new_ref.shape[1]
    heads = half // fresh
    fold = half * rope // 128
    me = lax.axis_index("seq")
    is_hub = (me == 1) | (me == 2)
    is_edge = jnp.logical_not(is_hub)
    hub = 1 + me // 2
    edge = me // 2 * 3
    across = 3 - hub
    far_edge = 3 - edge
    f32, bf16 = jnp.float32, jnp.bfloat16

    def start(copies):
        for copy in copies:
            copy.start()

    def remote(src, dst, send, recv, target):
        return pltpu.make_async_remote_copy(
            src_ref=src, dst_ref=dst, send_sem=send, recv_sem=recv,
            device_id={"seq": target}, device_id_type=pl.DeviceIdType.MESH,
        )

    def greet(target):
        pl.semaphore_signal(
            pltpu.get_barrier_semaphore(), inc=1, device_id={"seq": target},
            device_id_type=pl.DeviceIdType.MESH,
        )

    def load(c):
        return (
            pltpu.make_async_copy(codes_ref.at[c], raw.at[c], load_sem.at[0, c]),
            pltpu.make_async_copy(rope_ref.at[c], rawr.at[c], load_sem.at[1, c]),
        )

    def load_scales(c):
        return pltpu.make_async_copy(scale_ref.at[c], raws.at[c], load_sem.at[2, c])

    def load_rotary(c):
        return pltpu.make_async_copy(qr_ref.at[c], rawq.at[c], load_sem.at[4, c])

    def load_query(c):
        return pltpu.make_async_copy(q_ref.at[c], qbuf.at[c, 0], load_sem.at[3, c])

    def query_latent(c, flow, src, dst, target):
        return remote(q_ref.at[c] if src == 0 else qbuf.at[c, src], qbuf.at[c, dst],
                      q_send.at[0, flow, c], q_recv.at[0, dst, c], target)

    def query_rotary(c, flow, src, dst, target):
        return remote(qrbuf.at[c, src], qrbuf.at[c, dst],
                      q_send.at[1, flow, c], q_recv.at[1, dst, c], target)

    def queries(c, flow, src, dst, target):
        return (query_latent(c, flow, src, dst, target), query_rotary(c, flow, src, dst, target))

    def await_queries(c, slot):
        for copy in queries(c, 0, 0, slot, across):
            copy.wait_recv()

    def shard(c):
        return (
            remote(abuf.at[0, c], abuf.at[1, c], k_send.at[0, c], k_recv.at[0, c], hub),
            remote(kbuf.at[0, c], kbuf.at[1, c], k_send.at[1, c], k_recv.at[1, c], hub),
        )

    def shard_scales():
        return remote(sbuf.at[0], sbuf.at[1], s_send.at[2, 0], s_recv.at[groups], hub)

    def place_of(slot):
        return hub if slot == 0 else edge

    def handover(slot, c, target, lane):
        place = place_of(slot)
        spot = pl.multiple_of(place * rows, rows)
        return (
            remote(kbuf.at[slot, c, target], cache_ref.at[c, pl.ds(spot, rows)],
                   f_send.at[0, slot, lane, c], f_recv.at[0, place, c], target),
            remote(abuf.at[slot, c, target], crope_ref.at[c, :, pl.ds(spot, rows)],
                   f_send.at[1, slot, lane, c], f_recv.at[1, place, c], target),
        )

    def handover_far(slot, c):
        return handover(slot, c, far_edge, 1) + handover(slot, c, across, 0)

    def handover_scales(slot, target, lane):
        return remote(sbuf.at[slot, target], scale_in.at[place_of(slot)],
                      s_send.at[slot, lane], s_recv.at[place_of(slot)], target)

    def await_handover(c, place):
        spot = pl.multiple_of(place * rows, rows)
        remote(kbuf.at[0, c, 0], cache_ref.at[c, pl.ds(spot, rows)],
               f_send.at[0, 0, 0, c], f_recv.at[0, place, c], across).wait_recv()
        remote(abuf.at[0, c, 0], crope_ref.at[c, :, pl.ds(spot, rows)],
               f_send.at[1, 0, 0, c], f_recv.at[1, place, c], across).wait_recv()

    def keep_scales(tile, place):
        values = tile.astype(f32)
        for c in range(pairs):
            cscale_ref[c, :, pl.ds(pl.multiple_of(place * rows, rows), rows)] = (
                values[c * blocks:(c + 1) * blocks].astype(bf16)
            )

    def await_scales(place):
        remote(sbuf.at[0, 0], scale_in.at[place], s_send.at[0, 0], s_recv.at[place], across).wait_recv()
        keep_scales(scale_in[place], place)

    def keep(slot, c, place):
        spot = pl.multiple_of(place * rows, rows)
        return (
            pltpu.make_async_copy(
                kbuf.at[slot, c, me], cache_ref.at[c, pl.ds(spot, rows)], keep_sem.at[0, slot, c]
            ),
            pltpu.make_async_copy(
                abuf.at[slot, c, me], crope_ref.at[c, :, pl.ds(spot, rows)], keep_sem.at[1, slot, c]
            ),
        )

    def sums(c):
        return (
            remote(far_out.at[c], far_in.at[c], far_send.at[0, c], far_recv.at[0, c], across),
            remote(far_out_stat.at[c], far_in_stat.at[c], far_send.at[1, c], far_recv.at[1, c], across),
        )

    def own_result(c):
        return pltpu.make_async_copy(result.at[c, 0], att_ref.at[c], load_sem.at[5, c])

    def edge_result(c):
        return remote(result.at[c, 1], att_ref.at[c], r_send.at[c], r_recv.at[c], edge)

    for c in range(pairs):
        load_rotary(c).start()
    for c in range(pairs):
        load_scales(c).start()
        start(load(c))

    @pl.when(is_hub)
    def _():
        for c in range(pairs):
            load_query(c).start()
        greet(across)
        greet(edge)
        pl.semaphore_wait(pltpu.get_barrier_semaphore(), 3)
        for c in range(pairs):
            query_latent(c, 1, 0, 2, across).start()

    @pl.when(is_edge)
    def _():
        greet(hub)
        greet(across)
        pl.semaphore_wait(pltpu.get_barrier_semaphore(), 1)
        for c in range(pairs):
            query_latent(c, 0, 0, 1, hub).start()

    for c in range(pairs):
        load_rotary(c).wait()
        qrbuf[c, 0] = jnp.concatenate(
            [rawq[c, i * fold:(i + 1) * fold, :] for i in range(half // fold)], axis=1
        )

    @pl.when(is_hub)
    def _():
        for c in range(pairs):
            query_rotary(c, 1, 0, 2, across).start()

    @pl.when(is_edge)
    def _():
        for c in range(pairs):
            query_rotary(c, 0, 0, 1, hub).start()

    line = lax.broadcasted_iota(jnp.int32, (span, span), 0)
    column = lax.broadcasted_iota(jnp.int32, (span, span), 1)
    perm[...] = jnp.where(column == (line % rows) * groups + line // rows, 1.0, 0.0).astype(bf16)
    dims = (((1,), (1,)), ((), ()))

    tile_rows = sbuf.shape[2]
    for c in range(pairs):
        load_scales(c).wait()
    stacked = [raws[c].astype(f32) for c in range(pairs)]
    if tile_rows > pairs * blocks:
        stacked.append(jnp.zeros((tile_rows - pairs * blocks, span), f32))
    stacked = jnp.concatenate(stacked, axis=0).astype(bf16)
    sorted_scales = lax.dot_general(stacked, perm[...], dims, preferred_element_type=f32)
    for k in range(groups):
        sbuf[0, k] = sorted_scales[:, k * rows:(k + 1) * rows].astype(bf16)
    keep_scales(sbuf[0, me], me)

    def spread_scales(slot):
        scale_rows[slot] = jnp.zeros(scale_rows.shape[1:], f32)
        for k in range(groups):
            values = sbuf[slot, k].astype(f32)
            for c in range(pairs):
                scale_rows[slot, c, 0:blocks, k * rows:(k + 1) * rows] = (
                    values[c * blocks:(c + 1) * blocks]
                )

    def prepare(c):
        for copy in load(c):
            copy.wait()
        sorted_codes = jnp.dot(perm[...], raw[c], preferred_element_type=f32)
        for k in range(groups):
            kbuf[0, c, k] = sorted_codes[k * rows:(k + 1) * rows].astype(bf16)
        sorted_rope = lax.dot_general(rawr[c], perm[...], dims, preferred_element_type=f32)
        for k in range(groups):
            abuf[0, c, k] = sorted_rope[:, k * rows:(k + 1) * rows].astype(bf16)

    def stats_of(m, d):
        lane = lax.broadcasted_iota(jnp.int32, (half, 128), 1)
        return jnp.where(lane == 0, m, d).T[0:8]

    def columns_of(stat):
        turned = stat.T
        return turned[:, 0:1], turned[:, 1:2]

    def dequantize_keys(c):
        for slot in range(2):
            scales = scale_rows[slot, c].T
            for k in range(groups):
                for b in range(blocks):
                    lanes = slice(b * (width // blocks), (b + 1) * (width // blocks))
                    keys[slot * span + k * rows:slot * span + (k + 1) * rows, lanes] = (
                        kbuf[slot, c, k, :, lanes].astype(f32)
                        * scales[k * rows:(k + 1) * rows, b:b + 1]
                    ).astype(bf16)

    def partial(c, first):
        q = qbuf[c, first:first + 2].reshape(2 * half, width)
        qr = jnp.concatenate(
            [qrbuf[c, first + j, :, i * rope:(i + 1) * rope] for j in range(2) for i in range(half // fold)],
            axis=0,
        )
        ropes = jnp.concatenate(
            [abuf[slot, c, k] for slot in range(2) for k in range(groups)], axis=1
        )
        s = lax.dot_general(q, keys[...], dims, preferred_element_type=f32)
        s = (s + jnp.dot(qr, ropes, preferred_element_type=f32)) * softmax_gain
        column = lax.broadcasted_iota(jnp.int32, (1, 2 * span), 1)
        local = column % span
        position = jnp.where(column < span, hub, edge) * span + local % rows * groups + local // rows
        s = jnp.where(position < len_ref[c % len_ref.shape[0]], s, masked_score)
        m = jnp.max(s, axis=1, keepdims=True)
        if first == 0:
            t = lax.dot_general(q, nkbuf[c], dims, preferred_element_type=f32)
            t = (t + lax.dot_general(qr, nrbuf[c], dims, preferred_element_type=f32)) * softmax_gain
            token = lax.broadcasted_iota(jnp.int32, t.shape, 0) % half // heads
            t = jnp.where(lax.broadcasted_iota(jnp.int32, t.shape, 1) <= token, t, masked_score)
            m = jnp.maximum(m, jnp.max(t, axis=1, keepdims=True))
        w = jnp.exp(s - m).astype(bf16)
        d = jnp.sum(w.astype(f32), axis=1, keepdims=True)
        n = jnp.dot(w, keys[...], preferred_element_type=f32)
        if first == 0:
            v = jnp.exp(t - m).astype(bf16)
            d = d + jnp.sum(v.astype(f32), axis=1, keepdims=True)
            n = n + jnp.dot(v, nkbuf[c], preferred_element_type=f32)
        return [
            (n[j * half:(j + 1) * half], stats_of(m[j * half:(j + 1) * half], d[j * half:(j + 1) * half]))
            for j in range(2)
        ]

    def merge(c):
        for copy in sums(c):
            copy.wait_recv()
        for j in (1, 0):
            m0, d0 = columns_of(side_stat[c, j])
            m1, d1 = columns_of(far_in_stat[c, j])
            m = jnp.maximum(m0, m1)
            f0, f1 = jnp.exp(m0 - m), jnp.exp(m1 - m)
            numerator = f0 * side_sum[c, j] + f1 * far_in[c, j].astype(f32)
            result[c, j] = (numerator / (f0 * d0 + f1 * d1)).astype(bf16)
            if j == 1:
                edge_result(c).start()
        own_result(c).start()

    @pl.when(is_edge)
    def _():
        shard_scales().start()

        @pl.loop(0, pairs)
        def _(c):
            prepare(c)

            @pl.when(c >= 1)
            def _():
                for copy in shard(c - 1):
                    copy.wait_send()

            start(shard(c))
            start(keep(0, c, me))

        for copy in shard(pairs - 1):
            copy.wait_send()
        for place in (hub, across, far_edge):
            await_scales(place)

        @pl.loop(0, pairs)
        def _(c):
            for place in (hub, across, far_edge):
                await_handover(c, place)
            edge_result(c).wait_recv()
            for copy in keep(0, c, me):
                copy.wait()
            for copy in queries(c, 0, 0, 1, hub):
                copy.wait_send()

        shard_scales().wait_send()

    @pl.when(is_hub)
    def _():
        handover_scales(0, edge, 2).start()

        @pl.loop(0, pairs)
        def _(c):
            prepare(c)
            await_queries(c, 1)
            start(queries(c, 2, 1, 3, across))
            start(handover(0, c, edge, 2))
            start(keep(0, c, me))

        for lane, target in ((0, across), (1, far_edge)):
            handover_scales(0, target, lane).start()
        start(handover_far(0, 0))
        start(handover_far(0, 1))
        nkbuf[...] = jnp.zeros(nkbuf.shape, bf16)
        nrbuf[...] = jnp.zeros(nrbuf.shape, bf16)
        for c in range(pairs):
            nkbuf[c, 0:fresh, :] = new_ref[c]
            nrbuf[c, 0:fresh, :] = newr_ref[c]
            load_query(c).wait()
        spread_scales(0)
        shard_scales().wait_recv()
        for lane, target in ((0, across), (1, far_edge)):
            handover_scales(1, target, lane).start()
        keep_scales(sbuf[1, me], edge)
        spread_scales(1)

        @pl.loop(0, pairs)
        def _(c):
            for copy in shard(c):
                copy.wait_recv()
            start(handover_far(1, c))
            start(keep(1, c, edge))

            @pl.when((c >= 2) & (c < pairs - 1))
            def _():
                start(handover_far(0, c))

            await_queries(c, 2)
            await_queries(c, 3)
            dequantize_keys(c)
            far = partial(c, 2)
            for j in range(2):
                far_out[c, j], far_out_stat[c, j] = far[j][0].astype(bf16), far[j][1]
            start(sums(c))
            near = partial(c, 0)
            for j in range(2):
                side_sum[c, j], side_stat[c, j] = near[j]

            @pl.when(c >= 1)
            def _():
                merge(c - 1)

        start(handover_far(0, pairs - 1))
        merge(pairs - 1)
        for place in (across, far_edge):
            await_scales(place)

        @pl.loop(0, pairs)
        def _(c):
            for place in (across, far_edge):
                await_handover(c, place)
            for copy in keep(0, c, me) + keep(1, c, edge):
                copy.wait()
            own_result(c).wait()
            for copy in handover(0, c, edge, 2) + handover_far(0, c) + handover_far(1, c):
                copy.wait_send()
            for copy in queries(c, 1, 0, 2, across) + queries(c, 2, 1, 3, across) + sums(c):
                copy.wait_send()
            edge_result(c).wait_send()

        handover_scales(0, edge, 2).wait_send()
        for lane, target in ((0, across), (1, far_edge)):
            handover_scales(0, target, lane).wait_send()
            handover_scales(1, target, lane).wait_send()


def _emit_kernel(
    att_ref, cache_ref, crope_ref, cscale_ref, att_out, cache_out, crope_out, cscale_out,
    att_hold, cache_hold, crope_hold, cscale_hold, load_sem, store_sem,
):
    loads, stores = [], []

    def move(src, hold, dst):
        i = len(loads)
        loads.append(pltpu.make_async_copy(src, hold, load_sem.at[i]))
        stores.append(pltpu.make_async_copy(hold, dst, store_sem.at[i]))

    pairs, span = cache_ref.shape[0:2]
    for c in range(pairs):
        for j in range(1):
            spot = pl.ds(j * (span // 1), span // 1)
            move(cache_ref.at[c, spot], cache_hold.at[c, spot], cache_out.at[c, spot])
    move(att_ref, att_hold, att_out)
    move(crope_ref, crope_hold, crope_out)
    move(cscale_ref, cscale_hold, cscale_out)
    for copy in loads:
        copy.start()
    for load, store in zip(loads, stores):
        load.wait()
        store.start()
    for copy in stores:
        copy.wait()


def emit(values):
    shapes = [jax.ShapeDtypeStruct(v.shape, v.dtype) for v in values]
    count = values[1].shape[0] * 1 + 3
    return pl.pallas_call(
        _emit_kernel,
        out_shape=shapes,
        in_specs=[pl.BlockSpec(memory_space=pl.ANY)] * 4,
        out_specs=[pl.BlockSpec(memory_space=pl.ANY)] * 4,
        scratch_shapes=[pltpu.VMEM(s.shape, s.dtype) for s in shapes]
        + [pltpu.SemaphoreType.DMA((count,))] * 2,
        compiler_params=pltpu.CompilerParams(vmem_limit_bytes=60 << 20),
    )(*values)


def per_device_line(
    latent_codes, latent_scales, rope_keys, lengths, query_latent, query_rope, new_latent, new_rope
):
    layers, requests, span, width = latent_codes.shape
    pairs, rows = layers * requests, span // 4
    rope, blocks = rope_keys.shape[-1], latent_scales.shape[-1]
    tokens, heads = query_latent.shape[2:4]
    half = tokens * heads
    tile_rows = -(-pairs * blocks // 16) * 16
    hbm_spec = pl.BlockSpec(memory_space=pltpu.HBM)
    any_spec = pl.BlockSpec(memory_space=pl.ANY)
    vmem_spec = pl.BlockSpec(memory_space=pltpu.VMEM)
    dma = pltpu.SemaphoreType.DMA
    bf16, f32 = jnp.bfloat16, jnp.float32
    att, cache, crope, cscale = pl.pallas_call(
        _hub_kernel,
        out_shape=(
            jax.ShapeDtypeStruct((pairs, half, width), bf16),
            jax.ShapeDtypeStruct((pairs, span, width), bf16),
            jax.ShapeDtypeStruct((pairs, rope, span), bf16),
            jax.ShapeDtypeStruct((pairs, blocks, span), bf16),
        ),
        in_specs=[pl.BlockSpec(memory_space=pltpu.SMEM)] + [hbm_spec] * 5 + [vmem_spec] * 2,
        out_specs=(any_spec, any_spec, any_spec, vmem_spec),
        scratch_shapes=[
            pltpu.VMEM((span, span), bf16),
            pltpu.VMEM((2, pairs, 4, rows, width), bf16),
            pltpu.VMEM((2, pairs, 4, rope, rows), bf16),
            pltpu.VMEM((2, 4, tile_rows, rows), bf16),
            pltpu.VMEM((4, tile_rows, rows), bf16),
            pltpu.VMEM((2, pairs, 8, span), f32),
            pltpu.VMEM((pairs, span, width), bf16),
            pltpu.VMEM((pairs, rope, span), bf16),
            pltpu.VMEM((pairs, blocks, span), bf16),
            pltpu.VMEM((pairs, half, rope), bf16),
            pltpu.VMEM((pairs, 4, half, width), bf16),
            pltpu.VMEM((pairs, 4, half * rope // 128, 128), bf16),
            pltpu.VMEM((pairs, 128, width), bf16),
            pltpu.VMEM((pairs, 128, rope), bf16),
            pltpu.VMEM((2 * span, width), bf16),
            pltpu.VMEM((pairs, 2, half, width), bf16),
            pltpu.VMEM((pairs, 2, half, width), f32),
            pltpu.VMEM((pairs, 2, 8, 128), f32),
            pltpu.VMEM((pairs, 2, half, width), bf16),
            pltpu.VMEM((pairs, 2, 8, 128), f32),
            pltpu.VMEM((pairs, 2, half, width), bf16),
            pltpu.VMEM((pairs, 2, 8, 128), f32),
            dma((6, pairs)), dma((2, 2, pairs)), dma((2, 3, pairs)), dma((2, 4, pairs)),
            dma((2, pairs)), dma((2, pairs)), dma((2, 2, 3, pairs)), dma((2, 4, pairs)),
            dma((3, 3)), dma((5,)), dma((2, pairs)), dma((2, pairs)), dma((pairs,)), dma((pairs,)),
        ],
        compiler_params=pltpu.CompilerParams(
            collective_id=0, has_side_effects=True, vmem_limit_bytes=60 << 20
        ),
    )(
        lengths, latent_codes.reshape(pairs, span, width),
        rope_keys.transpose(0, 1, 3, 2).reshape(pairs, rope, span),
        latent_scales.transpose(0, 1, 3, 2).reshape(pairs, blocks, span),
        query_latent.reshape(pairs, half, width), query_rope.reshape(pairs, half, rope),
        new_latent.reshape(pairs, tokens, width), new_rope.reshape(pairs, tokens, rope),
    )

    att, cache, crope, cscale = emit((att, cache, crope, cscale))

    def as_cache(values):
        flipped = values.reshape(layers, requests, values.shape[1], span).transpose(0, 1, 3, 2)
        return flipped.reshape(layers, requests, span, 1, values.shape[1])

    return (
        att.reshape(query_latent.shape),
        cache.reshape(layers, requests, span, 1, width),
        as_cache(cscale),
        as_cache(crope),
    )


def solution(mesh):
    placed = (
        P(None, ("group", "req", "sub"), "seq", None),
        P(None, ("group", "req", "sub"), "seq", None),
        P(None, ("group", "req", "sub"), "seq", None),
        P(("group", "req", "sub")),
        P(None, ("group", "req", "sub"), None, "seq", None),
        P(None, ("group", "req", "sub"), None, "seq", None),
        P(None, ("group", "req", "sub"), None, None),
        P(None, ("group", "req", "sub"), None, None),
    )
    return jax.shard_map(
        per_device_line if mesh.shape["seq"] == 4 else per_device,
        mesh=mesh,
        in_specs=placed,
        out_specs=(
            P(None, ("group", "req", "sub"), None, "seq", None),
            P(None, ("group", "req", "sub"), None, "seq", None),
            P(None, ("group", "req", "sub"), None, "seq", None),
            P(None, ("group", "req", "sub"), None, "seq", None),
        ),
        check_vma=False,
    )
```

```python
import jax
import jax.numpy as jnp
from jax import lax
from jax.experimental import pallas as pl
from jax.experimental.pallas import tpu as pltpu
from jax.sharding import PartitionSpec as P

softmax_gain = 192.0 ** (-0.5)
masked_score = -1e30


def dequantize(code_values, scale_values):
    blocks = scale_values.shape[-1]
    latent_width = code_values.shape[-1]
    shaped = code_values.astype(jnp.float32).reshape(
        code_values.shape[:-1] + (blocks, latent_width // blocks)
    )
    scaled = shaped * scale_values.astype(jnp.float32)[..., None]
    return scaled.reshape(code_values.shape).astype(jnp.bfloat16)


def shard_partial(
    lat_query, rope_query, key_rows, rope_rows, usable, new_keys, new_rope_rows, holds_new
):
    tokens_new, head_count, latent_width = lat_query.shape
    query_rows = lat_query.reshape(tokens_new * head_count, latent_width)
    query_pos = rope_query.reshape(tokens_new * head_count, rope_query.shape[-1])
    scores = jnp.dot(query_rows, key_rows.T, preferred_element_type=jnp.float32)
    scores = (
        scores + jnp.dot(query_pos, rope_rows.T, preferred_element_type=jnp.float32)
    ) * softmax_gain
    fresh_scores = jnp.dot(query_rows, new_keys.T, preferred_element_type=jnp.float32)
    fresh_scores = (
        fresh_scores + jnp.dot(query_pos, new_rope_rows.T, preferred_element_type=jnp.float32)
    ) * softmax_gain
    token_of_row = jnp.arange(tokens_new * head_count, dtype=jnp.int32) // head_count
    causal = (jnp.arange(tokens_new, dtype=jnp.int32)[None, :] <= token_of_row[:, None]) & holds_new
    scores = jnp.where(usable[None, :], scores, masked_score)
    fresh_scores = jnp.where(causal, fresh_scores, masked_score)
    group_peak = jnp.maximum(jnp.max(scores, 1), jnp.max(fresh_scores, 1)).astype(jnp.bfloat16)
    peak_float = group_peak.astype(jnp.float32)[:, None]
    weights = jnp.where(usable[None, :], jnp.exp(scores - peak_float), 0.0).astype(jnp.bfloat16)
    fresh_weights = jnp.where(causal, jnp.exp(fresh_scores - peak_float), 0.0).astype(jnp.bfloat16)
    group_total = jnp.sum(weights.astype(jnp.float32), 1) + jnp.sum(
        fresh_weights.astype(jnp.float32), 1
    )
    group_sum = jnp.dot(weights, key_rows, preferred_element_type=jnp.float32)
    group_sum = group_sum + jnp.dot(fresh_weights, new_keys, preferred_element_type=jnp.float32)
    return (
        group_sum.astype(jnp.bfloat16).reshape(tokens_new, head_count, latent_width),
        group_peak.reshape(tokens_new, head_count),
        group_total.astype(jnp.bfloat16).reshape(tokens_new, head_count),
    )


def merge_groups(pieces):
    group_sum, group_peak, group_total = pieces
    peak_float = group_peak.astype(jnp.float32)
    overall = jnp.max(peak_float, 0)
    factor = jnp.exp(peak_float - overall)
    numerator = jnp.sum(factor[..., None] * group_sum.astype(jnp.float32), 0)
    denominator = jnp.sum(factor * group_total.astype(jnp.float32), 0)
    return (numerator / denominator[..., None]).astype(jnp.bfloat16)


def per_device(
    latent_codes, latent_scales, rope_keys, lengths, query_latent, query_rope, new_latent, new_rope
):
    shard_count = lax.axis_size("seq")
    seq_index = lax.axis_index("seq")
    layer_count, request_count, span, latent_width = latent_codes.shape
    lat_query, rope_query = (
        lax.all_gather(query_latent, "seq", axis=3, tiled=True),
        lax.all_gather(query_rope, "seq", axis=3, tiled=True),
    )

    def regroup_rows(values):
        return values.reshape(
            values.shape[0], values.shape[1], span // shard_count, shard_count, values.shape[-1]
        )

    codes_moved, scales_moved, rope_moved = (
        lax.all_to_all(regroup_rows(latent_codes), "seq", split_axis=3, concat_axis=2, tiled=True),
        lax.all_to_all(regroup_rows(latent_scales), "seq", split_axis=3, concat_axis=2, tiled=True),
        lax.all_to_all(regroup_rows(rope_keys), "seq", split_axis=3, concat_axis=2, tiled=True),
    )
    offsets = jnp.arange(span, dtype=jnp.int32)
    key_rows = dequantize(latent_codes, latent_scales)
    positions = seq_index * span + offsets
    usable = positions[None, :] < lengths[:, None]
    holds_new = seq_index == 0
    per_request = jax.vmap(shard_partial, in_axes=(0, 0, 0, 0, 0, 0, 0, None))
    per_layer = jax.vmap(per_request, in_axes=(0, 0, 0, 0, None, 0, 0, None))
    group_sum, group_peak, group_total = per_layer(
        lat_query, rope_query, key_rows, rope_keys, usable, new_latent, new_rope, holds_new
    )
    attended = merge_groups(
        (
            lax.all_to_all(group_sum[None], "seq", split_axis=4, concat_axis=0, tiled=True),
            lax.all_to_all(group_peak[None], "seq", split_axis=4, concat_axis=0, tiled=True),
            lax.all_to_all(group_total[None], "seq", split_axis=4, concat_axis=0, tiled=True),
        )
    )
    return (attended, codes_moved, scales_moved, rope_moved)


def _hub_kernel(
    len_ref, codes_ref, rope_ref, scale_ref, q_ref, qr_ref, new_ref, newr_ref,
    att_ref, cache_ref, crope_ref, cscale_ref,
    perm, kbuf, abuf, sbuf, scale_in, scale_rows, raw, rawr, raws, rawq, qbuf, qrbuf, nkbuf, nrbuf,
    keys, result, side_sum, side_stat, far_out, far_out_stat, far_in, far_in_stat,
    new_rows, newr_rows, scales_out, out_sem, load_sem, keep_sem, q_send, q_recv, k_send, k_recv, f_send, f_recv, s_send, s_recv,
    far_send, far_recv, r_send, r_recv,
):
    pairs, span, width = codes_ref.shape
    groups = 4
    rows = span // groups
    half = q_ref.shape[1]
    rope = qr_ref.shape[2]
    blocks = scale_ref.shape[1]
    fresh = new_ref.shape[1]
    heads = half // fresh
    fold = half * rope // 128
    me = lax.axis_index("seq")
    is_hub = (me == 1) | (me == 2)
    is_edge = jnp.logical_not(is_hub)
    hub = 1 + me // 2
    edge = me // 2 * 3
    across = 3 - hub
    far_edge = 3 - edge
    f32, bf16 = jnp.float32, jnp.bfloat16

    def start(copies):
        for copy in copies:
            copy.start()

    def remote(src, dst, send, recv, target):
        return pltpu.make_async_remote_copy(
            src_ref=src, dst_ref=dst, send_sem=send, recv_sem=recv,
            device_id={"seq": target}, device_id_type=pl.DeviceIdType.MESH,
        )

    def greet(target):
        pl.semaphore_signal(
            pltpu.get_barrier_semaphore(), inc=1, device_id={"seq": target},
            device_id_type=pl.DeviceIdType.MESH,
        )

    def load(c):
        return (
            pltpu.make_async_copy(codes_ref.at[c], raw.at[c], load_sem.at[0, c]),
            pltpu.make_async_copy(rope_ref.at[c], rawr.at[c], load_sem.at[1, c]),
        )

    def load_scales(c):
        return pltpu.make_async_copy(scale_ref.at[c], raws.at[c], load_sem.at[2, c])

    def load_rotary(c):
        return pltpu.make_async_copy(qr_ref.at[c], rawq.at[c], load_sem.at[4, c])

    def load_new():
        return (
            pltpu.make_async_copy(new_ref, new_rows, out_sem.at[0]),
            pltpu.make_async_copy(newr_ref, newr_rows, out_sem.at[1]),
        )

    def out_scales():
        return pltpu.make_async_copy(scales_out, cscale_ref, out_sem.at[2])

    def load_query(c):
        return pltpu.make_async_copy(q_ref.at[c], qbuf.at[c, 0], load_sem.at[3, c])

    def query_latent(c, flow, src, dst, target):
        return remote(q_ref.at[c] if src == 0 else qbuf.at[c, src], qbuf.at[c, dst],
                      q_send.at[0, flow, c], q_recv.at[0, dst, c], target)

    def query_rotary(c, flow, src, dst, target):
        return remote(qrbuf.at[c, src], qrbuf.at[c, dst],
                      q_send.at[1, flow, c], q_recv.at[1, dst, c], target)

    def queries(c, flow, src, dst, target):
        return (query_latent(c, flow, src, dst, target), query_rotary(c, flow, src, dst, target))

    def await_queries(c, slot):
        for copy in queries(c, 0, 0, slot, across):
            copy.wait_recv()

    def shard(c):
        return (
            remote(abuf.at[0, c], abuf.at[1, c], k_send.at[0, c], k_recv.at[0, c], hub),
            remote(kbuf.at[0, c], kbuf.at[1, c], k_send.at[1, c], k_recv.at[1, c], hub),
        )

    def shard_scales():
        return remote(sbuf.at[0], sbuf.at[1], s_send.at[2, 0], s_recv.at[groups], hub)

    def place_of(slot):
        return hub if slot == 0 else edge

    def handover(slot, c, target, lane):
        place = place_of(slot)
        spot = pl.multiple_of(place * rows, rows)
        return (
            remote(kbuf.at[slot, c, target], cache_ref.at[c, pl.ds(spot, rows)],
                   f_send.at[0, slot, lane, c], f_recv.at[0, place, c], target),
            remote(abuf.at[slot, c, target], crope_ref.at[c, :, pl.ds(spot, rows)],
                   f_send.at[1, slot, lane, c], f_recv.at[1, place, c], target),
        )

    def handover_far(slot, c):
        return handover(slot, c, far_edge, 1) + handover(slot, c, across, 0)

    def handover_scales(slot, target, lane):
        return remote(sbuf.at[slot, target], scale_in.at[place_of(slot)],
                      s_send.at[slot, lane], s_recv.at[place_of(slot)], target)

    def await_handover(c, place):
        spot = pl.multiple_of(place * rows, rows)
        remote(kbuf.at[0, c, 0], cache_ref.at[c, pl.ds(spot, rows)],
               f_send.at[0, 0, 0, c], f_recv.at[0, place, c], across).wait_recv()
        remote(abuf.at[0, c, 0], crope_ref.at[c, :, pl.ds(spot, rows)],
               f_send.at[1, 0, 0, c], f_recv.at[1, place, c], across).wait_recv()

    def keep_scales(tile, place):
        values = tile.astype(f32)
        for c in range(pairs):
            scales_out[c, :, pl.ds(pl.multiple_of(place * rows, rows), rows)] = (
                values[c * blocks:(c + 1) * blocks].astype(bf16)
            )

    def await_scales(place):
        remote(sbuf.at[0, 0], scale_in.at[place], s_send.at[0, 0], s_recv.at[place], across).wait_recv()
        keep_scales(scale_in[place], place)

    def keep(slot, c, place):
        spot = pl.multiple_of(place * rows, rows)
        return (
            pltpu.make_async_copy(
                kbuf.at[slot, c, me], cache_ref.at[c, pl.ds(spot, rows)], keep_sem.at[0, slot, c]
            ),
            pltpu.make_async_copy(
                abuf.at[slot, c, me], crope_ref.at[c, :, pl.ds(spot, rows)], keep_sem.at[1, slot, c]
            ),
        )

    def sums(c):
        return (
            remote(far_out.at[c], far_in.at[c], far_send.at[0, c], far_recv.at[0, c], across),
            remote(far_out_stat.at[c], far_in_stat.at[c], far_send.at[1, c], far_recv.at[1, c], across),
        )

    def own_result(c):
        return pltpu.make_async_copy(result.at[c, 0], att_ref.at[c], load_sem.at[5, c])

    def edge_result(c):
        return remote(result.at[c, 1], att_ref.at[c], r_send.at[c], r_recv.at[c], edge)

    @pl.when(is_hub)
    def _():
        greet(across)
        greet(edge)

    @pl.when(is_edge)
    def _():
        greet(across)
        greet(hub)

    for c in range(pairs):
        load_rotary(c).start()
    for c in range(pairs):
        load_scales(c).start()
        start(load(c))

    @pl.when(is_hub)
    def _():
        pl.semaphore_wait(pltpu.get_barrier_semaphore(), 3)
        for c in range(pairs):
            query_latent(c, 1, 0, 2, across).start()
        for c in range(pairs):
            load_query(c).start()
        start(load_new())

    @pl.when(is_edge)
    def _():
        pl.semaphore_wait(pltpu.get_barrier_semaphore(), 1)
        query_latent(0, 0, 0, 1, hub).start()

    for c in range(pairs):
        load_rotary(c).wait()
        qrbuf[c, 0] = jnp.concatenate(
            [rawq[c, i * fold:(i + 1) * fold, :] for i in range(half // fold)], axis=1
        )

    @pl.when(is_hub)
    def _():
        for c in range(pairs):
            query_rotary(c, 1, 0, 2, across).start()

    @pl.when(is_edge)
    def _():
        query_rotary(0, 0, 0, 1, hub).start()

    line = lax.broadcasted_iota(jnp.int32, (span, span), 0)
    column = lax.broadcasted_iota(jnp.int32, (span, span), 1)
    perm[...] = jnp.where(column == (line % rows) * groups + line // rows, 1.0, 0.0).astype(bf16)
    dims = (((1,), (1,)), ((), ()))

    tile_rows = sbuf.shape[2]
    for c in range(pairs):
        load_scales(c).wait()
    stacked = [raws[c].astype(f32) for c in range(pairs)]
    if tile_rows > pairs * blocks:
        stacked.append(jnp.zeros((tile_rows - pairs * blocks, span), f32))
    stacked = jnp.concatenate(stacked, axis=0).astype(bf16)
    sorted_scales = lax.dot_general(stacked, perm[...], dims, preferred_element_type=f32)
    for k in range(groups):
        sbuf[0, k] = sorted_scales[:, k * rows:(k + 1) * rows].astype(bf16)
    keep_scales(sbuf[0, me], me)

    def spread_scales(slot):
        scale_rows[slot] = jnp.zeros(scale_rows.shape[1:], f32)
        for k in range(groups):
            values = sbuf[slot, k].astype(f32)
            for c in range(pairs):
                scale_rows[slot, c, 0:blocks, k * rows:(k + 1) * rows] = (
                    values[c * blocks:(c + 1) * blocks]
                )

    def prepare(c):
        for copy in load(c):
            copy.wait()
        sorted_codes = jnp.dot(perm[...], raw[c], preferred_element_type=f32)
        for k in range(groups):
            kbuf[0, c, k] = sorted_codes[k * rows:(k + 1) * rows].astype(bf16)
        sorted_rope = lax.dot_general(rawr[c], perm[...], dims, preferred_element_type=f32)
        for k in range(groups):
            abuf[0, c, k] = sorted_rope[:, k * rows:(k + 1) * rows].astype(bf16)

    def stats_of(m, d):
        lane = lax.broadcasted_iota(jnp.int32, (half, 128), 1)
        return jnp.where(
            lane < 2, jnp.where(lane == 0, m[:half], d[:half]), jnp.where(lane == 2, m[half:], d[half:])
        ).T[0:8]

    def columns_of(stat, j):
        return stat[:, 2 * j:2 * j + 1], stat[:, 2 * j + 1:2 * j + 2]

    def dequantize_keys(c):
        for slot in range(2):
            scales = scale_rows[slot, c].T
            for k in range(groups):
                for b in range(blocks):
                    lanes = slice(b * (width // blocks), (b + 1) * (width // blocks))
                    keys[slot * span + k * rows:slot * span + (k + 1) * rows, lanes] = (
                        kbuf[slot, c, k, :, lanes].astype(f32)
                        * scales[k * rows:(k + 1) * rows, b:b + 1]
                    ).astype(bf16)

    def partial(c, first):
        q = qbuf[c, first:first + 2].reshape(2 * half, width)
        qr = jnp.concatenate(
            [qrbuf[c, first + j, :, i * rope:(i + 1) * rope] for j in range(2) for i in range(half // fold)],
            axis=0,
        )
        ropes = jnp.concatenate(
            [abuf[slot, c, k] for slot in range(2) for k in range(groups)], axis=1
        )
        s = lax.dot_general(q, keys[...], dims, preferred_element_type=f32)
        s = (s + jnp.dot(qr, ropes, preferred_element_type=f32)) * softmax_gain
        column = lax.broadcasted_iota(jnp.int32, (1, 2 * span), 1)
        local = column % span
        position = jnp.where(column < span, hub, edge) * span + local % rows * groups + local // rows
        s = jnp.where(position < len_ref[c % len_ref.shape[0]], s, masked_score)
        m = jnp.max(s, axis=1, keepdims=True)
        if first == 0:
            t = lax.dot_general(q, nkbuf[c], dims, preferred_element_type=f32)
            t = (t + lax.dot_general(qr, nrbuf[c], dims, preferred_element_type=f32)) * softmax_gain
            token = lax.broadcasted_iota(jnp.int32, t.shape, 0) % half // heads
            t = jnp.where(lax.broadcasted_iota(jnp.int32, t.shape, 1) <= token, t, masked_score)
            m = jnp.maximum(m, jnp.max(t, axis=1, keepdims=True))
        w = jnp.exp(s - m).astype(bf16)
        d = jnp.sum(w.astype(f32), axis=1, keepdims=True)
        n = jnp.dot(w, keys[...], preferred_element_type=f32)
        if first == 0:
            v = jnp.exp(t - m).astype(bf16)
            d = d + jnp.sum(v.astype(f32), axis=1, keepdims=True)
            n = n + jnp.dot(v, nkbuf[c], preferred_element_type=f32)
        return n, stats_of(m, d)

    def merge(c):
        for copy in sums(c):
            copy.wait_recv()
        side, far = side_stat[c].T, far_in_stat[c].T
        for j in (1, 0):
            m0, d0 = columns_of(side, j)
            m1, d1 = columns_of(far, j)
            m = jnp.maximum(m0, m1)
            f0, f1 = jnp.exp(m0 - m), jnp.exp(m1 - m)
            numerator = f0 * side_sum[c, j] + f1 * far_in[c, j].astype(f32)
            result[c, j] = (numerator / (f0 * d0 + f1 * d1)).astype(bf16)
            if j == 1:
                edge_result(c).start()
        own_result(c).start()

    @pl.when(is_edge)
    def _():
        shard_scales().start()

        @pl.loop(0, pairs)
        def _(c):
            prepare(c)

            @pl.when(c >= 1)
            def _():
                for copy in shard(c - 1):
                    copy.wait_send()

                start(queries(c, 0, 0, 1, hub))

            start(shard(c))
            start(keep(0, c, me))

        for copy in shard(pairs - 1):
            copy.wait_send()
        for place in (hub, across, far_edge):
            await_scales(place)
        out_scales().start()

        @pl.loop(0, pairs)
        def _(c):
            for place in (hub, across, far_edge):
                await_handover(c, place)
            edge_result(c).wait_recv()
            for copy in keep(0, c, me):
                copy.wait()
            for copy in queries(c, 0, 0, 1, hub):
                copy.wait_send()

        shard_scales().wait_send()
        out_scales().wait()

    @pl.when(is_hub)
    def _():
        handover_scales(0, edge, 2).start()

        @pl.loop(0, pairs)
        def _(c):
            prepare(c)
            start(handover(0, c, edge, 2))
            start(keep(0, c, me))

        for lane, target in ((0, across), (1, far_edge)):
            handover_scales(0, target, lane).start()
        await_queries(0, 1)
        start(queries(0, 2, 1, 3, across))
        start(handover_far(0, 0))
        for copy in load_new():
            copy.wait()
        nkbuf[...] = jnp.zeros(nkbuf.shape, bf16)
        nrbuf[...] = jnp.zeros(nrbuf.shape, bf16)
        for c in range(pairs):
            nkbuf[c, 0:fresh, :] = new_rows[c]
            nrbuf[c, 0:fresh, :] = newr_rows[c]
            load_query(c).wait()
        spread_scales(0)
        shard_scales().wait_recv()
        for lane, target in ((0, across), (1, far_edge)):
            handover_scales(1, target, lane).start()
        keep_scales(sbuf[1, me], edge)
        spread_scales(1)

        @pl.loop(0, pairs)
        def _(c):
            for copy in shard(c):
                copy.wait_recv()
            start(handover_far(1, c))
            start(keep(1, c, edge))

            @pl.when(c < pairs - 1)
            def _():
                await_queries(c + 1, 1)
                start(queries(c + 1, 2, 1, 3, across))

            await_queries(c, 2)
            await_queries(c, 3)
            dequantize_keys(c)
            far_sum, far_out_stat[c] = partial(c, 2)
            for j in range(2):
                far_out[c, j] = far_sum[j * half:(j + 1) * half].astype(bf16)
            start(sums(c))
            @pl.when(c == 1)
            def _():
                start(handover_far(0, c))

            near_sum, side_stat[c] = partial(c, 0)
            for j in range(2):
                side_sum[c, j] = near_sum[j * half:(j + 1) * half]

            @pl.when(c >= 1)
            def _():
                merge(c - 1)

        for c in range(2, pairs):
            start(handover_far(0, c))
        for place in (across, far_edge):
            await_scales(place)
        out_scales().start()
        merge(pairs - 1)

        @pl.loop(0, pairs)
        def _(c):
            for place in (across, far_edge):
                await_handover(c, place)
            for copy in keep(0, c, me) + keep(1, c, edge):
                copy.wait()
            own_result(c).wait()
            for copy in handover(0, c, edge, 2) + handover_far(0, c) + handover_far(1, c):
                copy.wait_send()
            for copy in queries(c, 1, 0, 2, across) + queries(c, 2, 1, 3, across) + sums(c):
                copy.wait_send()
            edge_result(c).wait_send()

        out_scales().wait()
        handover_scales(0, edge, 2).wait_send()
        for lane, target in ((0, across), (1, far_edge)):
            handover_scales(0, target, lane).wait_send()
            handover_scales(1, target, lane).wait_send()


def _emit_kernel(
    att_ref, cache_ref, crope_ref, cscale_ref, att_out, cache_out, crope_out, cscale_out,
    att_hold, cache_hold, crope_hold, cscale_hold, load_sem, store_sem,
):
    loads, stores = [], []

    def move(src, hold, dst):
        i = len(loads)
        loads.append(pltpu.make_async_copy(src, hold, load_sem.at[i]))
        stores.append(pltpu.make_async_copy(hold, dst, store_sem.at[i]))

    pairs, span = cache_ref.shape[0:2]
    for c in range(pairs):
        for j in range(1):
            spot = pl.ds(j * (span // 1), span // 1)
            move(cache_ref.at[c, spot], cache_hold.at[c, spot], cache_out.at[c, spot])
    move(att_ref, att_hold, att_out)
    move(crope_ref, crope_hold, crope_out)
    move(cscale_ref, cscale_hold, cscale_out)
    for copy in loads:
        copy.start()
    for load, store in zip(loads, stores):
        load.wait()
        store.start()
    for copy in stores:
        copy.wait()


def emit(values):
    shapes = [jax.ShapeDtypeStruct(v.shape, v.dtype) for v in values]
    count = values[1].shape[0] * 1 + 3
    return pl.pallas_call(
        _emit_kernel,
        out_shape=shapes,
        in_specs=[pl.BlockSpec(memory_space=pl.ANY)] * 4,
        out_specs=[pl.BlockSpec(memory_space=pl.ANY)] * 4,
        scratch_shapes=[pltpu.VMEM(s.shape, s.dtype) for s in shapes]
        + [pltpu.SemaphoreType.DMA((count,))] * 2,
        compiler_params=pltpu.CompilerParams(vmem_limit_bytes=60 << 20),
    )(*values)


def per_device_line(
    latent_codes, latent_scales, rope_keys, lengths, query_latent, query_rope, new_latent, new_rope
):
    layers, requests, span, width = latent_codes.shape
    pairs, rows = layers * requests, span // 4
    rope, blocks = rope_keys.shape[-1], latent_scales.shape[-1]
    tokens, heads = query_latent.shape[2:4]
    half = tokens * heads
    tile_rows = -(-pairs * blocks // 16) * 16
    hbm_spec = pl.BlockSpec(memory_space=pltpu.HBM)
    any_spec = pl.BlockSpec(memory_space=pl.ANY)
    dma = pltpu.SemaphoreType.DMA
    bf16, f32 = jnp.bfloat16, jnp.float32
    att, cache, crope, cscale = pl.pallas_call(
        _hub_kernel,
        out_shape=(
            jax.ShapeDtypeStruct((pairs, half, width), bf16),
            jax.ShapeDtypeStruct((pairs, span, width), bf16),
            jax.ShapeDtypeStruct((pairs, rope, span), bf16),
            jax.ShapeDtypeStruct((pairs, blocks, span), bf16),
        ),
        in_specs=[pl.BlockSpec(memory_space=pltpu.SMEM)] + [hbm_spec] * 7,
        out_specs=(any_spec, any_spec, any_spec, any_spec),
        scratch_shapes=[
            pltpu.VMEM((span, span), bf16),
            pltpu.VMEM((2, pairs, 4, rows, width), bf16),
            pltpu.VMEM((2, pairs, 4, rope, rows), bf16),
            pltpu.VMEM((2, 4, tile_rows, rows), bf16),
            pltpu.VMEM((4, tile_rows, rows), bf16),
            pltpu.VMEM((2, pairs, 8, span), f32),
            pltpu.VMEM((pairs, span, width), bf16),
            pltpu.VMEM((pairs, rope, span), bf16),
            pltpu.VMEM((pairs, blocks, span), bf16),
            pltpu.VMEM((pairs, half, rope), bf16),
            pltpu.VMEM((pairs, 4, half, width), bf16),
            pltpu.VMEM((pairs, 4, half * rope // 128, 128), bf16),
            pltpu.VMEM((pairs, 128, width), bf16),
            pltpu.VMEM((pairs, 128, rope), bf16),
            pltpu.VMEM((2 * span, width), bf16),
            pltpu.VMEM((pairs, 2, half, width), bf16),
            pltpu.VMEM((pairs, 2, half, width), f32),
            pltpu.VMEM((pairs, 8, 128), f32),
            pltpu.VMEM((pairs, 2, half, width), bf16),
            pltpu.VMEM((pairs, 8, 128), f32),
            pltpu.VMEM((pairs, 2, half, width), bf16),
            pltpu.VMEM((pairs, 8, 128), f32),
            pltpu.VMEM((pairs, tokens, width), bf16),
            pltpu.VMEM((pairs, tokens, rope), bf16),
            pltpu.VMEM((pairs, blocks, span), bf16),
            dma((3,)), dma((6, pairs)), dma((2, 2, pairs)), dma((2, 3, pairs)), dma((2, 4, pairs)),
            dma((2, pairs)), dma((2, pairs)), dma((2, 2, 3, pairs)), dma((2, 4, pairs)),
            dma((3, 3)), dma((5,)), dma((2, pairs)), dma((2, pairs)), dma((pairs,)), dma((pairs,)),
        ],
        compiler_params=pltpu.CompilerParams(
            collective_id=0, has_side_effects=True, vmem_limit_bytes=60 << 20
        ),
    )(
        lengths, latent_codes.reshape(pairs, span, width),
        rope_keys.transpose(0, 1, 3, 2).reshape(pairs, rope, span),
        latent_scales.transpose(0, 1, 3, 2).reshape(pairs, blocks, span),
        query_latent.reshape(pairs, half, width), query_rope.reshape(pairs, half, rope),
        new_latent.reshape(pairs, tokens, width), new_rope.reshape(pairs, tokens, rope),
    )

    att, cache, crope, cscale = emit((att, cache, crope, cscale))

    def as_cache(values):
        flipped = values.reshape(layers, requests, values.shape[1], span).transpose(0, 1, 3, 2)
        return flipped.reshape(layers, requests, span, 1, values.shape[1])

    return (
        att.reshape(query_latent.shape),
        cache.reshape(layers, requests, span, 1, width),
        as_cache(cscale),
        as_cache(crope),
    )


def solution(mesh):
    placed = (
        P(None, ("group", "req", "sub"), "seq", None),
        P(None, ("group", "req", "sub"), "seq", None),
        P(None, ("group", "req", "sub"), "seq", None),
        P(("group", "req", "sub")),
        P(None, ("group", "req", "sub"), None, "seq", None),
        P(None, ("group", "req", "sub"), None, "seq", None),
        P(None, ("group", "req", "sub"), None, None),
        P(None, ("group", "req", "sub"), None, None),
    )
    return jax.shard_map(
        per_device_line if mesh.shape["seq"] == 4 else per_device,
        mesh=mesh,
        in_specs=placed,
        out_specs=(
            P(None, ("group", "req", "sub"), None, "seq", None),
            P(None, ("group", "req", "sub"), None, "seq", None),
            P(None, ("group", "req", "sub"), None, "seq", None),
            P(None, ("group", "req", "sub"), None, "seq", None),
        ),
        check_vma=False,
    )
```

```python
import jax
import jax.numpy as jnp
from jax import lax
from jax.experimental import pallas as pl
from jax.experimental.pallas import tpu as pltpu
from jax.sharding import PartitionSpec as P

softmax_gain = 192.0 ** (-0.5)
masked_score = -1e30


def dequantize(code_values, scale_values):
    blocks = scale_values.shape[-1]
    latent_width = code_values.shape[-1]
    shaped = code_values.astype(jnp.float32).reshape(
        code_values.shape[:-1] + (blocks, latent_width // blocks)
    )
    scaled = shaped * scale_values.astype(jnp.float32)[..., None]
    return scaled.reshape(code_values.shape).astype(jnp.bfloat16)


def shard_partial(
    lat_query, rope_query, key_rows, rope_rows, usable, new_keys, new_rope_rows, holds_new
):
    tokens_new, head_count, latent_width = lat_query.shape
    query_rows = lat_query.reshape(tokens_new * head_count, latent_width)
    query_pos = rope_query.reshape(tokens_new * head_count, rope_query.shape[-1])
    scores = jnp.dot(query_rows, key_rows.T, preferred_element_type=jnp.float32)
    scores = (
        scores + jnp.dot(query_pos, rope_rows.T, preferred_element_type=jnp.float32)
    ) * softmax_gain
    fresh_scores = jnp.dot(query_rows, new_keys.T, preferred_element_type=jnp.float32)
    fresh_scores = (
        fresh_scores + jnp.dot(query_pos, new_rope_rows.T, preferred_element_type=jnp.float32)
    ) * softmax_gain
    token_of_row = jnp.arange(tokens_new * head_count, dtype=jnp.int32) // head_count
    causal = (jnp.arange(tokens_new, dtype=jnp.int32)[None, :] <= token_of_row[:, None]) & holds_new
    scores = jnp.where(usable[None, :], scores, masked_score)
    fresh_scores = jnp.where(causal, fresh_scores, masked_score)
    group_peak = jnp.maximum(jnp.max(scores, 1), jnp.max(fresh_scores, 1)).astype(jnp.bfloat16)
    peak_float = group_peak.astype(jnp.float32)[:, None]
    weights = jnp.where(usable[None, :], jnp.exp(scores - peak_float), 0.0).astype(jnp.bfloat16)
    fresh_weights = jnp.where(causal, jnp.exp(fresh_scores - peak_float), 0.0).astype(jnp.bfloat16)
    group_total = jnp.sum(weights.astype(jnp.float32), 1) + jnp.sum(
        fresh_weights.astype(jnp.float32), 1
    )
    group_sum = jnp.dot(weights, key_rows, preferred_element_type=jnp.float32)
    group_sum = group_sum + jnp.dot(fresh_weights, new_keys, preferred_element_type=jnp.float32)
    return (
        group_sum.astype(jnp.bfloat16).reshape(tokens_new, head_count, latent_width),
        group_peak.reshape(tokens_new, head_count),
        group_total.astype(jnp.bfloat16).reshape(tokens_new, head_count),
    )


def merge_groups(pieces):
    group_sum, group_peak, group_total = pieces
    peak_float = group_peak.astype(jnp.float32)
    overall = jnp.max(peak_float, 0)
    factor = jnp.exp(peak_float - overall)
    numerator = jnp.sum(factor[..., None] * group_sum.astype(jnp.float32), 0)
    denominator = jnp.sum(factor * group_total.astype(jnp.float32), 0)
    return (numerator / denominator[..., None]).astype(jnp.bfloat16)


def per_device(
    latent_codes, latent_scales, rope_keys, lengths, query_latent, query_rope, new_latent, new_rope
):
    shard_count = lax.axis_size("seq")
    seq_index = lax.axis_index("seq")
    layer_count, request_count, span, latent_width = latent_codes.shape
    lat_query, rope_query = (
        lax.all_gather(query_latent, "seq", axis=3, tiled=True),
        lax.all_gather(query_rope, "seq", axis=3, tiled=True),
    )

    def regroup_rows(values):
        return values.reshape(
            values.shape[0], values.shape[1], span // shard_count, shard_count, values.shape[-1]
        )

    codes_moved, scales_moved, rope_moved = (
        lax.all_to_all(regroup_rows(latent_codes), "seq", split_axis=3, concat_axis=2, tiled=True),
        lax.all_to_all(regroup_rows(latent_scales), "seq", split_axis=3, concat_axis=2, tiled=True),
        lax.all_to_all(regroup_rows(rope_keys), "seq", split_axis=3, concat_axis=2, tiled=True),
    )
    offsets = jnp.arange(span, dtype=jnp.int32)
    key_rows = dequantize(latent_codes, latent_scales)
    positions = seq_index * span + offsets
    usable = positions[None, :] < lengths[:, None]
    holds_new = seq_index == 0
    per_request = jax.vmap(shard_partial, in_axes=(0, 0, 0, 0, 0, 0, 0, None))
    per_layer = jax.vmap(per_request, in_axes=(0, 0, 0, 0, None, 0, 0, None))
    group_sum, group_peak, group_total = per_layer(
        lat_query, rope_query, key_rows, rope_keys, usable, new_latent, new_rope, holds_new
    )
    attended = merge_groups(
        (
            lax.all_to_all(group_sum[None], "seq", split_axis=4, concat_axis=0, tiled=True),
            lax.all_to_all(group_peak[None], "seq", split_axis=4, concat_axis=0, tiled=True),
            lax.all_to_all(group_total[None], "seq", split_axis=4, concat_axis=0, tiled=True),
        )
    )
    return (attended, codes_moved, scales_moved, rope_moved)


def _hub_kernel(
    len_ref, codes_ref, rope_ref, scale_ref, q_ref, qr_ref, new_ref, newr_ref,
    att_ref, cache_ref, crope_ref, cscale_ref,
    perm, kbuf, abuf, sbuf, scale_in, scale_rows, raw, rawr, raws, rawq, qbuf, qrbuf, nkbuf, nrbuf,
    keys, result, side_sum, side_stat, far_out, far_out_stat, far_in, far_in_stat,
    new_rows, newr_rows, scales_out, out_sem, load_sem, keep_sem, q_send, q_recv, k_send, k_recv, f_send, f_recv, s_send, s_recv,
    far_send, far_recv, r_send, r_recv,
):
    pairs, span, width = codes_ref.shape
    groups = 4
    rows = span // groups
    half = q_ref.shape[1]
    rope = qr_ref.shape[2]
    blocks = scale_ref.shape[1]
    fresh = new_ref.shape[1]
    heads = half // fresh
    fold = half * rope // 128
    me = lax.axis_index("seq")
    is_hub = (me == 1) | (me == 2)
    is_edge = jnp.logical_not(is_hub)
    hub = 1 + me // 2
    edge = me // 2 * 3
    across = 3 - hub
    far_edge = 3 - edge
    f32, bf16 = jnp.float32, jnp.bfloat16

    def start(copies):
        for copy in copies:
            copy.start()

    def remote(src, dst, send, recv, target):
        return pltpu.make_async_remote_copy(
            src_ref=src, dst_ref=dst, send_sem=send, recv_sem=recv,
            device_id={"seq": target}, device_id_type=pl.DeviceIdType.MESH,
        )

    def greet(target):
        pl.semaphore_signal(
            pltpu.get_barrier_semaphore(), inc=1, device_id={"seq": target},
            device_id_type=pl.DeviceIdType.MESH,
        )

    def load(c):
        return (
            pltpu.make_async_copy(codes_ref.at[c], raw.at[c], load_sem.at[0, c]),
            pltpu.make_async_copy(rope_ref.at[c], rawr.at[c], load_sem.at[1, c]),
        )

    def load_scales(c):
        return pltpu.make_async_copy(scale_ref.at[c], raws.at[c], load_sem.at[2, c])

    def load_rotary(c):
        return pltpu.make_async_copy(qr_ref.at[c], rawq.at[c], load_sem.at[4, c])

    def load_new():
        return (
            pltpu.make_async_copy(new_ref, new_rows, out_sem.at[0]),
            pltpu.make_async_copy(newr_ref, newr_rows, out_sem.at[1]),
        )

    def out_scales():
        return pltpu.make_async_copy(scales_out, cscale_ref, out_sem.at[2])

    def load_query(c):
        return pltpu.make_async_copy(q_ref.at[c], qbuf.at[c, 0], load_sem.at[3, c])

    def query_latent(c, flow, src, dst, target):
        return remote(q_ref.at[c] if src == 0 else qbuf.at[c, src], qbuf.at[c, dst],
                      q_send.at[0, flow, c], q_recv.at[0, dst, c], target)

    def query_rotary(c, flow, src, dst, target):
        return remote(qrbuf.at[c, src], qrbuf.at[c, dst],
                      q_send.at[1, flow, c], q_recv.at[1, dst, c], target)

    def queries(c, flow, src, dst, target):
        return (query_latent(c, flow, src, dst, target), query_rotary(c, flow, src, dst, target))

    def await_queries(c, slot):
        for copy in queries(c, 0, 0, slot, across):
            copy.wait_recv()

    def shard(c):
        return (
            remote(abuf.at[0, c], abuf.at[1, c], k_send.at[0, c], k_recv.at[0, c], hub),
            remote(kbuf.at[0, c], kbuf.at[1, c], k_send.at[1, c], k_recv.at[1, c], hub),
        )

    def shard_scales():
        return remote(sbuf.at[0], sbuf.at[1], s_send.at[2, 0], s_recv.at[groups], hub)

    def place_of(slot):
        return hub if slot == 0 else edge

    def handover(slot, c, target, lane):
        place = place_of(slot)
        spot = pl.multiple_of(place * rows, rows)
        return (
            remote(kbuf.at[slot, c, target], cache_ref.at[c, pl.ds(spot, rows)],
                   f_send.at[0, slot, lane, c], f_recv.at[0, place, c], target),
            remote(abuf.at[slot, c, target], crope_ref.at[c, :, pl.ds(spot, rows)],
                   f_send.at[1, slot, lane, c], f_recv.at[1, place, c], target),
        )

    def handover_far(slot, c):
        return handover(slot, c, far_edge, 1) + handover(slot, c, across, 0)

    def handover_scales(slot, target, lane):
        return remote(sbuf.at[slot, target], scale_in.at[place_of(slot)],
                      s_send.at[slot, lane], s_recv.at[place_of(slot)], target)

    def await_handover(c, place):
        spot = pl.multiple_of(place * rows, rows)
        remote(kbuf.at[0, c, 0], cache_ref.at[c, pl.ds(spot, rows)],
               f_send.at[0, 0, 0, c], f_recv.at[0, place, c], across).wait_recv()
        remote(abuf.at[0, c, 0], crope_ref.at[c, :, pl.ds(spot, rows)],
               f_send.at[1, 0, 0, c], f_recv.at[1, place, c], across).wait_recv()

    def keep_scales(tile, place):
        values = tile.astype(f32)
        for c in range(pairs):
            scales_out[c, :, pl.ds(pl.multiple_of(place * rows, rows), rows)] = (
                values[c * blocks:(c + 1) * blocks].astype(bf16)
            )

    def await_scales(place):
        remote(sbuf.at[0, 0], scale_in.at[place], s_send.at[0, 0], s_recv.at[place], across).wait_recv()
        keep_scales(scale_in[place], place)

    def keep(slot, c, place):
        spot = pl.multiple_of(place * rows, rows)
        return (
            pltpu.make_async_copy(
                kbuf.at[slot, c, me], cache_ref.at[c, pl.ds(spot, rows)], keep_sem.at[0, slot, c]
            ),
            pltpu.make_async_copy(
                abuf.at[slot, c, me], crope_ref.at[c, :, pl.ds(spot, rows)], keep_sem.at[1, slot, c]
            ),
        )

    def sums(c):
        return (
            remote(far_out.at[c], far_in.at[c], far_send.at[0, c], far_recv.at[0, c], across),
            remote(far_out_stat.at[c], far_in_stat.at[c], far_send.at[1, c], far_recv.at[1, c], across),
        )

    def own_result(c):
        return pltpu.make_async_copy(result.at[c, 0], att_ref.at[c], load_sem.at[5, c])

    def edge_result(c):
        return remote(result.at[c, 1], att_ref.at[c], r_send.at[c], r_recv.at[c], edge)

    @pl.when(is_hub)
    def _():
        greet(across)
        greet(edge)

    @pl.when(is_edge)
    def _():
        greet(across)
        greet(hub)

    for c in range(pairs):
        load_rotary(c).start()
    for c in range(pairs):
        load_scales(c).start()
        start(load(c))

    @pl.when(is_hub)
    def _():
        pl.semaphore_wait(pltpu.get_barrier_semaphore(), 3)
        for c in range(pairs):
            query_latent(c, 1, 0, 2, across).start()
        for c in range(pairs):
            load_query(c).start()
        start(load_new())

    @pl.when(is_edge)
    def _():
        pl.semaphore_wait(pltpu.get_barrier_semaphore(), 1)
        query_latent(0, 0, 0, 1, hub).start()

    for c in range(pairs):
        load_rotary(c).wait()
        qrbuf[c, 0] = jnp.concatenate(
            [rawq[c, i * fold:(i + 1) * fold, :] for i in range(half // fold)], axis=1
        )

    @pl.when(is_hub)
    def _():
        for c in range(pairs):
            query_rotary(c, 1, 0, 2, across).start()

    @pl.when(is_edge)
    def _():
        query_rotary(0, 0, 0, 1, hub).start()

    line = lax.broadcasted_iota(jnp.int32, (span, span), 0)
    column = lax.broadcasted_iota(jnp.int32, (span, span), 1)
    perm[...] = jnp.where(column == (line % rows) * groups + line // rows, 1.0, 0.0).astype(bf16)
    dims = (((1,), (1,)), ((), ()))

    tile_rows = sbuf.shape[2]
    for c in range(pairs):
        load_scales(c).wait()
    stacked = [raws[c].astype(f32) for c in range(pairs)]
    if tile_rows > pairs * blocks:
        stacked.append(jnp.zeros((tile_rows - pairs * blocks, span), f32))
    stacked = jnp.concatenate(stacked, axis=0).astype(bf16)
    sorted_scales = lax.dot_general(stacked, perm[...], dims, preferred_element_type=f32)
    for k in range(groups):
        sbuf[0, k] = sorted_scales[:, k * rows:(k + 1) * rows].astype(bf16)
    keep_scales(sbuf[0, me], me)

    def spread_scales(slot):
        scale_rows[slot] = jnp.zeros(scale_rows.shape[1:], f32)
        for k in range(groups):
            values = sbuf[slot, k].astype(f32)
            for c in range(pairs):
                scale_rows[slot, c, 0:blocks, k * rows:(k + 1) * rows] = (
                    values[c * blocks:(c + 1) * blocks]
                )

    def prepare(c):
        for copy in load(c):
            copy.wait()
        sorted_codes = jnp.dot(perm[...], raw[c], preferred_element_type=f32)
        for k in range(groups):
            kbuf[0, c, k] = sorted_codes[k * rows:(k + 1) * rows].astype(bf16)
        sorted_rope = lax.dot_general(rawr[c], perm[...], dims, preferred_element_type=f32)
        for k in range(groups):
            abuf[0, c, k] = sorted_rope[:, k * rows:(k + 1) * rows].astype(bf16)

    def stats_of(m, d):
        lane = lax.broadcasted_iota(jnp.int32, (half, 128), 1)
        return jnp.where(
            lane < 2, jnp.where(lane == 0, m[:half], d[:half]), jnp.where(lane == 2, m[half:], d[half:])
        ).T[0:8]

    def columns_of(stat, j):
        return stat[:, 2 * j:2 * j + 1], stat[:, 2 * j + 1:2 * j + 2]

    def dequantize_keys(c):
        for slot in range(2):
            scales = scale_rows[slot, c].T
            for k in range(groups):
                for b in range(blocks):
                    lanes = slice(b * (width // blocks), (b + 1) * (width // blocks))
                    keys[slot * span + k * rows:slot * span + (k + 1) * rows, lanes] = (
                        kbuf[slot, c, k, :, lanes].astype(f32)
                        * scales[k * rows:(k + 1) * rows, b:b + 1]
                    ).astype(bf16)

    def partial(c, first):
        q = qbuf[c, first:first + 2].reshape(2 * half, width)
        qr = jnp.concatenate(
            [qrbuf[c, first + j, :, i * rope:(i + 1) * rope] for j in range(2) for i in range(half // fold)],
            axis=0,
        )
        ropes = jnp.concatenate(
            [abuf[slot, c, k] for slot in range(2) for k in range(groups)], axis=1
        )
        s = lax.dot_general(q, keys[...], dims, preferred_element_type=f32)
        s = (s + jnp.dot(qr, ropes, preferred_element_type=f32)) * softmax_gain
        column = lax.broadcasted_iota(jnp.int32, (1, 2 * span), 1)
        local = column % span
        position = jnp.where(column < span, hub, edge) * span + local % rows * groups + local // rows
        s = jnp.where(position < len_ref[c % len_ref.shape[0]], s, masked_score)
        m = jnp.max(s, axis=1, keepdims=True)
        if first == 0:
            t = lax.dot_general(q, nkbuf[c], dims, preferred_element_type=f32)
            t = (t + lax.dot_general(qr, nrbuf[c], dims, preferred_element_type=f32)) * softmax_gain
            token = lax.broadcasted_iota(jnp.int32, t.shape, 0) % half // heads
            t = jnp.where(lax.broadcasted_iota(jnp.int32, t.shape, 1) <= token, t, masked_score)
            m = jnp.maximum(m, jnp.max(t, axis=1, keepdims=True))
        w = jnp.exp(s - m).astype(bf16)
        d = jnp.sum(w.astype(f32), axis=1, keepdims=True)
        n = jnp.dot(w, keys[...], preferred_element_type=f32)
        if first == 0:
            v = jnp.exp(t - m).astype(bf16)
            d = d + jnp.sum(v.astype(f32), axis=1, keepdims=True)
            n = n + jnp.dot(v, nkbuf[c], preferred_element_type=f32)
        return n, stats_of(m, d)

    def merge(c):
        for copy in sums(c):
            copy.wait_recv()
        side, far = side_stat[c].T, far_in_stat[c].T
        for j in (1, 0):
            m0, d0 = columns_of(side, j)
            m1, d1 = columns_of(far, j)
            m = jnp.maximum(m0, m1)
            f0, f1 = jnp.exp(m0 - m), jnp.exp(m1 - m)
            numerator = f0 * side_sum[c, j] + f1 * far_in[c, j].astype(f32)
            result[c, j] = (numerator / (f0 * d0 + f1 * d1)).astype(bf16)
            if j == 1:
                edge_result(c).start()
        own_result(c).start()

    @pl.when(is_edge)
    def _():
        shard_scales().start()

        @pl.loop(0, pairs)
        def _(c):
            prepare(c)

            @pl.when(c >= 1)
            def _():
                for copy in shard(c - 1):
                    copy.wait_send()

                start(queries(c, 0, 0, 1, hub))

            start(shard(c))
            start(keep(0, c, me))

        for copy in shard(pairs - 1):
            copy.wait_send()
        for place in (hub, across, far_edge):
            await_scales(place)
        out_scales().start()

        @pl.loop(0, pairs)
        def _(c):
            for place in (hub, across, far_edge):
                await_handover(c, place)
            edge_result(c).wait_recv()
            for copy in keep(0, c, me):
                copy.wait()
            for copy in queries(c, 0, 0, 1, hub):
                copy.wait_send()

        shard_scales().wait_send()
        out_scales().wait()

    @pl.when(is_hub)
    def _():
        handover_scales(0, edge, 2).start()

        @pl.loop(0, pairs)
        def _(c):
            prepare(c)
            start(handover(0, c, edge, 2))
            start(keep(0, c, me))

        for lane, target in ((0, across), (1, far_edge)):
            handover_scales(0, target, lane).start()
        await_queries(0, 1)
        start(queries(0, 2, 1, 3, across))
        start(handover_far(0, 0))
        for copy in load_new():
            copy.wait()
        nkbuf[...] = jnp.zeros(nkbuf.shape, bf16)
        nrbuf[...] = jnp.zeros(nrbuf.shape, bf16)
        for c in range(pairs):
            nkbuf[c, 0:fresh, :] = new_rows[c]
            nrbuf[c, 0:fresh, :] = newr_rows[c]
            load_query(c).wait()
        spread_scales(0)
        shard_scales().wait_recv()
        for lane, target in ((0, across), (1, far_edge)):
            handover_scales(1, target, lane).start()
        keep_scales(sbuf[1, me], edge)
        spread_scales(1)

        @pl.loop(0, pairs)
        def _(c):
            for copy in shard(c):
                copy.wait_recv()
            start(handover_far(1, c))
            start(keep(1, c, edge))

            @pl.when(c < pairs - 1)
            def _():
                await_queries(c + 1, 1)
                start(queries(c + 1, 2, 1, 3, across))

            await_queries(c, 2)
            await_queries(c, 3)
            dequantize_keys(c)
            far_sum, far_out_stat[c] = partial(c, 2)
            for j in range(2):
                far_out[c, j] = far_sum[j * half:(j + 1) * half].astype(bf16)
            start(sums(c))
            @pl.when(c == 1)
            def _():
                start(handover_far(0, c))

            near_sum, side_stat[c] = partial(c, 0)
            for j in range(2):
                side_sum[c, j] = near_sum[j * half:(j + 1) * half]

            @pl.when(c >= 1)
            def _():
                merge(c - 1)

        for c in range(2, pairs):
            start(handover_far(0, c))
        for place in (across, far_edge):
            await_scales(place)
        out_scales().start()
        merge(pairs - 1)

        @pl.loop(0, pairs)
        def _(c):
            for place in (across, far_edge):
                await_handover(c, place)
            for copy in keep(0, c, me) + keep(1, c, edge):
                copy.wait()
            own_result(c).wait()
            for copy in handover(0, c, edge, 2) + handover_far(0, c) + handover_far(1, c):
                copy.wait_send()
            for copy in queries(c, 1, 0, 2, across) + queries(c, 2, 1, 3, across) + sums(c):
                copy.wait_send()
            edge_result(c).wait_send()

        out_scales().wait()
        handover_scales(0, edge, 2).wait_send()
        for lane, target in ((0, across), (1, far_edge)):
            handover_scales(0, target, lane).wait_send()
            handover_scales(1, target, lane).wait_send()


def _emit_kernel(att_ref, cache_ref, crope_ref, cscale_ref, att_out, cache_out, crope_out, cscale_out, sem):
    copies = []
    for c in range(cache_ref.shape[0]):
        copies.append(pltpu.make_async_copy(cache_ref.at[c], cache_out.at[c], sem.at[len(copies)]))
    for src, dst in ((att_ref, att_out), (crope_ref, crope_out), (cscale_ref, cscale_out)):
        copies.append(pltpu.make_async_copy(src, dst, sem.at[len(copies)]))
    for copy in copies:
        copy.start()
    for copy in copies:
        copy.wait()


def emit(values):
    return pl.pallas_call(
        _emit_kernel,
        out_shape=[jax.ShapeDtypeStruct(v.shape, v.dtype) for v in values],
        in_specs=[pl.BlockSpec(memory_space=pl.ANY)] * 4,
        out_specs=[pl.BlockSpec(memory_space=pl.ANY)] * 4,
        scratch_shapes=[pltpu.SemaphoreType.DMA((values[1].shape[0] + 3,))],
        compiler_params=pltpu.CompilerParams(vmem_limit_bytes=1 << 20),
    )(*values)


def per_device_line(
    latent_codes, latent_scales, rope_keys, lengths, query_latent, query_rope, new_latent, new_rope
):
    layers, requests, span, width = latent_codes.shape
    pairs, rows = layers * requests, span // 4
    rope, blocks = rope_keys.shape[-1], latent_scales.shape[-1]
    tokens, heads = query_latent.shape[2:4]
    half = tokens * heads
    tile_rows = -(-pairs * blocks // 16) * 16
    hbm_spec = pl.BlockSpec(memory_space=pltpu.HBM)
    any_spec = pl.BlockSpec(memory_space=pl.ANY)
    dma = pltpu.SemaphoreType.DMA
    bf16, f32 = jnp.bfloat16, jnp.float32
    att, cache, crope, cscale = pl.pallas_call(
        _hub_kernel,
        out_shape=(
            pltpu.VMEM((pairs, half, width), bf16),
            pltpu.VMEM((pairs, span, width), bf16),
            pltpu.VMEM((pairs, rope, span), bf16),
            pltpu.VMEM((pairs, blocks, span), bf16),
        ),
        in_specs=[pl.BlockSpec(memory_space=pltpu.SMEM)] + [hbm_spec] * 7,
        out_specs=(any_spec, any_spec, any_spec, any_spec),
        scratch_shapes=[
            pltpu.VMEM((span, span), bf16),
            pltpu.VMEM((2, pairs, 4, rows, width), bf16),
            pltpu.VMEM((2, pairs, 4, rope, rows), bf16),
            pltpu.VMEM((2, 4, tile_rows, rows), bf16),
            pltpu.VMEM((4, tile_rows, rows), bf16),
            pltpu.VMEM((2, pairs, 8, span), f32),
            pltpu.VMEM((pairs, span, width), bf16),
            pltpu.VMEM((pairs, rope, span), bf16),
            pltpu.VMEM((pairs, blocks, span), bf16),
            pltpu.VMEM((pairs, half, rope), bf16),
            pltpu.VMEM((pairs, 4, half, width), bf16),
            pltpu.VMEM((pairs, 4, half * rope // 128, 128), bf16),
            pltpu.VMEM((pairs, 128, width), bf16),
            pltpu.VMEM((pairs, 128, rope), bf16),
            pltpu.VMEM((2 * span, width), bf16),
            pltpu.VMEM((pairs, 2, half, width), bf16),
            pltpu.VMEM((pairs, 2, half, width), f32),
            pltpu.VMEM((pairs, 8, 128), f32),
            pltpu.VMEM((pairs, 2, half, width), bf16),
            pltpu.VMEM((pairs, 8, 128), f32),
            pltpu.VMEM((pairs, 2, half, width), bf16),
            pltpu.VMEM((pairs, 8, 128), f32),
            pltpu.VMEM((pairs, tokens, width), bf16),
            pltpu.VMEM((pairs, tokens, rope), bf16),
            pltpu.VMEM((pairs, blocks, span), bf16),
            dma((3,)), dma((6, pairs)), dma((2, 2, pairs)), dma((2, 3, pairs)), dma((2, 4, pairs)),
            dma((2, pairs)), dma((2, pairs)), dma((2, 2, 3, pairs)), dma((2, 4, pairs)),
            dma((3, 3)), dma((5,)), dma((2, pairs)), dma((2, pairs)), dma((pairs,)), dma((pairs,)),
        ],
        compiler_params=pltpu.CompilerParams(
            collective_id=0, has_side_effects=True, vmem_limit_bytes=56 << 20
        ),
    )(
        lengths, latent_codes.reshape(pairs, span, width),
        rope_keys.transpose(0, 1, 3, 2).reshape(pairs, rope, span),
        latent_scales.transpose(0, 1, 3, 2).reshape(pairs, blocks, span),
        query_latent.reshape(pairs, half, width), query_rope.reshape(pairs, half, rope),
        new_latent.reshape(pairs, tokens, width), new_rope.reshape(pairs, tokens, rope),
    )

    att, cache, crope, cscale = emit((att, cache, crope, cscale))

    def as_cache(values):
        flipped = values.reshape(layers, requests, values.shape[1], span).transpose(0, 1, 3, 2)
        return flipped.reshape(layers, requests, span, 1, values.shape[1])

    return (
        att.reshape(query_latent.shape),
        cache.reshape(layers, requests, span, 1, width),
        as_cache(cscale),
        as_cache(crope),
    )


def solution(mesh):
    placed = (
        P(None, ("group", "req", "sub"), "seq", None),
        P(None, ("group", "req", "sub"), "seq", None),
        P(None, ("group", "req", "sub"), "seq", None),
        P(("group", "req", "sub")),
        P(None, ("group", "req", "sub"), None, "seq", None),
        P(None, ("group", "req", "sub"), None, "seq", None),
        P(None, ("group", "req", "sub"), None, None),
        P(None, ("group", "req", "sub"), None, None),
    )
    return jax.shard_map(
        per_device_line if mesh.shape["seq"] == 4 else per_device,
        mesh=mesh,
        in_specs=placed,
        out_specs=(
            P(None, ("group", "req", "sub"), None, "seq", None),
            P(None, ("group", "req", "sub"), None, "seq", None),
            P(None, ("group", "req", "sub"), None, "seq", None),
            P(None, ("group", "req", "sub"), None, "seq", None),
        ),
        check_vma=False,
    )
```

```python
import jax
import jax.numpy as jnp
from jax import lax
from jax.experimental import pallas as pl
from jax.experimental.pallas import tpu as pltpu
from jax.sharding import PartitionSpec as P

softmax_gain = 192.0 ** (-0.5)
masked_score = -1e30


def dequantize(code_values, scale_values):
    blocks = scale_values.shape[-1]
    latent_width = code_values.shape[-1]
    shaped = code_values.astype(jnp.float32).reshape(
        code_values.shape[:-1] + (blocks, latent_width // blocks)
    )
    scaled = shaped * scale_values.astype(jnp.float32)[..., None]
    return scaled.reshape(code_values.shape).astype(jnp.bfloat16)


def shard_partial(
    lat_query, rope_query, key_rows, rope_rows, usable, new_keys, new_rope_rows, holds_new
):
    tokens_new, head_count, latent_width = lat_query.shape
    query_rows = lat_query.reshape(tokens_new * head_count, latent_width)
    query_pos = rope_query.reshape(tokens_new * head_count, rope_query.shape[-1])
    scores = jnp.dot(query_rows, key_rows.T, preferred_element_type=jnp.float32)
    scores = (
        scores + jnp.dot(query_pos, rope_rows.T, preferred_element_type=jnp.float32)
    ) * softmax_gain
    fresh_scores = jnp.dot(query_rows, new_keys.T, preferred_element_type=jnp.float32)
    fresh_scores = (
        fresh_scores + jnp.dot(query_pos, new_rope_rows.T, preferred_element_type=jnp.float32)
    ) * softmax_gain
    token_of_row = jnp.arange(tokens_new * head_count, dtype=jnp.int32) // head_count
    causal = (jnp.arange(tokens_new, dtype=jnp.int32)[None, :] <= token_of_row[:, None]) & holds_new
    scores = jnp.where(usable[None, :], scores, masked_score)
    fresh_scores = jnp.where(causal, fresh_scores, masked_score)
    group_peak = jnp.maximum(jnp.max(scores, 1), jnp.max(fresh_scores, 1)).astype(jnp.bfloat16)
    peak_float = group_peak.astype(jnp.float32)[:, None]
    weights = jnp.where(usable[None, :], jnp.exp(scores - peak_float), 0.0).astype(jnp.bfloat16)
    fresh_weights = jnp.where(causal, jnp.exp(fresh_scores - peak_float), 0.0).astype(jnp.bfloat16)
    group_total = jnp.sum(weights.astype(jnp.float32), 1) + jnp.sum(
        fresh_weights.astype(jnp.float32), 1
    )
    group_sum = jnp.dot(weights, key_rows, preferred_element_type=jnp.float32)
    group_sum = group_sum + jnp.dot(fresh_weights, new_keys, preferred_element_type=jnp.float32)
    return (
        group_sum.astype(jnp.bfloat16).reshape(tokens_new, head_count, latent_width),
        group_peak.reshape(tokens_new, head_count),
        group_total.astype(jnp.bfloat16).reshape(tokens_new, head_count),
    )


def merge_groups(pieces):
    group_sum, group_peak, group_total = pieces
    peak_float = group_peak.astype(jnp.float32)
    overall = jnp.max(peak_float, 0)
    factor = jnp.exp(peak_float - overall)
    numerator = jnp.sum(factor[..., None] * group_sum.astype(jnp.float32), 0)
    denominator = jnp.sum(factor * group_total.astype(jnp.float32), 0)
    return (numerator / denominator[..., None]).astype(jnp.bfloat16)


def per_device(
    latent_codes, latent_scales, rope_keys, lengths, query_latent, query_rope, new_latent, new_rope
):
    shard_count = lax.axis_size("seq")
    seq_index = lax.axis_index("seq")
    layer_count, request_count, span, latent_width = latent_codes.shape
    lat_query, rope_query = (
        lax.all_gather(query_latent, "seq", axis=3, tiled=True),
        lax.all_gather(query_rope, "seq", axis=3, tiled=True),
    )

    def regroup_rows(values):
        return values.reshape(
            values.shape[0], values.shape[1], span // shard_count, shard_count, values.shape[-1]
        )

    codes_moved, scales_moved, rope_moved = (
        lax.all_to_all(regroup_rows(latent_codes), "seq", split_axis=3, concat_axis=2, tiled=True),
        lax.all_to_all(regroup_rows(latent_scales), "seq", split_axis=3, concat_axis=2, tiled=True),
        lax.all_to_all(regroup_rows(rope_keys), "seq", split_axis=3, concat_axis=2, tiled=True),
    )
    offsets = jnp.arange(span, dtype=jnp.int32)
    key_rows = dequantize(latent_codes, latent_scales)
    positions = seq_index * span + offsets
    usable = positions[None, :] < lengths[:, None]
    holds_new = seq_index == 0
    per_request = jax.vmap(shard_partial, in_axes=(0, 0, 0, 0, 0, 0, 0, None))
    per_layer = jax.vmap(per_request, in_axes=(0, 0, 0, 0, None, 0, 0, None))
    group_sum, group_peak, group_total = per_layer(
        lat_query, rope_query, key_rows, rope_keys, usable, new_latent, new_rope, holds_new
    )
    attended = merge_groups(
        (
            lax.all_to_all(group_sum[None], "seq", split_axis=4, concat_axis=0, tiled=True),
            lax.all_to_all(group_peak[None], "seq", split_axis=4, concat_axis=0, tiled=True),
            lax.all_to_all(group_total[None], "seq", split_axis=4, concat_axis=0, tiled=True),
        )
    )
    return (attended, codes_moved, scales_moved, rope_moved)


def _hub_kernel(
    len_ref, codes_ref, rope_ref, scale_ref, q_ref, qr_ref, new_ref, newr_ref,
    att_ref, cache_ref, crope_ref, cscale_ref,
    lengths, perm, kbuf, abuf, sbuf, scale_in, scale_rows, raw, raws, rawq, qbuf, nkbuf, nrbuf,
    new_rows, newr_rows, keys, result, side_sum, side_stat, far_out, far_out_stat, far_in, far_in_stat,
    meter, load_sem, misc_sem, q_send, q_recv, k_send, k_recv, f_send, f_recv, s_send, s_recv,
    far_send, far_recv, r_send, r_recv,
):
    pairs, span, width = codes_ref.shape
    groups = 4
    rows = span // groups
    half = q_ref.shape[1]
    rope = qr_ref.shape[2]
    blocks = scale_ref.shape[1]
    fresh = new_ref.shape[1]
    heads = half // fresh
    fold = half * rope // width
    me = lax.axis_index("seq")
    is_hub = (me == 1) | (me == 2)
    is_edge = jnp.logical_not(is_hub)
    hub = 1 + me // 2
    edge = me // 2 * 3
    across = 3 - hub
    far_edge = 3 - edge
    f32, bf16 = jnp.float32, jnp.bfloat16

    def start(copies):
        for copy in copies:
            copy.start()

    def remote(src, dst, send, recv, target):
        return pltpu.make_async_remote_copy(
            src_ref=src, dst_ref=dst, send_sem=send, recv_sem=recv,
            device_id={"seq": target}, device_id_type=pl.DeviceIdType.MESH,
        )

    def greet(target):
        pl.semaphore_signal(
            pltpu.get_barrier_semaphore(), inc=1, device_id={"seq": target},
            device_id_type=pl.DeviceIdType.MESH,
        )

    def wait_bytes(ref, sem):
        pltpu.make_async_copy(ref, ref, sem).wait()

    def load(c):
        return (
            pltpu.make_async_copy(codes_ref.at[c], raw.at[c, pl.ds(0, span)], load_sem.at[c]),
            pltpu.make_async_copy(rope_ref.at[c], raw.at[c, pl.ds(span, rope)], load_sem.at[c]),
        )

    load_scales = pltpu.make_async_copy(scale_ref, raws, misc_sem.at[0])
    load_rotary = pltpu.make_async_copy(qr_ref, rawq, misc_sem.at[1])
    load_query = pltpu.make_async_copy(q_ref, qbuf.at[:, 0, pl.ds(0, half)], misc_sem.at[2])
    load_new = (
        pltpu.make_async_copy(new_ref, new_rows, misc_sem.at[3]),
        pltpu.make_async_copy(newr_ref, newr_rows, misc_sem.at[4]),
    )
    load_lengths = pltpu.make_async_copy(len_ref, lengths, misc_sem.at[5])

    def query_latent(c, flow, dst, target):
        return remote(q_ref.at[c], qbuf.at[c, dst, pl.ds(0, half)],
                      q_send.at[flow], q_recv.at[flow, c], target)

    def query_rotary(c, flow, dst, target):
        return remote(qbuf.at[c, 0, pl.ds(half, fold)], qbuf.at[c, dst, pl.ds(half, fold)],
                      q_send.at[flow], q_recv.at[flow, c], target)

    def forward_query(c):
        return remote(qbuf.at[c, 1], qbuf.at[c, 3], q_send.at[2], q_recv.at[1, c], across)

    def shard(c):
        return (
            remote(abuf.at[0, c], abuf.at[1, c], k_send.at[c], k_recv.at[c], hub),
            remote(kbuf.at[0, c], kbuf.at[1, c], k_send.at[c], k_recv.at[c], hub),
        )

    shard_scales = remote(sbuf.at[0], sbuf.at[1], s_send.at[0], s_recv.at[groups], hub)

    def place_of(slot):
        return hub if slot == 0 else edge

    def handover(slot, c, target, send):
        place = place_of(slot)
        spot = pl.multiple_of(place * rows, rows)
        return (
            remote(kbuf.at[slot, c, target], cache_ref.at[c, pl.ds(spot, rows)],
                   f_send.at[send], f_recv.at[place], target),
            remote(abuf.at[slot, c, target], crope_ref.at[c, :, pl.ds(spot, rows)],
                   f_send.at[send], f_recv.at[place], target),
        )

    def handover_far(slot, c):
        return handover(slot, c, far_edge, 1 + slot) + handover(slot, c, across, 1 + slot)

    def handover_scales(slot, target, send):
        return remote(sbuf.at[slot, target], scale_in.at[place_of(slot)],
                      s_send.at[send], s_recv.at[place_of(slot)], target)

    def keep_scales(tile, place):
        values = tile.astype(f32)
        for c in range(pairs):
            cscale_ref[c, :, pl.ds(pl.multiple_of(place * rows, rows), rows)] = (
                values[c * blocks:(c + 1) * blocks].astype(bf16)
            )

    def await_scales(place):
        wait_bytes(scale_in.at[place], s_recv.at[place])
        keep_scales(scale_in[place], place)

    def keep(slot, c, place):
        spot = pl.multiple_of(place * rows, rows)
        cache_ref[c, pl.ds(spot, rows), :] = kbuf[slot, c, me]
        crope_ref[c, :, pl.ds(spot, rows)] = abuf[slot, c, me]

    def sums(c):
        return (
            remote(far_out.at[c], far_in.at[c], far_send.at[0], far_recv.at[c], across),
            remote(far_out_stat.at[c], far_in_stat.at[c], far_send.at[0], far_recv.at[c], across),
        )

    def edge_result(c):
        return remote(result.at[c], att_ref.at[c], r_send.at[0], r_recv.at[0], edge)

    @pl.when(is_hub)
    def _():
        greet(across)
        greet(edge)

    @pl.when(is_edge)
    def _():
        greet(across)
        greet(hub)

    start((load_rotary, load_scales))
    for c in range(pairs):
        start(load(c))
    load_lengths.start()

    @pl.when(is_hub)
    def _():
        pl.semaphore_wait(pltpu.get_barrier_semaphore(), 3)
        for c in range(pairs):
            query_latent(c, 1, 2, across).start()
        load_query.start()
        start(load_new)

    @pl.when(is_edge)
    def _():
        pl.semaphore_wait(pltpu.get_barrier_semaphore(), 1)
        query_latent(0, 0, 1, hub).start()

    load_rotary.wait()
    for c in range(pairs):
        qbuf[c, 0, half:half + fold, :] = jnp.concatenate(
            [rawq[c, i * fold:(i + 1) * fold, :] for i in range(half // fold)], axis=1
        )

    @pl.when(is_hub)
    def _():
        for c in range(pairs):
            query_rotary(c, 1, 2, across).start()

    @pl.when(is_edge)
    def _():
        query_rotary(0, 0, 1, hub).start()

    line = lax.broadcasted_iota(jnp.int32, (span, span), 0)
    column = lax.broadcasted_iota(jnp.int32, (span, span), 1)
    perm[...] = jnp.where(column == (line % rows) * groups + line // rows, 1.0, 0.0).astype(bf16)
    dims = (((1,), (1,)), ((), ()))

    tile_rows = sbuf.shape[2]
    load_scales.wait()
    load_lengths.wait()
    stacked = [raws[c].astype(f32) for c in range(pairs)]
    if tile_rows > pairs * blocks:
        stacked.append(jnp.zeros((tile_rows - pairs * blocks, span), f32))
    stacked = jnp.concatenate(stacked, axis=0).astype(bf16)
    sorted_scales = lax.dot_general(stacked, perm[...], dims, preferred_element_type=f32)
    for k in range(groups):
        sbuf[0, k] = sorted_scales[:, k * rows:(k + 1) * rows].astype(bf16)
    keep_scales(sbuf[0, me], me)

    def spread_scales(slot):
        scale_rows[slot] = jnp.zeros(scale_rows.shape[1:], f32)
        for k in range(groups):
            values = sbuf[slot, k].astype(f32)
            for c in range(pairs):
                scale_rows[slot, c, 0:blocks, k * rows:(k + 1) * rows] = (
                    values[c * blocks:(c + 1) * blocks]
                )

    def prepare(c):
        wait_bytes(raw.at[c], load_sem.at[c])
        sorted_codes = jnp.dot(perm[...], raw[c, 0:span], preferred_element_type=f32)
        for k in range(groups):
            kbuf[0, c, k] = sorted_codes[k * rows:(k + 1) * rows].astype(bf16)
        sorted_rope = lax.dot_general(raw[c, span:span + rope], perm[...], dims, preferred_element_type=f32)
        for k in range(groups):
            abuf[0, c, k] = sorted_rope[:, k * rows:(k + 1) * rows].astype(bf16)

    def stats_of(m, d):
        lane = lax.broadcasted_iota(jnp.int32, (half, 128), 1)
        return jnp.where(
            lane < 2, jnp.where(lane == 0, m[:half], d[:half]), jnp.where(lane == 2, m[half:], d[half:])
        ).T[0:8]

    def columns_of(stat, j):
        return stat[:, 2 * j:2 * j + 1], stat[:, 2 * j + 1:2 * j + 2]

    def dequantize_keys(c):
        for slot in range(2):
            scales = scale_rows[slot, c].T
            for k in range(groups):
                for b in range(blocks):
                    lanes = slice(b * (width // blocks), (b + 1) * (width // blocks))
                    keys[slot * span + k * rows:slot * span + (k + 1) * rows, lanes] = (
                        kbuf[slot, c, k, :, lanes].astype(f32)
                        * scales[k * rows:(k + 1) * rows, b:b + 1]
                    ).astype(bf16)

    def partial(c, first):
        q = qbuf[c, first:first + 2, 0:half, :].reshape(2 * half, width)
        qr = jnp.concatenate(
            [
                qbuf[c, first + j, half:half + fold, i * rope:(i + 1) * rope]
                for j in range(2) for i in range(half // fold)
            ],
            axis=0,
        )
        ropes = jnp.concatenate(
            [abuf[slot, c, k] for slot in range(2) for k in range(groups)], axis=1
        )
        s = lax.dot_general(q, keys[...], dims, preferred_element_type=f32)
        s = (s + jnp.dot(qr, ropes, preferred_element_type=f32)) * softmax_gain
        column = lax.broadcasted_iota(jnp.int32, (1, 2 * span), 1)
        local = column % span
        position = jnp.where(column < span, hub, edge) * span + local % rows * groups + local // rows
        s = jnp.where(position < lengths[c % lengths.shape[0]], s, masked_score)
        m = jnp.max(s, axis=1, keepdims=True)
        if first == 0:
            t = lax.dot_general(q, nkbuf[c], dims, preferred_element_type=f32)
            t = (t + lax.dot_general(qr, nrbuf[c], dims, preferred_element_type=f32)) * softmax_gain
            token = lax.broadcasted_iota(jnp.int32, t.shape, 0) % half // heads
            t = jnp.where(lax.broadcasted_iota(jnp.int32, t.shape, 1) <= token, t, masked_score)
            m = jnp.maximum(m, jnp.max(t, axis=1, keepdims=True))
        w = jnp.exp(s - m).astype(bf16)
        d = jnp.sum(w.astype(f32), axis=1, keepdims=True)
        n = jnp.dot(w, keys[...], preferred_element_type=f32)
        if first == 0:
            v = jnp.exp(t - m).astype(bf16)
            d = d + jnp.sum(v.astype(f32), axis=1, keepdims=True)
            n = n + jnp.dot(v, nkbuf[c], preferred_element_type=f32)
        return n, stats_of(m, d)

    def merge(c):
        wait_bytes(meter.at[c], far_recv.at[c])
        side, far = side_stat[c].T, far_in_stat[c].T
        for j in (1, 0):
            m0, d0 = columns_of(side, j)
            m1, d1 = columns_of(far, j)
            m = jnp.maximum(m0, m1)
            f0, f1 = jnp.exp(m0 - m), jnp.exp(m1 - m)
            numerator = f0 * side_sum[c, j] + f1 * far_in[c, j].astype(f32)
            merged = (numerator / (f0 * d0 + f1 * d1)).astype(bf16)
            if j == 1:
                result[c] = merged
                edge_result(c).start()
            else:
                att_ref[c] = merged

    @pl.when(is_edge)
    def _():
        shard_scales.start()

        @pl.loop(0, pairs)
        def _(c):
            prepare(c)

            @pl.when(c >= 1)
            def _():
                wait_bytes(raw.at[0], k_send.at[c - 1])
                start((query_latent(c, 0, 1, hub), query_rotary(c, 0, 1, hub)))

            start(shard(c))
            keep(0, c, me)

        wait_bytes(raw.at[0], k_send.at[pairs - 1])
        shard_scales.wait_send()
        wait_bytes(qbuf.at[:, 0], q_send.at[0])
        for place in (hub, across, far_edge):
            await_scales(place)
        for place in (hub, across, far_edge):
            wait_bytes(qbuf.at[:, 0], f_recv.at[place])
        wait_bytes(att_ref, r_recv.at[0])

    @pl.when(is_hub)
    def _():
        handover_scales(0, edge, 0).start()

        @pl.loop(0, pairs)
        def _(c):
            prepare(c)
            start(handover(0, c, edge, 0))
            keep(0, c, me)

        for target in (across, far_edge):
            handover_scales(0, target, 1).start()
        wait_bytes(qbuf.at[0, 1], q_recv.at[0, 0])
        forward_query(0).start()
        start(handover_far(0, 0))
        for copy in load_new:
            copy.wait()
        nkbuf[...] = jnp.zeros(nkbuf.shape, bf16)
        nrbuf[...] = jnp.zeros(nrbuf.shape, bf16)
        for c in range(pairs):
            nkbuf[c, 0:fresh, :] = new_rows[c]
            nrbuf[c, 0:fresh, :] = newr_rows[c]
        load_query.wait()
        spread_scales(0)
        shard_scales.wait_recv()
        for target in (across, far_edge):
            handover_scales(1, target, 1).start()
        keep_scales(sbuf[1, me], edge)
        spread_scales(1)

        @pl.loop(0, pairs)
        def _(c):
            wait_bytes(raw.at[0], k_recv.at[c])
            start(handover_far(1, c))
            keep(1, c, edge)

            @pl.when(c < pairs - 1)
            def _():
                wait_bytes(qbuf.at[0, 1], q_recv.at[0, c + 1])
                forward_query(c + 1).start()

            wait_bytes(qbuf.at[0, pl.ds(2, 2)], q_recv.at[1, c])
            dequantize_keys(c)
            far_sum, far_out_stat[c] = partial(c, 2)
            for j in range(2):
                far_out[c, j] = far_sum[j * half:(j + 1) * half].astype(bf16)
            start(sums(c))

            @pl.when(c == 1)
            def _():
                start(handover_far(0, c))

            near_sum, side_stat[c] = partial(c, 0)
            for j in range(2):
                side_sum[c, j] = near_sum[j * half:(j + 1) * half]

            @pl.when(c >= 1)
            def _():
                merge(c - 1)

        for c in range(2, pairs):
            start(handover_far(0, c))
        for place in (across, far_edge):
            await_scales(place)
        merge(pairs - 1)
        wait_bytes(sbuf.at[0, 0], s_send.at[0])
        wait_bytes(sbuf.at[0], s_send.at[1])
        for flow in (1, 2):
            wait_bytes(qbuf.at[:, 0], q_send.at[flow])
        wait_bytes(meter, far_send.at[0])
        wait_bytes(result, r_send.at[0])
        wait_bytes(qbuf.at[:, 0], f_send.at[0])
        for slot in range(2):
            wait_bytes(qbuf.at[:, pl.ds(0, 2)], f_send.at[1 + slot])
        for place in (across, far_edge):
            wait_bytes(qbuf.at[:, 0], f_recv.at[place])


def _emit_kernel(att_ref, cache_ref, crope_ref, cscale_ref, att_out, cache_out, crope_out, cscale_out, sem):
    copies = []
    for c in range(cache_ref.shape[0]):
        copies.append(pltpu.make_async_copy(cache_ref.at[c], cache_out.at[c], sem.at[len(copies)]))
    for src, dst in ((att_ref, att_out), (crope_ref, crope_out), (cscale_ref, cscale_out)):
        copies.append(pltpu.make_async_copy(src, dst, sem.at[len(copies)]))
    for copy in copies:
        copy.start()
    for copy in copies:
        copy.wait()


def emit(values):
    return pl.pallas_call(
        _emit_kernel,
        out_shape=[jax.ShapeDtypeStruct(v.shape, v.dtype) for v in values],
        in_specs=[pl.BlockSpec(memory_space=pl.ANY)] * 4,
        out_specs=[pl.BlockSpec(memory_space=pl.ANY)] * 4,
        scratch_shapes=[pltpu.SemaphoreType.DMA((values[1].shape[0] + 3,))],
        compiler_params=pltpu.CompilerParams(vmem_limit_bytes=1 << 20),
    )(*values)


def per_device_line(
    latent_codes, latent_scales, rope_keys, lengths, query_latent, query_rope, new_latent, new_rope
):
    layers, requests, span, width = latent_codes.shape
    pairs, rows = layers * requests, span // 4
    rope, blocks = rope_keys.shape[-1], latent_scales.shape[-1]
    tokens, heads = query_latent.shape[2:4]
    half = tokens * heads
    tile_rows = -(-pairs * blocks // 16) * 16
    hbm_spec = pl.BlockSpec(memory_space=pltpu.HBM)
    vmem_spec = pl.BlockSpec(memory_space=pltpu.VMEM)
    dma = pltpu.SemaphoreType.DMA
    bf16, f32 = jnp.bfloat16, jnp.float32
    att, cache, crope, cscale = pl.pallas_call(
        _hub_kernel,
        out_shape=(
            pltpu.VMEM((pairs, half, width), bf16),
            pltpu.VMEM((pairs, span, width), bf16),
            pltpu.VMEM((pairs, rope, span), bf16),
            pltpu.VMEM((pairs, blocks, span), bf16),
        ),
        in_specs=[hbm_spec] * 8,
        out_specs=(vmem_spec,) * 4,
        scratch_shapes=[
            pltpu.SMEM(lengths.shape, lengths.dtype),
            pltpu.VMEM((span, span), bf16),
            pltpu.VMEM((2, pairs, 4, rows, width), bf16),
            pltpu.VMEM((2, pairs, 4, rope, rows), bf16),
            pltpu.VMEM((2, 4, tile_rows, rows), bf16),
            pltpu.VMEM((4, tile_rows, rows), bf16),
            pltpu.VMEM((2, pairs, 8, span), f32),
            pltpu.VMEM((pairs, span + rope, width), bf16),
            pltpu.VMEM((pairs, blocks, span), bf16),
            pltpu.VMEM((pairs, half, rope), bf16),
            pltpu.VMEM((pairs, 4, half + half * rope // width, width), bf16),
            pltpu.VMEM((pairs, 128, width), bf16),
            pltpu.VMEM((pairs, 128, rope), bf16),
            pltpu.VMEM((pairs, tokens, width), bf16),
            pltpu.VMEM((pairs, tokens, rope), bf16),
            pltpu.VMEM((2 * span, width), bf16),
            pltpu.VMEM((pairs, half, width), bf16),
            pltpu.VMEM((pairs, 2, half, width), f32),
            pltpu.VMEM((pairs, 8, 128), f32),
            pltpu.VMEM((pairs, 2, half, width), bf16),
            pltpu.VMEM((pairs, 8, 128), f32),
            pltpu.VMEM((pairs, 2, half, width), bf16),
            pltpu.VMEM((pairs, 8, 128), f32),
            pltpu.VMEM((pairs, half * width // 128 + 8, 128), f32),
            dma((pairs,)), dma((6,)), dma((3,)), dma((2, pairs)), dma((pairs,)), dma((pairs,)),
            dma((3,)), dma((4,)), dma((2,)), dma((5,)), dma((1,)), dma((pairs,)), dma((1,)), dma((1,)),
        ],
        compiler_params=pltpu.CompilerParams(
            collective_id=0, has_side_effects=True, vmem_limit_bytes=56 << 20
        ),
    )(
        lengths, latent_codes.reshape(pairs, span, width),
        rope_keys.transpose(0, 1, 3, 2).reshape(pairs, rope, span),
        latent_scales.transpose(0, 1, 3, 2).reshape(pairs, blocks, span),
        query_latent.reshape(pairs, half, width), query_rope.reshape(pairs, half, rope),
        new_latent.reshape(pairs, tokens, width), new_rope.reshape(pairs, tokens, rope),
    )

    att, cache, crope, cscale = emit((att, cache, crope, cscale))

    def as_cache(values):
        flipped = values.reshape(layers, requests, values.shape[1], span).transpose(0, 1, 3, 2)
        return flipped.reshape(layers, requests, span, 1, values.shape[1])

    return (
        att.reshape(query_latent.shape),
        cache.reshape(layers, requests, span, 1, width),
        as_cache(cscale),
        as_cache(crope),
    )


def solution(mesh):
    placed = (
        P(None, ("group", "req", "sub"), "seq", None),
        P(None, ("group", "req", "sub"), "seq", None),
        P(None, ("group", "req", "sub"), "seq", None),
        P(("group", "req", "sub")),
        P(None, ("group", "req", "sub"), None, "seq", None),
        P(None, ("group", "req", "sub"), None, "seq", None),
        P(None, ("group", "req", "sub"), None, None),
        P(None, ("group", "req", "sub"), None, None),
    )
    return jax.shard_map(
        per_device_line if mesh.shape["seq"] == 4 else per_device,
        mesh=mesh,
        in_specs=placed,
        out_specs=(
            P(None, ("group", "req", "sub"), None, "seq", None),
            P(None, ("group", "req", "sub"), None, "seq", None),
            P(None, ("group", "req", "sub"), None, "seq", None),
            P(None, ("group", "req", "sub"), None, "seq", None),
        ),
        check_vma=False,
    )
```

```python
import jax
import jax.numpy as jnp
from jax import lax
from jax.experimental import pallas as pl
from jax.experimental.pallas import tpu as pltpu
from jax.sharding import PartitionSpec as P

softmax_gain = 192.0 ** (-0.5)
masked_score = -1e30


def dequantize(code_values, scale_values):
    blocks = scale_values.shape[-1]
    latent_width = code_values.shape[-1]
    shaped = code_values.astype(jnp.float32).reshape(
        code_values.shape[:-1] + (blocks, latent_width // blocks)
    )
    scaled = shaped * scale_values.astype(jnp.float32)[..., None]
    return scaled.reshape(code_values.shape).astype(jnp.bfloat16)


def shard_partial(
    lat_query, rope_query, key_rows, rope_rows, usable, new_keys, new_rope_rows, holds_new
):
    tokens_new, head_count, latent_width = lat_query.shape
    query_rows = lat_query.reshape(tokens_new * head_count, latent_width)
    query_pos = rope_query.reshape(tokens_new * head_count, rope_query.shape[-1])
    scores = jnp.dot(query_rows, key_rows.T, preferred_element_type=jnp.float32)
    scores = (
        scores + jnp.dot(query_pos, rope_rows.T, preferred_element_type=jnp.float32)
    ) * softmax_gain
    fresh_scores = jnp.dot(query_rows, new_keys.T, preferred_element_type=jnp.float32)
    fresh_scores = (
        fresh_scores + jnp.dot(query_pos, new_rope_rows.T, preferred_element_type=jnp.float32)
    ) * softmax_gain
    token_of_row = jnp.arange(tokens_new * head_count, dtype=jnp.int32) // head_count
    causal = (jnp.arange(tokens_new, dtype=jnp.int32)[None, :] <= token_of_row[:, None]) & holds_new
    scores = jnp.where(usable[None, :], scores, masked_score)
    fresh_scores = jnp.where(causal, fresh_scores, masked_score)
    group_peak = jnp.maximum(jnp.max(scores, 1), jnp.max(fresh_scores, 1)).astype(jnp.bfloat16)
    peak_float = group_peak.astype(jnp.float32)[:, None]
    weights = jnp.where(usable[None, :], jnp.exp(scores - peak_float), 0.0).astype(jnp.bfloat16)
    fresh_weights = jnp.where(causal, jnp.exp(fresh_scores - peak_float), 0.0).astype(jnp.bfloat16)
    group_total = jnp.sum(weights.astype(jnp.float32), 1) + jnp.sum(
        fresh_weights.astype(jnp.float32), 1
    )
    group_sum = jnp.dot(weights, key_rows, preferred_element_type=jnp.float32)
    group_sum = group_sum + jnp.dot(fresh_weights, new_keys, preferred_element_type=jnp.float32)
    return (
        group_sum.astype(jnp.bfloat16).reshape(tokens_new, head_count, latent_width),
        group_peak.reshape(tokens_new, head_count),
        group_total.astype(jnp.bfloat16).reshape(tokens_new, head_count),
    )


def merge_groups(pieces):
    group_sum, group_peak, group_total = pieces
    peak_float = group_peak.astype(jnp.float32)
    overall = jnp.max(peak_float, 0)
    factor = jnp.exp(peak_float - overall)
    numerator = jnp.sum(factor[..., None] * group_sum.astype(jnp.float32), 0)
    denominator = jnp.sum(factor * group_total.astype(jnp.float32), 0)
    return (numerator / denominator[..., None]).astype(jnp.bfloat16)


def per_device(
    latent_codes, latent_scales, rope_keys, lengths, query_latent, query_rope, new_latent, new_rope
):
    shard_count = lax.axis_size("seq")
    seq_index = lax.axis_index("seq")
    layer_count, request_count, span, latent_width = latent_codes.shape
    lat_query, rope_query = (
        lax.all_gather(query_latent, "seq", axis=3, tiled=True),
        lax.all_gather(query_rope, "seq", axis=3, tiled=True),
    )

    def regroup_rows(values):
        return values.reshape(
            values.shape[0], values.shape[1], span // shard_count, shard_count, values.shape[-1]
        )

    codes_moved, scales_moved, rope_moved = (
        lax.all_to_all(regroup_rows(latent_codes), "seq", split_axis=3, concat_axis=2, tiled=True),
        lax.all_to_all(regroup_rows(latent_scales), "seq", split_axis=3, concat_axis=2, tiled=True),
        lax.all_to_all(regroup_rows(rope_keys), "seq", split_axis=3, concat_axis=2, tiled=True),
    )
    offsets = jnp.arange(span, dtype=jnp.int32)
    key_rows = dequantize(latent_codes, latent_scales)
    positions = seq_index * span + offsets
    usable = positions[None, :] < lengths[:, None]
    holds_new = seq_index == 0
    per_request = jax.vmap(shard_partial, in_axes=(0, 0, 0, 0, 0, 0, 0, None))
    per_layer = jax.vmap(per_request, in_axes=(0, 0, 0, 0, None, 0, 0, None))
    group_sum, group_peak, group_total = per_layer(
        lat_query, rope_query, key_rows, rope_keys, usable, new_latent, new_rope, holds_new
    )
    attended = merge_groups(
        (
            lax.all_to_all(group_sum[None], "seq", split_axis=4, concat_axis=0, tiled=True),
            lax.all_to_all(group_peak[None], "seq", split_axis=4, concat_axis=0, tiled=True),
            lax.all_to_all(group_total[None], "seq", split_axis=4, concat_axis=0, tiled=True),
        )
    )
    return (attended, codes_moved, scales_moved, rope_moved)


def _hub_kernel(
    len_ref, codes_ref, rope_ref, scale_ref, q_ref, qr_ref, new_ref, newr_ref,
    att_ref, cache_ref, crope_ref, cscale_ref,
    lengths, perm, kbuf, abuf, sbuf, scale_in, scale_rows, raw, raws, rawq, qbuf, nkbuf, nrbuf,
    new_rows, newr_rows, keys, result, side_sum, side_stat, far_out, far_out_stat, far_in, far_in_stat,
    meter, load_sem, misc_sem, q_send, q_recv, k_send, k_recv, f_send, f_recv, s_send, s_recv,
    far_send, far_recv, r_send, r_recv, edge_in, far_edge_in,
):
    pairs, span, width = codes_ref.shape
    groups = 4
    rows = span // groups
    half = q_ref.shape[1]
    rope = qr_ref.shape[2]
    blocks = scale_ref.shape[1]
    fresh = new_ref.shape[1]
    heads = half // fresh
    fold = half * rope // width
    me = lax.axis_index("seq")
    is_hub = (me == 1) | (me == 2)
    is_edge = jnp.logical_not(is_hub)
    hub = 1 + me // 2
    edge = me // 2 * 3
    across = 3 - hub
    far_edge = 3 - edge
    f32, bf16 = jnp.float32, jnp.bfloat16

    def start(copies):
        for copy in copies:
            copy.start()

    def remote(src, dst, send, recv, target):
        return pltpu.make_async_remote_copy(
            src_ref=src, dst_ref=dst, send_sem=send, recv_sem=recv,
            device_id={"seq": target}, device_id_type=pl.DeviceIdType.MESH,
        )

    def greet(target):
        pl.semaphore_signal(
            pltpu.get_barrier_semaphore(), inc=1, device_id={"seq": target},
            device_id_type=pl.DeviceIdType.MESH,
        )

    def tell(sem, target):
        pl.semaphore_signal(sem, inc=1, device_id={"seq": target}, device_id_type=pl.DeviceIdType.MESH)

    def wait_bytes(ref, sem):
        pltpu.make_async_copy(ref, ref, sem).wait()

    def load(c):
        return (
            pltpu.make_async_copy(codes_ref.at[c], raw.at[c, pl.ds(0, span)], load_sem.at[c]),
            pltpu.make_async_copy(rope_ref.at[c], raw.at[c, pl.ds(span, rope)], load_sem.at[c]),
        )

    load_scales = pltpu.make_async_copy(scale_ref, raws, misc_sem.at[0])
    load_rotary = pltpu.make_async_copy(qr_ref, rawq, misc_sem.at[1])
    load_query = pltpu.make_async_copy(q_ref, qbuf.at[:, 0, pl.ds(0, half)], misc_sem.at[2])
    load_new = (
        pltpu.make_async_copy(new_ref, new_rows, misc_sem.at[3]),
        pltpu.make_async_copy(newr_ref, newr_rows, misc_sem.at[4]),
    )
    load_lengths = pltpu.make_async_copy(len_ref, lengths, misc_sem.at[5])

    def query_latent(c, flow, dst, target):
        return remote(q_ref.at[c], qbuf.at[c, dst, pl.ds(0, half)],
                      q_send.at[flow], q_recv.at[flow, c], target)

    def query_rotary(c, flow, dst, target):
        return remote(qbuf.at[c, 0, pl.ds(half, fold)], qbuf.at[c, dst, pl.ds(half, fold)],
                      q_send.at[flow], q_recv.at[flow, c], target)

    def forward_query(c):
        return remote(qbuf.at[c, 1], qbuf.at[c, 3], q_send.at[2], q_recv.at[1, c], across)

    def shard(c):
        return (
            remote(abuf.at[0, c], abuf.at[1, c], k_send.at[c], k_recv.at[c], hub),
            remote(kbuf.at[0, c], kbuf.at[1, c], k_send.at[c], k_recv.at[c], hub),
        )

    shard_scales = remote(sbuf.at[0], sbuf.at[1], s_send.at[0], s_recv.at[groups], hub)

    def place_of(slot):
        return hub if slot == 0 else edge

    def handover(slot, c, target, send):
        place = place_of(slot)
        spot = pl.multiple_of(place * rows, rows)
        return (
            remote(kbuf.at[slot, c, target], cache_ref.at[c, pl.ds(spot, rows)],
                   f_send.at[send], f_recv.at[place], target),
            remote(abuf.at[slot, c, target], crope_ref.at[c, :, pl.ds(spot, rows)],
                   f_send.at[send], f_recv.at[place], target),
        )

    def handover_far(slot, c):
        return handover(slot, c, far_edge, 1 + slot) + handover(slot, c, across, 1 + slot)

    def handover_scales(slot, target, send):
        return remote(sbuf.at[slot, target], scale_in.at[place_of(slot)],
                      s_send.at[send], s_recv.at[place_of(slot)], target)

    def keep_scales(tile, place):
        values = tile.astype(f32)
        for c in range(pairs):
            cscale_ref[c, :, pl.ds(pl.multiple_of(place * rows, rows), rows)] = (
                values[c * blocks:(c + 1) * blocks].astype(bf16)
            )

    def await_scales(place):
        wait_bytes(scale_in.at[place], s_recv.at[place])
        keep_scales(scale_in[place], place)

    def keep(slot, c, place):
        spot = pl.multiple_of(place * rows, rows)
        cache_ref[c, pl.ds(spot, rows), :] = kbuf[slot, c, me]
        crope_ref[c, :, pl.ds(spot, rows)] = abuf[slot, c, me]

    def sums(c):
        return (
            remote(far_out.at[c], far_in.at[c], far_send.at[0], far_recv.at[c], across),
            remote(far_out_stat.at[c], far_in_stat.at[c], far_send.at[0], far_recv.at[c], across),
        )

    def edge_result(c):
        return remote(result.at[c], att_ref.at[c], r_send.at[0], r_recv.at[0], edge)

    @pl.when(is_hub)
    def _():
        greet(across)
        greet(edge)

    start((load_rotary, load_scales))
    for c in range(pairs):
        start(load(c))
    load_lengths.start()

    @pl.when(is_hub)
    def _():
        pl.semaphore_wait(pltpu.get_barrier_semaphore(), 1)
        for c in range(pairs):
            query_latent(c, 1, 2, across).start()
        load_query.start()
        start(load_new)

    @pl.when(is_edge)
    def _():
        pl.semaphore_wait(pltpu.get_barrier_semaphore(), 1)
        tell(edge_in, hub)
        query_latent(0, 0, 1, hub).start()

    load_rotary.wait()
    for c in range(pairs):
        qbuf[c, 0, half:half + fold, :] = jnp.concatenate(
            [rawq[c, i * fold:(i + 1) * fold, :] for i in range(half // fold)], axis=1
        )

    @pl.when(is_hub)
    def _():
        for c in range(pairs):
            query_rotary(c, 1, 2, across).start()

    @pl.when(is_edge)
    def _():
        query_rotary(0, 0, 1, hub).start()

    line = lax.broadcasted_iota(jnp.int32, (span, span), 0)
    column = lax.broadcasted_iota(jnp.int32, (span, span), 1)
    perm[...] = jnp.where(column == (line % rows) * groups + line // rows, 1.0, 0.0).astype(bf16)
    dims = (((1,), (1,)), ((), ()))

    tile_rows = sbuf.shape[2]
    load_scales.wait()
    load_lengths.wait()
    stacked = [raws[c].astype(f32) for c in range(pairs)]
    if tile_rows > pairs * blocks:
        stacked.append(jnp.zeros((tile_rows - pairs * blocks, span), f32))
    stacked = jnp.concatenate(stacked, axis=0).astype(bf16)
    sorted_scales = lax.dot_general(stacked, perm[...], dims, preferred_element_type=f32)
    for k in range(groups):
        sbuf[0, k] = sorted_scales[:, k * rows:(k + 1) * rows].astype(bf16)
    keep_scales(sbuf[0, me], me)

    def spread_scales(slot):
        scale_rows[slot] = jnp.zeros(scale_rows.shape[1:], f32)
        for k in range(groups):
            values = sbuf[slot, k].astype(f32)
            for c in range(pairs):
                scale_rows[slot, c, 0:blocks, k * rows:(k + 1) * rows] = (
                    values[c * blocks:(c + 1) * blocks]
                )

    def prepare(c):
        wait_bytes(raw.at[c], load_sem.at[c])
        sorted_codes = jnp.dot(perm[...], raw[c, 0:span], preferred_element_type=f32)
        for k in range(groups):
            kbuf[0, c, k] = sorted_codes[k * rows:(k + 1) * rows].astype(bf16)
        sorted_rope = lax.dot_general(raw[c, span:span + rope], perm[...], dims, preferred_element_type=f32)
        for k in range(groups):
            abuf[0, c, k] = sorted_rope[:, k * rows:(k + 1) * rows].astype(bf16)

    def stats_of(m, d):
        lane = lax.broadcasted_iota(jnp.int32, (half, 128), 1)
        return jnp.where(
            lane < 2, jnp.where(lane == 0, m[:half], d[:half]), jnp.where(lane == 2, m[half:], d[half:])
        ).T[0:8]

    def columns_of(stat, j):
        return stat[:, 2 * j:2 * j + 1], stat[:, 2 * j + 1:2 * j + 2]

    def dequantize_keys(c):
        for slot in range(2):
            scales = scale_rows[slot, c].T
            for k in range(groups):
                for b in range(blocks):
                    lanes = slice(b * (width // blocks), (b + 1) * (width // blocks))
                    keys[slot * span + k * rows:slot * span + (k + 1) * rows, lanes] = (
                        kbuf[slot, c, k, :, lanes].astype(f32)
                        * scales[k * rows:(k + 1) * rows, b:b + 1]
                    ).astype(bf16)

    def partial(c, first):
        q = qbuf[c, first:first + 2, 0:half, :].reshape(2 * half, width)
        qr = jnp.concatenate(
            [
                qbuf[c, first + j, half:half + fold, i * rope:(i + 1) * rope]
                for j in range(2) for i in range(half // fold)
            ],
            axis=0,
        )
        ropes = jnp.concatenate(
            [abuf[slot, c, k] for slot in range(2) for k in range(groups)], axis=1
        )
        s = lax.dot_general(q, keys[...], dims, preferred_element_type=f32)
        s = (s + jnp.dot(qr, ropes, preferred_element_type=f32)) * softmax_gain
        column = lax.broadcasted_iota(jnp.int32, (1, 2 * span), 1)
        local = column % span
        position = jnp.where(column < span, hub, edge) * span + local % rows * groups + local // rows
        s = jnp.where(position < lengths[c % lengths.shape[0]], s, masked_score)
        m = jnp.max(s, axis=1, keepdims=True)
        if first == 0:
            t = lax.dot_general(q, nkbuf[c], dims, preferred_element_type=f32)
            t = (t + lax.dot_general(qr, nrbuf[c], dims, preferred_element_type=f32)) * softmax_gain
            token = lax.broadcasted_iota(jnp.int32, t.shape, 0) % half // heads
            t = jnp.where(lax.broadcasted_iota(jnp.int32, t.shape, 1) <= token, t, masked_score)
            m = jnp.maximum(m, jnp.max(t, axis=1, keepdims=True))
        w = jnp.exp(s - m).astype(bf16)
        d = jnp.sum(w.astype(f32), axis=1, keepdims=True)
        n = jnp.dot(w, keys[...], preferred_element_type=f32)
        if first == 0:
            v = jnp.exp(t - m).astype(bf16)
            d = d + jnp.sum(v.astype(f32), axis=1, keepdims=True)
            n = n + jnp.dot(v, nkbuf[c], preferred_element_type=f32)
        return n, stats_of(m, d)

    def merge(c):
        wait_bytes(meter.at[c], far_recv.at[c])
        side, far = side_stat[c].T, far_in_stat[c].T
        for j in (1, 0):
            m0, d0 = columns_of(side, j)
            m1, d1 = columns_of(far, j)
            m = jnp.maximum(m0, m1)
            f0, f1 = jnp.exp(m0 - m), jnp.exp(m1 - m)
            numerator = f0 * side_sum[c, j] + f1 * far_in[c, j].astype(f32)
            merged = (numerator / (f0 * d0 + f1 * d1)).astype(bf16)
            if j == 1:
                result[c] = merged
                edge_result(c).start()
            else:
                att_ref[c] = merged

    @pl.when(is_edge)
    def _():
        shard_scales.start()

        @pl.loop(0, pairs)
        def _(c):
            prepare(c)

            @pl.when(c >= 1)
            def _():
                wait_bytes(raw.at[0], k_send.at[c - 1])
                start((query_latent(c, 0, 1, hub), query_rotary(c, 0, 1, hub)))

            start(shard(c))
            keep(0, c, me)

        wait_bytes(raw.at[0], k_send.at[pairs - 1])
        shard_scales.wait_send()
        wait_bytes(qbuf.at[:, 0], q_send.at[0])
        for place in (hub, across, far_edge):
            await_scales(place)
        for place in (hub, across, far_edge):
            wait_bytes(qbuf.at[:, 0], f_recv.at[place])
        wait_bytes(att_ref, r_recv.at[0])

    @pl.when(is_hub)
    def _():
        pl.semaphore_wait(edge_in, 1)
        tell(far_edge_in, across)
        handover_scales(0, edge, 0).start()

        @pl.loop(0, pairs)
        def _(c):
            prepare(c)
            start(handover(0, c, edge, 0))
            keep(0, c, me)

        pl.semaphore_wait(far_edge_in, 1)
        for target in (across, far_edge):
            handover_scales(0, target, 1).start()
        wait_bytes(qbuf.at[0, 1], q_recv.at[0, 0])
        forward_query(0).start()
        start(handover_far(0, 0))
        for copy in load_new:
            copy.wait()
        nkbuf[...] = jnp.zeros(nkbuf.shape, bf16)
        nrbuf[...] = jnp.zeros(nrbuf.shape, bf16)
        for c in range(pairs):
            nkbuf[c, 0:fresh, :] = new_rows[c]
            nrbuf[c, 0:fresh, :] = newr_rows[c]
        load_query.wait()
        spread_scales(0)
        shard_scales.wait_recv()
        for target in (across, far_edge):
            handover_scales(1, target, 1).start()
        keep_scales(sbuf[1, me], edge)
        spread_scales(1)

        @pl.loop(0, pairs)
        def _(c):
            wait_bytes(raw.at[0], k_recv.at[c])
            start(handover_far(1, c))
            keep(1, c, edge)

            @pl.when(c < pairs - 1)
            def _():
                wait_bytes(qbuf.at[0, 1], q_recv.at[0, c + 1])
                forward_query(c + 1).start()

            wait_bytes(qbuf.at[0, pl.ds(2, 2)], q_recv.at[1, c])
            dequantize_keys(c)
            far_sum, far_out_stat[c] = partial(c, 2)
            for j in range(2):
                far_out[c, j] = far_sum[j * half:(j + 1) * half].astype(bf16)
            start(sums(c))

            @pl.when(c == 1)
            def _():
                start(handover_far(0, c))

            near_sum, side_stat[c] = partial(c, 0)
            for j in range(2):
                side_sum[c, j] = near_sum[j * half:(j + 1) * half]

            @pl.when(c >= 1)
            def _():
                merge(c - 1)

        for c in range(2, pairs):
            start(handover_far(0, c))
        for place in (across, far_edge):
            await_scales(place)
        merge(pairs - 1)
        wait_bytes(sbuf.at[0, 0], s_send.at[0])
        wait_bytes(sbuf.at[0], s_send.at[1])
        for flow in (1, 2):
            wait_bytes(qbuf.at[:, 0], q_send.at[flow])
        wait_bytes(meter, far_send.at[0])
        wait_bytes(result, r_send.at[0])
        wait_bytes(qbuf.at[:, 0], f_send.at[0])
        for slot in range(2):
            wait_bytes(qbuf.at[:, pl.ds(0, 2)], f_send.at[1 + slot])
        for place in (across, far_edge):
            wait_bytes(qbuf.at[:, 0], f_recv.at[place])


def _emit_kernel(att_ref, cache_ref, crope_ref, cscale_ref, att_out, cache_out, crope_out, cscale_out, sem):
    copies = []
    for c in range(cache_ref.shape[0]):
        copies.append(pltpu.make_async_copy(cache_ref.at[c], cache_out.at[c], sem.at[len(copies)]))
    for src, dst in ((att_ref, att_out), (crope_ref, crope_out), (cscale_ref, cscale_out)):
        copies.append(pltpu.make_async_copy(src, dst, sem.at[len(copies)]))
    for copy in copies:
        copy.start()
    for copy in copies:
        copy.wait()


def emit(values):
    return pl.pallas_call(
        _emit_kernel,
        out_shape=[jax.ShapeDtypeStruct(v.shape, v.dtype) for v in values],
        in_specs=[pl.BlockSpec(memory_space=pl.ANY)] * 4,
        out_specs=[pl.BlockSpec(memory_space=pl.ANY)] * 4,
        scratch_shapes=[pltpu.SemaphoreType.DMA((values[1].shape[0] + 3,))],
        compiler_params=pltpu.CompilerParams(vmem_limit_bytes=1 << 20),
    )(*values)


def per_device_line(
    latent_codes, latent_scales, rope_keys, lengths, query_latent, query_rope, new_latent, new_rope
):
    layers, requests, span, width = latent_codes.shape
    pairs, rows = layers * requests, span // 4
    rope, blocks = rope_keys.shape[-1], latent_scales.shape[-1]
    tokens, heads = query_latent.shape[2:4]
    half = tokens * heads
    tile_rows = -(-pairs * blocks // 16) * 16
    hbm_spec = pl.BlockSpec(memory_space=pltpu.HBM)
    vmem_spec = pl.BlockSpec(memory_space=pltpu.VMEM)
    dma = pltpu.SemaphoreType.DMA
    bf16, f32 = jnp.bfloat16, jnp.float32
    att, cache, crope, cscale = pl.pallas_call(
        _hub_kernel,
        out_shape=(
            pltpu.VMEM((pairs, half, width), bf16),
            pltpu.VMEM((pairs, span, width), bf16),
            pltpu.VMEM((pairs, rope, span), bf16),
            pltpu.VMEM((pairs, blocks, span), bf16),
        ),
        in_specs=[hbm_spec] * 8,
        out_specs=(vmem_spec,) * 4,
        scratch_shapes=[
            pltpu.SMEM(lengths.shape, lengths.dtype),
            pltpu.VMEM((span, span), bf16),
            pltpu.VMEM((2, pairs, 4, rows, width), bf16),
            pltpu.VMEM((2, pairs, 4, rope, rows), bf16),
            pltpu.VMEM((2, 4, tile_rows, rows), bf16),
            pltpu.VMEM((4, tile_rows, rows), bf16),
            pltpu.VMEM((2, pairs, 8, span), f32),
            pltpu.VMEM((pairs, span + rope, width), bf16),
            pltpu.VMEM((pairs, blocks, span), bf16),
            pltpu.VMEM((pairs, half, rope), bf16),
            pltpu.VMEM((pairs, 4, half + half * rope // width, width), bf16),
            pltpu.VMEM((pairs, 128, width), bf16),
            pltpu.VMEM((pairs, 128, rope), bf16),
            pltpu.VMEM((pairs, tokens, width), bf16),
            pltpu.VMEM((pairs, tokens, rope), bf16),
            pltpu.VMEM((2 * span, width), bf16),
            pltpu.VMEM((pairs, half, width), bf16),
            pltpu.VMEM((pairs, 2, half, width), f32),
            pltpu.VMEM((pairs, 8, 128), f32),
            pltpu.VMEM((pairs, 2, half, width), bf16),
            pltpu.VMEM((pairs, 8, 128), f32),
            pltpu.VMEM((pairs, 2, half, width), bf16),
            pltpu.VMEM((pairs, 8, 128), f32),
            pltpu.VMEM((pairs, half * width // 128 + 8, 128), f32),
            dma((pairs,)), dma((6,)), dma((3,)), dma((2, pairs)), dma((pairs,)), dma((pairs,)),
            dma((3,)), dma((4,)), dma((2,)), dma((5,)), dma((1,)), dma((pairs,)), dma((1,)), dma((1,)),
            pltpu.SemaphoreType.REGULAR, pltpu.SemaphoreType.REGULAR,
        ],
        compiler_params=pltpu.CompilerParams(
            collective_id=0, has_side_effects=True, vmem_limit_bytes=56 << 20
        ),
    )(
        lengths, latent_codes.reshape(pairs, span, width),
        rope_keys.transpose(0, 1, 3, 2).reshape(pairs, rope, span),
        latent_scales.transpose(0, 1, 3, 2).reshape(pairs, blocks, span),
        query_latent.reshape(pairs, half, width), query_rope.reshape(pairs, half, rope),
        new_latent.reshape(pairs, tokens, width), new_rope.reshape(pairs, tokens, rope),
    )

    att, cache, crope, cscale = emit((att, cache, crope, cscale))

    def as_cache(values):
        flipped = values.reshape(layers, requests, values.shape[1], span).transpose(0, 1, 3, 2)
        return flipped.reshape(layers, requests, span, 1, values.shape[1])

    return (
        att.reshape(query_latent.shape),
        cache.reshape(layers, requests, span, 1, width),
        as_cache(cscale),
        as_cache(crope),
    )


def solution(mesh):
    placed = (
        P(None, ("group", "req", "sub"), "seq", None),
        P(None, ("group", "req", "sub"), "seq", None),
        P(None, ("group", "req", "sub"), "seq", None),
        P(("group", "req", "sub")),
        P(None, ("group", "req", "sub"), None, "seq", None),
        P(None, ("group", "req", "sub"), None, "seq", None),
        P(None, ("group", "req", "sub"), None, None),
        P(None, ("group", "req", "sub"), None, None),
    )
    return jax.shard_map(
        per_device_line if mesh.shape["seq"] == 4 else per_device,
        mesh=mesh,
        in_specs=placed,
        out_specs=(
            P(None, ("group", "req", "sub"), None, "seq", None),
            P(None, ("group", "req", "sub"), None, "seq", None),
            P(None, ("group", "req", "sub"), None, "seq", None),
            P(None, ("group", "req", "sub"), None, "seq", None),
        ),
        check_vma=False,
    )
```

```python
import jax
import jax.numpy as jnp
from jax import lax
from jax.experimental import pallas as pl
from jax.experimental.pallas import tpu as pltpu
from jax.sharding import PartitionSpec as P

softmax_gain = 192.0 ** (-0.5)
masked_score = -1e30


def dequantize(code_values, scale_values):
    blocks = scale_values.shape[-1]
    latent_width = code_values.shape[-1]
    shaped = code_values.astype(jnp.float32).reshape(
        code_values.shape[:-1] + (blocks, latent_width // blocks)
    )
    scaled = shaped * scale_values.astype(jnp.float32)[..., None]
    return scaled.reshape(code_values.shape).astype(jnp.bfloat16)


def shard_partial(
    lat_query, rope_query, key_rows, rope_rows, usable, new_keys, new_rope_rows, holds_new
):
    tokens_new, head_count, latent_width = lat_query.shape
    query_rows = lat_query.reshape(tokens_new * head_count, latent_width)
    query_pos = rope_query.reshape(tokens_new * head_count, rope_query.shape[-1])
    scores = jnp.dot(query_rows, key_rows.T, preferred_element_type=jnp.float32)
    scores = (
        scores + jnp.dot(query_pos, rope_rows.T, preferred_element_type=jnp.float32)
    ) * softmax_gain
    fresh_scores = jnp.dot(query_rows, new_keys.T, preferred_element_type=jnp.float32)
    fresh_scores = (
        fresh_scores + jnp.dot(query_pos, new_rope_rows.T, preferred_element_type=jnp.float32)
    ) * softmax_gain
    token_of_row = jnp.arange(tokens_new * head_count, dtype=jnp.int32) // head_count
    causal = (jnp.arange(tokens_new, dtype=jnp.int32)[None, :] <= token_of_row[:, None]) & holds_new
    scores = jnp.where(usable[None, :], scores, masked_score)
    fresh_scores = jnp.where(causal, fresh_scores, masked_score)
    group_peak = jnp.maximum(jnp.max(scores, 1), jnp.max(fresh_scores, 1)).astype(jnp.bfloat16)
    peak_float = group_peak.astype(jnp.float32)[:, None]
    weights = jnp.where(usable[None, :], jnp.exp(scores - peak_float), 0.0).astype(jnp.bfloat16)
    fresh_weights = jnp.where(causal, jnp.exp(fresh_scores - peak_float), 0.0).astype(jnp.bfloat16)
    group_total = jnp.sum(weights.astype(jnp.float32), 1) + jnp.sum(
        fresh_weights.astype(jnp.float32), 1
    )
    group_sum = jnp.dot(weights, key_rows, preferred_element_type=jnp.float32)
    group_sum = group_sum + jnp.dot(fresh_weights, new_keys, preferred_element_type=jnp.float32)
    return (
        group_sum.astype(jnp.bfloat16).reshape(tokens_new, head_count, latent_width),
        group_peak.reshape(tokens_new, head_count),
        group_total.astype(jnp.bfloat16).reshape(tokens_new, head_count),
    )


def merge_groups(pieces):
    group_sum, group_peak, group_total = pieces
    peak_float = group_peak.astype(jnp.float32)
    overall = jnp.max(peak_float, 0)
    factor = jnp.exp(peak_float - overall)
    numerator = jnp.sum(factor[..., None] * group_sum.astype(jnp.float32), 0)
    denominator = jnp.sum(factor * group_total.astype(jnp.float32), 0)
    return (numerator / denominator[..., None]).astype(jnp.bfloat16)


def per_device(
    latent_codes, latent_scales, rope_keys, lengths, query_latent, query_rope, new_latent, new_rope
):
    shard_count = lax.axis_size("seq")
    seq_index = lax.axis_index("seq")
    layer_count, request_count, span, latent_width = latent_codes.shape
    lat_query, rope_query = (
        lax.all_gather(query_latent, "seq", axis=3, tiled=True),
        lax.all_gather(query_rope, "seq", axis=3, tiled=True),
    )

    def regroup_rows(values):
        return values.reshape(
            values.shape[0], values.shape[1], span // shard_count, shard_count, values.shape[-1]
        )

    codes_moved, scales_moved, rope_moved = (
        lax.all_to_all(regroup_rows(latent_codes), "seq", split_axis=3, concat_axis=2, tiled=True),
        lax.all_to_all(regroup_rows(latent_scales), "seq", split_axis=3, concat_axis=2, tiled=True),
        lax.all_to_all(regroup_rows(rope_keys), "seq", split_axis=3, concat_axis=2, tiled=True),
    )
    offsets = jnp.arange(span, dtype=jnp.int32)
    key_rows = dequantize(latent_codes, latent_scales)
    positions = seq_index * span + offsets
    usable = positions[None, :] < lengths[:, None]
    holds_new = seq_index == 0
    per_request = jax.vmap(shard_partial, in_axes=(0, 0, 0, 0, 0, 0, 0, None))
    per_layer = jax.vmap(per_request, in_axes=(0, 0, 0, 0, None, 0, 0, None))
    group_sum, group_peak, group_total = per_layer(
        lat_query, rope_query, key_rows, rope_keys, usable, new_latent, new_rope, holds_new
    )
    attended = merge_groups(
        (
            lax.all_to_all(group_sum[None], "seq", split_axis=4, concat_axis=0, tiled=True),
            lax.all_to_all(group_peak[None], "seq", split_axis=4, concat_axis=0, tiled=True),
            lax.all_to_all(group_total[None], "seq", split_axis=4, concat_axis=0, tiled=True),
        )
    )
    return (attended, codes_moved, scales_moved, rope_moved)


def _hub_kernel(
    len_ref, codes_ref, rope_ref, scale_ref, q_ref, qr_ref, new_ref, newr_ref,
    att_ref, cache_ref, crope_ref, cscale_ref,
    lengths, perm, kbuf, abuf, sbuf, scale_in, scale_rows, raw, raws, rawq, qbuf, nkbuf, nrbuf,
    new_rows, newr_rows, keys, result, side_sum, side_stat, far_out, far_out_stat, far_in, far_in_stat,
    meter, load_sem, misc_sem, q_send, q_recv, k_send, k_recv, f_send, f_recv, s_send, s_recv,
    far_send, far_recv, r_send, r_recv, edge_in, far_edge_in,
):
    pairs, span, width = codes_ref.shape
    groups = 4
    rows = span // groups
    half = q_ref.shape[1]
    rope = qr_ref.shape[2]
    blocks = scale_ref.shape[1]
    fresh = new_ref.shape[1]
    heads = half // fresh
    fold = half * rope // width
    me = lax.axis_index("seq")
    is_hub = (me == 1) | (me == 2)
    is_edge = jnp.logical_not(is_hub)
    hub = 1 + me // 2
    edge = me // 2 * 3
    across = 3 - hub
    far_edge = 3 - edge
    f32, bf16 = jnp.float32, jnp.bfloat16

    def start(copies):
        for copy in copies:
            copy.start()

    def remote(src, dst, send, recv, target):
        return pltpu.make_async_remote_copy(
            src_ref=src, dst_ref=dst, send_sem=send, recv_sem=recv,
            device_id={"seq": target}, device_id_type=pl.DeviceIdType.MESH,
        )

    def greet(target):
        pl.semaphore_signal(
            pltpu.get_barrier_semaphore(), inc=1, device_id={"seq": target},
            device_id_type=pl.DeviceIdType.MESH,
        )

    def tell(sem, target):
        pl.semaphore_signal(sem, inc=1, device_id={"seq": target}, device_id_type=pl.DeviceIdType.MESH)

    def wait_bytes(ref, sem):
        pltpu.make_async_copy(ref, ref, sem).wait()

    def load(c):
        return (
            pltpu.make_async_copy(codes_ref.at[c], raw.at[c, pl.ds(0, span)], load_sem.at[c]),
            pltpu.make_async_copy(rope_ref.at[c], raw.at[c, pl.ds(span, rope)], load_sem.at[c]),
        )

    load_scales = pltpu.make_async_copy(scale_ref, raws, misc_sem.at[0])
    load_rotary = pltpu.make_async_copy(qr_ref, rawq, misc_sem.at[1])
    load_query = pltpu.make_async_copy(q_ref, qbuf.at[:, 0, pl.ds(0, half)], misc_sem.at[2])
    load_new = (
        pltpu.make_async_copy(new_ref, new_rows, misc_sem.at[3]),
        pltpu.make_async_copy(newr_ref, newr_rows, misc_sem.at[4]),
    )
    load_lengths = pltpu.make_async_copy(len_ref, lengths, misc_sem.at[5])

    def query_latent(c, flow, dst, target):
        return remote(q_ref.at[c], qbuf.at[c, dst, pl.ds(0, half)],
                      q_send.at[flow], q_recv.at[flow, c], target)

    def query_rotary(c, flow, dst, target):
        return remote(qbuf.at[c, 0, pl.ds(half, fold)], qbuf.at[c, dst, pl.ds(half, fold)],
                      q_send.at[flow], q_recv.at[flow, c], target)

    def forward_query(c):
        return remote(qbuf.at[c, 1], qbuf.at[c, 3], q_send.at[2], q_recv.at[1, c], across)

    def shard(c):
        return (
            remote(abuf.at[0, c], abuf.at[1, c], k_send.at[c], k_recv.at[c], hub),
            remote(kbuf.at[0, c], kbuf.at[1, c], k_send.at[c], k_recv.at[c], hub),
        )

    shard_scales = remote(sbuf.at[0], sbuf.at[1], s_send.at[0], s_recv.at[groups], hub)

    def place_of(slot):
        return hub if slot == 0 else edge

    def handover(slot, c, target, send):
        place = place_of(slot)
        spot = pl.multiple_of(place * rows, rows)
        return (
            remote(kbuf.at[slot, c, target], cache_ref.at[c, pl.ds(spot, rows)],
                   f_send.at[send], f_recv.at[place], target),
            remote(abuf.at[slot, c, target], crope_ref.at[c, :, pl.ds(spot, rows)],
                   f_send.at[send], f_recv.at[place], target),
        )

    def handover_far(slot, c):
        return handover(slot, c, far_edge, 1 + slot) + handover(slot, c, across, 1 + slot)

    def handover_scales(slot, target, send):
        return remote(sbuf.at[slot, target], scale_in.at[place_of(slot)],
                      s_send.at[send], s_recv.at[place_of(slot)], target)

    def keep_scales(tile, place):
        values = tile.astype(f32)
        for c in range(pairs):
            cscale_ref[c, :, pl.ds(pl.multiple_of(place * rows, rows), rows)] = (
                values[c * blocks:(c + 1) * blocks].astype(bf16)
            )

    def await_scales(place):
        wait_bytes(scale_in.at[place], s_recv.at[place])
        keep_scales(scale_in[place], place)

    def keep(slot, c, place):
        spot = pl.multiple_of(place * rows, rows)
        cache_ref[c, pl.ds(spot, rows), :] = kbuf[slot, c, me]
        crope_ref[c, :, pl.ds(spot, rows)] = abuf[slot, c, me]

    def sums(c):
        return (
            remote(far_out.at[c], far_in.at[c], far_send.at[0], far_recv.at[c], across),
            remote(far_out_stat.at[c], far_in_stat.at[c], far_send.at[0], far_recv.at[c], across),
        )

    def edge_result(c):
        return remote(result.at[c], att_ref.at[c], r_send.at[0], r_recv.at[0], edge)

    @pl.when(is_hub)
    def _():
        greet(across)
        greet(edge)

    load_rotary.start()

    @pl.when(is_hub)
    def _():
        pl.semaphore_wait(pltpu.get_barrier_semaphore(), 1)
        for c in range(pairs):
            query_latent(c, 1, 2, across).start()
        load_query.start()
        start(load_new)

    @pl.when(is_edge)
    def _():
        pl.semaphore_wait(pltpu.get_barrier_semaphore(), 1)
        tell(edge_in, hub)
        query_latent(0, 0, 1, hub).start()

    load_scales.start()
    for c in range(pairs):
        start(load(c))
    load_lengths.start()
    load_rotary.wait()
    for c in range(pairs):
        qbuf[c, 0, half:half + fold, :] = jnp.concatenate(
            [rawq[c, i * fold:(i + 1) * fold, :] for i in range(half // fold)], axis=1
        )

    @pl.when(is_hub)
    def _():
        for c in range(pairs):
            query_rotary(c, 1, 2, across).start()

    @pl.when(is_edge)
    def _():
        query_rotary(0, 0, 1, hub).start()

    line = lax.broadcasted_iota(jnp.int32, (span, span), 0)
    column = lax.broadcasted_iota(jnp.int32, (span, span), 1)
    perm[...] = jnp.where(column == (line % rows) * groups + line // rows, 1.0, 0.0).astype(bf16)
    dims = (((1,), (1,)), ((), ()))

    tile_rows = sbuf.shape[2]
    load_scales.wait()
    load_lengths.wait()
    stacked = [raws[c].astype(f32) for c in range(pairs)]
    if tile_rows > pairs * blocks:
        stacked.append(jnp.zeros((tile_rows - pairs * blocks, span), f32))
    stacked = jnp.concatenate(stacked, axis=0).astype(bf16)
    sorted_scales = lax.dot_general(stacked, perm[...], dims, preferred_element_type=f32)
    for k in range(groups):
        sbuf[0, k] = sorted_scales[:, k * rows:(k + 1) * rows].astype(bf16)
    keep_scales(sbuf[0, me], me)

    def spread_scales(slot):
        scale_rows[slot] = jnp.zeros(scale_rows.shape[1:], f32)
        for k in range(groups):
            values = sbuf[slot, k].astype(f32)
            for c in range(pairs):
                scale_rows[slot, c, 0:blocks, k * rows:(k + 1) * rows] = (
                    values[c * blocks:(c + 1) * blocks]
                )

    def prepare(c):
        wait_bytes(raw.at[c], load_sem.at[c])
        sorted_codes = jnp.dot(perm[...], raw[c, 0:span], preferred_element_type=f32)
        for k in range(groups):
            kbuf[0, c, k] = sorted_codes[k * rows:(k + 1) * rows].astype(bf16)
        sorted_rope = lax.dot_general(raw[c, span:span + rope], perm[...], dims, preferred_element_type=f32)
        for k in range(groups):
            abuf[0, c, k] = sorted_rope[:, k * rows:(k + 1) * rows].astype(bf16)

    def stats_of(m, d):
        lane = lax.broadcasted_iota(jnp.int32, (half, 128), 1)
        return jnp.where(
            lane < 2, jnp.where(lane == 0, m[:half], d[:half]), jnp.where(lane == 2, m[half:], d[half:])
        ).T[0:8]

    def columns_of(stat, j):
        return stat[:, 2 * j:2 * j + 1], stat[:, 2 * j + 1:2 * j + 2]

    def dequantize_keys(c):
        for slot in range(2):
            scales = scale_rows[slot, c].T
            for k in range(groups):
                for b in range(blocks):
                    lanes = slice(b * (width // blocks), (b + 1) * (width // blocks))
                    keys[slot * span + k * rows:slot * span + (k + 1) * rows, lanes] = (
                        kbuf[slot, c, k, :, lanes].astype(f32)
                        * scales[k * rows:(k + 1) * rows, b:b + 1]
                    ).astype(bf16)

    def partial(c, first):
        q = qbuf[c, first:first + 2, 0:half, :].reshape(2 * half, width)
        qr = jnp.concatenate(
            [
                qbuf[c, first + j, half:half + fold, i * rope:(i + 1) * rope]
                for j in range(2) for i in range(half // fold)
            ],
            axis=0,
        )
        ropes = jnp.concatenate(
            [abuf[slot, c, k] for slot in range(2) for k in range(groups)], axis=1
        )
        s = lax.dot_general(q, keys[...], dims, preferred_element_type=f32)
        s = (s + jnp.dot(qr, ropes, preferred_element_type=f32)) * softmax_gain
        column = lax.broadcasted_iota(jnp.int32, (1, 2 * span), 1)
        local = column % span
        position = jnp.where(column < span, hub, edge) * span + local % rows * groups + local // rows
        s = jnp.where(position < lengths[c % lengths.shape[0]], s, masked_score)
        m = jnp.max(s, axis=1, keepdims=True)
        if first == 0:
            t = lax.dot_general(q, nkbuf[c], dims, preferred_element_type=f32)
            t = (t + lax.dot_general(qr, nrbuf[c], dims, preferred_element_type=f32)) * softmax_gain
            token = lax.broadcasted_iota(jnp.int32, t.shape, 0) % half // heads
            t = jnp.where(lax.broadcasted_iota(jnp.int32, t.shape, 1) <= token, t, masked_score)
            m = jnp.maximum(m, jnp.max(t, axis=1, keepdims=True))
        w = jnp.exp(s - m).astype(bf16)
        d = jnp.sum(w.astype(f32), axis=1, keepdims=True)
        n = jnp.dot(w, keys[...], preferred_element_type=f32)
        if first == 0:
            v = jnp.exp(t - m).astype(bf16)
            d = d + jnp.sum(v.astype(f32), axis=1, keepdims=True)
            n = n + jnp.dot(v, nkbuf[c], preferred_element_type=f32)
        return n, stats_of(m, d)

    def merge(c):
        wait_bytes(meter.at[c], far_recv.at[c])
        side, far = side_stat[c].T, far_in_stat[c].T
        for j in (1, 0):
            m0, d0 = columns_of(side, j)
            m1, d1 = columns_of(far, j)
            m = jnp.maximum(m0, m1)
            f0, f1 = jnp.exp(m0 - m), jnp.exp(m1 - m)
            numerator = f0 * side_sum[c, j] + f1 * far_in[c, j].astype(f32)
            merged = (numerator / (f0 * d0 + f1 * d1)).astype(bf16)
            if j == 1:
                result[c] = merged
                edge_result(c).start()
            else:
                att_ref[c] = merged

    @pl.when(is_edge)
    def _():
        shard_scales.start()

        @pl.loop(0, pairs)
        def _(c):
            prepare(c)

            @pl.when(c >= 1)
            def _():
                wait_bytes(raw.at[0], k_send.at[c - 1])
                start((query_latent(c, 0, 1, hub), query_rotary(c, 0, 1, hub)))

            start(shard(c))
            keep(0, c, me)

        wait_bytes(raw.at[0], k_send.at[pairs - 1])
        shard_scales.wait_send()
        wait_bytes(qbuf.at[:, 0], q_send.at[0])
        for place in (hub, across, far_edge):
            await_scales(place)
        for place in (hub, across, far_edge):
            wait_bytes(qbuf.at[:, 0], f_recv.at[place])
        wait_bytes(att_ref, r_recv.at[0])

    @pl.when(is_hub)
    def _():
        pl.semaphore_wait(edge_in, 1)
        tell(far_edge_in, across)
        handover_scales(0, edge, 0).start()

        @pl.loop(0, pairs)
        def _(c):
            prepare(c)
            start(handover(0, c, edge, 0))
            keep(0, c, me)

        pl.semaphore_wait(far_edge_in, 1)
        for target in (across, far_edge):
            handover_scales(0, target, 1).start()
        wait_bytes(qbuf.at[0, 1], q_recv.at[0, 0])
        forward_query(0).start()
        start(handover_far(0, 0))
        for copy in load_new:
            copy.wait()
        nkbuf[...] = jnp.zeros(nkbuf.shape, bf16)
        nrbuf[...] = jnp.zeros(nrbuf.shape, bf16)
        for c in range(pairs):
            nkbuf[c, 0:fresh, :] = new_rows[c]
            nrbuf[c, 0:fresh, :] = newr_rows[c]
        load_query.wait()
        spread_scales(0)
        shard_scales.wait_recv()
        for target in (across, far_edge):
            handover_scales(1, target, 1).start()
        keep_scales(sbuf[1, me], edge)
        spread_scales(1)

        @pl.loop(0, pairs)
        def _(c):
            wait_bytes(raw.at[0], k_recv.at[c])
            start(handover_far(1, c))
            keep(1, c, edge)

            @pl.when(c < pairs - 1)
            def _():
                wait_bytes(qbuf.at[0, 1], q_recv.at[0, c + 1])
                forward_query(c + 1).start()

            wait_bytes(qbuf.at[0, pl.ds(2, 2)], q_recv.at[1, c])
            dequantize_keys(c)
            far_sum, far_out_stat[c] = partial(c, 2)
            for j in range(2):
                far_out[c, j] = far_sum[j * half:(j + 1) * half].astype(bf16)
            start(sums(c))

            @pl.when(c == 1)
            def _():
                start(handover_far(0, c))

            near_sum, side_stat[c] = partial(c, 0)
            for j in range(2):
                side_sum[c, j] = near_sum[j * half:(j + 1) * half]

            @pl.when(c >= 1)
            def _():
                merge(c - 1)

        for c in range(2, pairs):
            start(handover(0, c, far_edge, 1))
        for c in range(2, pairs):
            start(handover(0, c, across, 1))
        for place in (across, far_edge):
            await_scales(place)
        merge(pairs - 1)
        wait_bytes(sbuf.at[0, 0], s_send.at[0])
        wait_bytes(sbuf.at[0], s_send.at[1])
        for flow in (1, 2):
            wait_bytes(qbuf.at[:, 0], q_send.at[flow])
        wait_bytes(meter, far_send.at[0])
        wait_bytes(result, r_send.at[0])
        wait_bytes(qbuf.at[:, 0], f_send.at[0])
        for slot in range(2):
            wait_bytes(qbuf.at[:, pl.ds(0, 2)], f_send.at[1 + slot])
        for place in (across, far_edge):
            wait_bytes(qbuf.at[:, 0], f_recv.at[place])


def _emit_kernel(att_ref, cache_ref, crope_ref, cscale_ref, att_out, cache_out, crope_out, cscale_out, sem):
    copies = []
    for c in range(cache_ref.shape[0]):
        copies.append(pltpu.make_async_copy(cache_ref.at[c], cache_out.at[c], sem.at[len(copies)]))
    for src, dst in ((att_ref, att_out), (crope_ref, crope_out), (cscale_ref, cscale_out)):
        copies.append(pltpu.make_async_copy(src, dst, sem.at[len(copies)]))
    for copy in copies:
        copy.start()
    for copy in copies:
        copy.wait()


def emit(values):
    return pl.pallas_call(
        _emit_kernel,
        out_shape=[jax.ShapeDtypeStruct(v.shape, v.dtype) for v in values],
        in_specs=[pl.BlockSpec(memory_space=pl.ANY)] * 4,
        out_specs=[pl.BlockSpec(memory_space=pl.ANY)] * 4,
        scratch_shapes=[pltpu.SemaphoreType.DMA((values[1].shape[0] + 3,))],
        compiler_params=pltpu.CompilerParams(vmem_limit_bytes=1 << 20),
    )(*values)


def per_device_line(
    latent_codes, latent_scales, rope_keys, lengths, query_latent, query_rope, new_latent, new_rope
):
    layers, requests, span, width = latent_codes.shape
    pairs, rows = layers * requests, span // 4
    rope, blocks = rope_keys.shape[-1], latent_scales.shape[-1]
    tokens, heads = query_latent.shape[2:4]
    half = tokens * heads
    tile_rows = -(-pairs * blocks // 16) * 16
    hbm_spec = pl.BlockSpec(memory_space=pltpu.HBM)
    vmem_spec = pl.BlockSpec(memory_space=pltpu.VMEM)
    dma = pltpu.SemaphoreType.DMA
    bf16, f32 = jnp.bfloat16, jnp.float32
    att, cache, crope, cscale = pl.pallas_call(
        _hub_kernel,
        out_shape=(
            pltpu.VMEM((pairs, half, width), bf16),
            pltpu.VMEM((pairs, span, width), bf16),
            pltpu.VMEM((pairs, rope, span), bf16),
            pltpu.VMEM((pairs, blocks, span), bf16),
        ),
        in_specs=[hbm_spec] * 8,
        out_specs=(vmem_spec,) * 4,
        scratch_shapes=[
            pltpu.SMEM(lengths.shape, lengths.dtype),
            pltpu.VMEM((span, span), bf16),
            pltpu.VMEM((2, pairs, 4, rows, width), bf16),
            pltpu.VMEM((2, pairs, 4, rope, rows), bf16),
            pltpu.VMEM((2, 4, tile_rows, rows), bf16),
            pltpu.VMEM((4, tile_rows, rows), bf16),
            pltpu.VMEM((2, pairs, 8, span), f32),
            pltpu.VMEM((pairs, span + rope, width), bf16),
            pltpu.VMEM((pairs, blocks, span), bf16),
            pltpu.VMEM((pairs, half, rope), bf16),
            pltpu.VMEM((pairs, 4, half + half * rope // width, width), bf16),
            pltpu.VMEM((pairs, 128, width), bf16),
            pltpu.VMEM((pairs, 128, rope), bf16),
            pltpu.VMEM((pairs, tokens, width), bf16),
            pltpu.VMEM((pairs, tokens, rope), bf16),
            pltpu.VMEM((2 * span, width), bf16),
            pltpu.VMEM((pairs, half, width), bf16),
            pltpu.VMEM((pairs, 2, half, width), f32),
            pltpu.VMEM((pairs, 8, 128), f32),
            pltpu.VMEM((pairs, 2, half, width), bf16),
            pltpu.VMEM((pairs, 8, 128), f32),
            pltpu.VMEM((pairs, 2, half, width), bf16),
            pltpu.VMEM((pairs, 8, 128), f32),
            pltpu.VMEM((pairs, half * width // 128 + 8, 128), f32),
            dma((pairs,)), dma((6,)), dma((3,)), dma((2, pairs)), dma((pairs,)), dma((pairs,)),
            dma((3,)), dma((4,)), dma((2,)), dma((5,)), dma((1,)), dma((pairs,)), dma((1,)), dma((1,)),
            pltpu.SemaphoreType.REGULAR, pltpu.SemaphoreType.REGULAR,
        ],
        compiler_params=pltpu.CompilerParams(
            collective_id=0, has_side_effects=True, vmem_limit_bytes=56 << 20
        ),
    )(
        lengths, latent_codes.reshape(pairs, span, width),
        rope_keys.transpose(0, 1, 3, 2).reshape(pairs, rope, span),
        latent_scales.transpose(0, 1, 3, 2).reshape(pairs, blocks, span),
        query_latent.reshape(pairs, half, width), query_rope.reshape(pairs, half, rope),
        new_latent.reshape(pairs, tokens, width), new_rope.reshape(pairs, tokens, rope),
    )

    att, cache, crope, cscale = emit((att, cache, crope, cscale))

    def as_cache(values):
        flipped = values.reshape(layers, requests, values.shape[1], span).transpose(0, 1, 3, 2)
        return flipped.reshape(layers, requests, span, 1, values.shape[1])

    return (
        att.reshape(query_latent.shape),
        cache.reshape(layers, requests, span, 1, width),
        as_cache(cscale),
        as_cache(crope),
    )


def solution(mesh):
    placed = (
        P(None, ("group", "req", "sub"), "seq", None),
        P(None, ("group", "req", "sub"), "seq", None),
        P(None, ("group", "req", "sub"), "seq", None),
        P(("group", "req", "sub")),
        P(None, ("group", "req", "sub"), None, "seq", None),
        P(None, ("group", "req", "sub"), None, "seq", None),
        P(None, ("group", "req", "sub"), None, None),
        P(None, ("group", "req", "sub"), None, None),
    )
    return jax.shard_map(
        per_device_line if mesh.shape["seq"] == 4 else per_device,
        mesh=mesh,
        in_specs=placed,
        out_specs=(
            P(None, ("group", "req", "sub"), None, "seq", None),
            P(None, ("group", "req", "sub"), None, "seq", None),
            P(None, ("group", "req", "sub"), None, "seq", None),
            P(None, ("group", "req", "sub"), None, "seq", None),
        ),
        check_vma=False,
    )
```

```python
import jax
import jax.numpy as jnp
from jax import lax
from jax.experimental import pallas as pl
from jax.experimental.pallas import tpu as pltpu
from jax.sharding import PartitionSpec as P

softmax_gain = 192.0 ** (-0.5)
masked_score = -1e30


def dequantize(code_values, scale_values):
    blocks = scale_values.shape[-1]
    latent_width = code_values.shape[-1]
    shaped = code_values.astype(jnp.float32).reshape(
        code_values.shape[:-1] + (blocks, latent_width // blocks)
    )
    scaled = shaped * scale_values.astype(jnp.float32)[..., None]
    return scaled.reshape(code_values.shape).astype(jnp.bfloat16)


def shard_partial(
    lat_query, rope_query, key_rows, rope_rows, usable, new_keys, new_rope_rows, holds_new
):
    tokens_new, head_count, latent_width = lat_query.shape
    query_rows = lat_query.reshape(tokens_new * head_count, latent_width)
    query_pos = rope_query.reshape(tokens_new * head_count, rope_query.shape[-1])
    scores = jnp.dot(query_rows, key_rows.T, preferred_element_type=jnp.float32)
    scores = (
        scores + jnp.dot(query_pos, rope_rows.T, preferred_element_type=jnp.float32)
    ) * softmax_gain
    fresh_scores = jnp.dot(query_rows, new_keys.T, preferred_element_type=jnp.float32)
    fresh_scores = (
        fresh_scores + jnp.dot(query_pos, new_rope_rows.T, preferred_element_type=jnp.float32)
    ) * softmax_gain
    token_of_row = jnp.arange(tokens_new * head_count, dtype=jnp.int32) // head_count
    causal = (jnp.arange(tokens_new, dtype=jnp.int32)[None, :] <= token_of_row[:, None]) & holds_new
    scores = jnp.where(usable[None, :], scores, masked_score)
    fresh_scores = jnp.where(causal, fresh_scores, masked_score)
    group_peak = jnp.maximum(jnp.max(scores, 1), jnp.max(fresh_scores, 1)).astype(jnp.bfloat16)
    peak_float = group_peak.astype(jnp.float32)[:, None]
    weights = jnp.where(usable[None, :], jnp.exp(scores - peak_float), 0.0).astype(jnp.bfloat16)
    fresh_weights = jnp.where(causal, jnp.exp(fresh_scores - peak_float), 0.0).astype(jnp.bfloat16)
    group_total = jnp.sum(weights.astype(jnp.float32), 1) + jnp.sum(
        fresh_weights.astype(jnp.float32), 1
    )
    group_sum = jnp.dot(weights, key_rows, preferred_element_type=jnp.float32)
    group_sum = group_sum + jnp.dot(fresh_weights, new_keys, preferred_element_type=jnp.float32)
    return (
        group_sum.astype(jnp.bfloat16).reshape(tokens_new, head_count, latent_width),
        group_peak.reshape(tokens_new, head_count),
        group_total.astype(jnp.bfloat16).reshape(tokens_new, head_count),
    )


def merge_groups(pieces):
    group_sum, group_peak, group_total = pieces
    peak_float = group_peak.astype(jnp.float32)
    overall = jnp.max(peak_float, 0)
    factor = jnp.exp(peak_float - overall)
    numerator = jnp.sum(factor[..., None] * group_sum.astype(jnp.float32), 0)
    denominator = jnp.sum(factor * group_total.astype(jnp.float32), 0)
    return (numerator / denominator[..., None]).astype(jnp.bfloat16)


def per_device(
    latent_codes, latent_scales, rope_keys, lengths, query_latent, query_rope, new_latent, new_rope
):
    shard_count = lax.axis_size("seq")
    seq_index = lax.axis_index("seq")
    layer_count, request_count, span, latent_width = latent_codes.shape
    lat_query, rope_query = (
        lax.all_gather(query_latent, "seq", axis=3, tiled=True),
        lax.all_gather(query_rope, "seq", axis=3, tiled=True),
    )

    def regroup_rows(values):
        return values.reshape(
            values.shape[0], values.shape[1], span // shard_count, shard_count, values.shape[-1]
        )

    codes_moved, scales_moved, rope_moved = (
        lax.all_to_all(regroup_rows(latent_codes), "seq", split_axis=3, concat_axis=2, tiled=True),
        lax.all_to_all(regroup_rows(latent_scales), "seq", split_axis=3, concat_axis=2, tiled=True),
        lax.all_to_all(regroup_rows(rope_keys), "seq", split_axis=3, concat_axis=2, tiled=True),
    )
    offsets = jnp.arange(span, dtype=jnp.int32)
    key_rows = dequantize(latent_codes, latent_scales)
    positions = seq_index * span + offsets
    usable = positions[None, :] < lengths[:, None]
    holds_new = seq_index == 0
    per_request = jax.vmap(shard_partial, in_axes=(0, 0, 0, 0, 0, 0, 0, None))
    per_layer = jax.vmap(per_request, in_axes=(0, 0, 0, 0, None, 0, 0, None))
    group_sum, group_peak, group_total = per_layer(
        lat_query, rope_query, key_rows, rope_keys, usable, new_latent, new_rope, holds_new
    )
    attended = merge_groups(
        (
            lax.all_to_all(group_sum[None], "seq", split_axis=4, concat_axis=0, tiled=True),
            lax.all_to_all(group_peak[None], "seq", split_axis=4, concat_axis=0, tiled=True),
            lax.all_to_all(group_total[None], "seq", split_axis=4, concat_axis=0, tiled=True),
        )
    )
    return (attended, codes_moved, scales_moved, rope_moved)


def _hub_kernel(
    len_ref, codes_ref, rope_ref, scale_ref, q_ref, qr_ref, new_ref, newr_ref,
    att_ref, cache_ref, crope_ref, cscale_ref,
    lengths, perm, kbuf, abuf, sbuf, scale_in, scale_rows, raw, raws, rawq, qbuf, nkbuf, nrbuf,
    new_rows, newr_rows, keys, result, side_sum, side_stat, far_out, far_out_stat, far_in, far_in_stat,
    meter, load_sem, misc_sem, q_send, q_recv, k_send, k_recv, f_send, f_recv, s_send, s_recv,
    far_send, far_recv, r_send, r_recv, edge_in, far_edge_in,
):
    pairs, span, width = codes_ref.shape
    groups = 4
    rows = span // groups
    half = q_ref.shape[1]
    rope = qr_ref.shape[2]
    blocks = scale_ref.shape[1]
    fresh = new_ref.shape[1]
    heads = half // fresh
    fold = half * rope // width
    me = lax.axis_index("seq")
    is_hub = (me == 1) | (me == 2)
    is_edge = jnp.logical_not(is_hub)
    hub = 1 + me // 2
    edge = me // 2 * 3
    across = 3 - hub
    far_edge = 3 - edge
    f32, bf16 = jnp.float32, jnp.bfloat16

    def start(copies):
        for copy in copies:
            copy.start()

    def remote(src, dst, send, recv, target):
        return pltpu.make_async_remote_copy(
            src_ref=src, dst_ref=dst, send_sem=send, recv_sem=recv,
            device_id={"seq": target}, device_id_type=pl.DeviceIdType.MESH,
        )

    def greet(target):
        pl.semaphore_signal(
            pltpu.get_barrier_semaphore(), inc=1, device_id={"seq": target},
            device_id_type=pl.DeviceIdType.MESH,
        )

    def tell(sem, target):
        pl.semaphore_signal(sem, inc=1, device_id={"seq": target}, device_id_type=pl.DeviceIdType.MESH)

    def wait_bytes(ref, sem):
        pltpu.make_async_copy(ref, ref, sem).wait()

    def load(c):
        return (
            pltpu.make_async_copy(codes_ref.at[c], raw.at[c, pl.ds(0, span)], load_sem.at[0]),
            pltpu.make_async_copy(rope_ref.at[c], raw.at[c, pl.ds(span, rope)], load_sem.at[0]),
        )

    load_scales = pltpu.make_async_copy(scale_ref, raws, misc_sem.at[0])
    load_rotary = pltpu.make_async_copy(qr_ref, rawq, misc_sem.at[1])
    load_query = pltpu.make_async_copy(q_ref, qbuf.at[:, 0, pl.ds(0, half)], misc_sem.at[2])
    load_new = (
        pltpu.make_async_copy(new_ref, new_rows, misc_sem.at[3]),
        pltpu.make_async_copy(newr_ref, newr_rows, misc_sem.at[4]),
    )
    load_lengths = pltpu.make_async_copy(len_ref, lengths, misc_sem.at[5])

    def query_latent(c, flow, dst, target):
        return remote(q_ref.at[c], qbuf.at[c, dst, pl.ds(0, half)],
                      q_send.at[flow], q_recv.at[flow, c], target)

    def query_rotary(c, flow, dst, target):
        return remote(qbuf.at[c, 0, pl.ds(half, fold)], qbuf.at[c, dst, pl.ds(half, fold)],
                      q_send.at[flow], q_recv.at[flow, c], target)

    def forward_query(c):
        return remote(qbuf.at[c, 1], qbuf.at[c, 3], q_send.at[2], q_recv.at[1, c], across)

    def shard(c):
        return (
            remote(abuf.at[0, c], abuf.at[1, c], k_send.at[0], k_recv.at[c], hub),
            remote(kbuf.at[0, c], kbuf.at[1, c], k_send.at[0], k_recv.at[c], hub),
        )

    shard_scales = remote(sbuf.at[0], sbuf.at[1], s_send.at[0], s_recv.at[groups], hub)

    def place_of(slot):
        return hub if slot == 0 else edge

    def handover(slot, c, target, send):
        place = place_of(slot)
        spot = pl.multiple_of(place * rows, rows)
        return (
            remote(kbuf.at[slot, c, target], cache_ref.at[c, pl.ds(spot, rows)],
                   f_send.at[send], f_recv.at[place], target),
            remote(abuf.at[slot, c, target], crope_ref.at[c, :, pl.ds(spot, rows)],
                   f_send.at[send], f_recv.at[place], target),
        )

    def handover_far(slot, c):
        return handover(slot, c, far_edge, 1 + slot) + handover(slot, c, across, 1 + slot)

    def handover_scales(slot, target, send):
        return remote(sbuf.at[slot, target], scale_in.at[place_of(slot)],
                      s_send.at[send], s_recv.at[place_of(slot)], target)

    def keep_scales(tile, place):
        values = tile.astype(f32)
        for c in range(pairs):
            cscale_ref[c, :, pl.ds(pl.multiple_of(place * rows, rows), rows)] = (
                values[c * blocks:(c + 1) * blocks].astype(bf16)
            )

    def await_scales(place):
        wait_bytes(scale_in.at[place], s_recv.at[place])
        keep_scales(scale_in[place], place)

    def keep(slot, c, place):
        spot = pl.multiple_of(place * rows, rows)
        cache_ref[c, pl.ds(spot, rows), :] = kbuf[slot, c, me]
        crope_ref[c, :, pl.ds(spot, rows)] = abuf[slot, c, me]

    def sums(c):
        return (
            remote(far_out.at[c], far_in.at[c], far_send.at[0], far_recv.at[c], across),
            remote(far_out_stat.at[c], far_in_stat.at[c], far_send.at[0], far_recv.at[c], across),
        )

    def edge_result(c):
        return remote(result.at[c], att_ref.at[c], r_send.at[0], r_recv.at[0], edge)

    @pl.when(is_hub)
    def _():
        greet(across)
        greet(edge)

    load_rotary.start()

    @pl.when(is_hub)
    def _():
        pl.semaphore_wait(pltpu.get_barrier_semaphore(), 1)
        for c in range(pairs):
            query_latent(c, 1, 2, across).start()
        load_query.start()
        start(load_new)

    @pl.when(is_edge)
    def _():
        pl.semaphore_wait(pltpu.get_barrier_semaphore(), 1)
        tell(edge_in, hub)
        query_latent(0, 0, 1, hub).start()

    load_scales.start()
    for c in range(pairs):
        start(load(c))
    load_lengths.start()
    load_rotary.wait()
    for c in range(pairs):
        qbuf[c, 0, half:half + fold, :] = jnp.concatenate(
            [rawq[c, i * fold:(i + 1) * fold, :] for i in range(half // fold)], axis=1
        )

    @pl.when(is_hub)
    def _():
        for c in range(pairs):
            query_rotary(c, 1, 2, across).start()

    @pl.when(is_edge)
    def _():
        query_rotary(0, 0, 1, hub).start()

    line = lax.broadcasted_iota(jnp.int32, (span, span), 0)
    column = lax.broadcasted_iota(jnp.int32, (span, span), 1)
    perm[...] = jnp.where(column == (line % rows) * groups + line // rows, 1.0, 0.0).astype(bf16)
    dims = (((1,), (1,)), ((), ()))

    tile_rows = sbuf.shape[2]
    load_scales.wait()
    load_lengths.wait()
    wait_bytes(raw, load_sem.at[0])
    stacked = [raws[c].astype(f32) for c in range(pairs)]
    if tile_rows > pairs * blocks:
        stacked.append(jnp.zeros((tile_rows - pairs * blocks, span), f32))
    stacked = jnp.concatenate(stacked, axis=0).astype(bf16)
    sorted_scales = lax.dot_general(stacked, perm[...], dims, preferred_element_type=f32)
    for k in range(groups):
        sbuf[0, k] = sorted_scales[:, k * rows:(k + 1) * rows].astype(bf16)
    keep_scales(sbuf[0, me], me)

    def spread_scales(slot):
        scale_rows[slot] = jnp.zeros(scale_rows.shape[1:], f32)
        for k in range(groups):
            values = sbuf[slot, k].astype(f32)
            for c in range(pairs):
                scale_rows[slot, c, 0:blocks, k * rows:(k + 1) * rows] = (
                    values[c * blocks:(c + 1) * blocks]
                )

    def prepare(c):
        sorted_codes = jnp.dot(perm[...], raw[c, 0:span], preferred_element_type=f32)
        for k in range(groups):
            kbuf[0, c, k] = sorted_codes[k * rows:(k + 1) * rows].astype(bf16)
        sorted_rope = lax.dot_general(raw[c, span:span + rope], perm[...], dims, preferred_element_type=f32)
        for k in range(groups):
            abuf[0, c, k] = sorted_rope[:, k * rows:(k + 1) * rows].astype(bf16)

    def stats_of(m, d):
        lane = lax.broadcasted_iota(jnp.int32, (half, 128), 1)
        return jnp.where(
            lane < 2, jnp.where(lane == 0, m[:half], d[:half]), jnp.where(lane == 2, m[half:], d[half:])
        ).T[0:4]

    def columns_of(stat, j):
        return stat[:, 2 * j:2 * j + 1], stat[:, 2 * j + 1:2 * j + 2]

    def dequantize_keys(c):
        for slot in range(2):
            scales = scale_rows[slot, c].T
            for k in range(groups):
                for b in range(blocks):
                    lanes = slice(b * (width // blocks), (b + 1) * (width // blocks))
                    keys[slot * span + k * rows:slot * span + (k + 1) * rows, lanes] = (
                        kbuf[slot, c, k, :, lanes].astype(f32)
                        * scales[k * rows:(k + 1) * rows, b:b + 1]
                    ).astype(bf16)

    def partial(c, first):
        q = qbuf[c, first:first + 2, 0:half, :].reshape(2 * half, width)
        qr = jnp.concatenate(
            [
                qbuf[c, first + j, half:half + fold, i * rope:(i + 1) * rope]
                for j in range(2) for i in range(half // fold)
            ],
            axis=0,
        )
        ropes = jnp.concatenate(
            [abuf[slot, c, k] for slot in range(2) for k in range(groups)], axis=1
        )
        s = lax.dot_general(q, keys[...], dims, preferred_element_type=f32)
        s = (s + jnp.dot(qr, ropes, preferred_element_type=f32)) * softmax_gain
        column = lax.broadcasted_iota(jnp.int32, (1, 2 * span), 1)
        local = column % span
        position = jnp.where(column < span, hub, edge) * span + local % rows * groups + local // rows
        s = jnp.where(position < lengths[c % lengths.shape[0]], s, masked_score)
        m = jnp.max(s, axis=1, keepdims=True)
        if first == 0:
            t = lax.dot_general(q, nkbuf[c], dims, preferred_element_type=f32)
            t = (t + lax.dot_general(qr, nrbuf[c], dims, preferred_element_type=f32)) * softmax_gain
            token = lax.broadcasted_iota(jnp.int32, t.shape, 0) % half // heads
            t = jnp.where(lax.broadcasted_iota(jnp.int32, t.shape, 1) <= token, t, masked_score)
            m = jnp.maximum(m, jnp.max(t, axis=1, keepdims=True))
        w = jnp.exp(s - m).astype(bf16)
        d = jnp.sum(w.astype(f32), axis=1, keepdims=True)
        n = jnp.dot(w, keys[...], preferred_element_type=f32)
        if first == 0:
            v = jnp.exp(t - m).astype(bf16)
            d = d + jnp.sum(v.astype(f32), axis=1, keepdims=True)
            n = n + jnp.dot(v, nkbuf[c], preferred_element_type=f32)
        return n, stats_of(m, d)

    def merge(c):
        wait_bytes(meter.at[c], far_recv.at[c])
        pad = jnp.zeros((4, 128), f32)
        side = jnp.concatenate([side_stat[c], pad], axis=0).T
        far = jnp.concatenate([far_in_stat[c], pad], axis=0).T
        for j in (1, 0):
            m0, d0 = columns_of(side, j)
            m1, d1 = columns_of(far, j)
            m = jnp.maximum(m0, m1)
            f0, f1 = jnp.exp(m0 - m), jnp.exp(m1 - m)
            numerator = f0 * side_sum[c, j] + f1 * far_in[c, j].astype(f32)
            merged = (numerator / (f0 * d0 + f1 * d1)).astype(bf16)
            if j == 1:
                result[c] = merged
                edge_result(c).start()
            else:
                att_ref[c] = merged

    @pl.when(is_edge)
    def _():
        shard_scales.start()

        @pl.loop(0, pairs)
        def _(c):
            prepare(c)

            @pl.when(c >= 1)
            def _():
                wait_bytes(raw.at[0], k_send.at[0])
                start((query_latent(c, 0, 1, hub), query_rotary(c, 0, 1, hub)))

            start(shard(c))
            keep(0, c, me)

        wait_bytes(raw.at[0], k_send.at[0])
        shard_scales.wait_send()
        wait_bytes(qbuf.at[:, 0], q_send.at[0])
        for place in (hub, across, far_edge):
            await_scales(place)
        for place in (hub, across, far_edge):
            wait_bytes(qbuf.at[:, 0], f_recv.at[place])
        wait_bytes(att_ref, r_recv.at[0])

    @pl.when(is_hub)
    def _():
        pl.semaphore_wait(edge_in, 1)
        tell(far_edge_in, across)
        handover_scales(0, edge, 0).start()

        @pl.loop(0, pairs)
        def _(c):
            prepare(c)
            start(handover(0, c, edge, 0))
            keep(0, c, me)

        pl.semaphore_wait(far_edge_in, 1)
        for target in (across, far_edge):
            handover_scales(0, target, 1).start()
        wait_bytes(qbuf.at[0, 1], q_recv.at[0, 0])
        forward_query(0).start()
        start(handover_far(0, 0))
        for copy in load_new:
            copy.wait()
        nkbuf[...] = jnp.zeros(nkbuf.shape, bf16)
        nrbuf[...] = jnp.zeros(nrbuf.shape, bf16)
        for c in range(pairs):
            nkbuf[c, 0:fresh, :] = new_rows[c]
            nrbuf[c, 0:fresh, :] = newr_rows[c]
        load_query.wait()
        spread_scales(0)
        shard_scales.wait_recv()
        for target in (across, far_edge):
            handover_scales(1, target, 1).start()
        keep_scales(sbuf[1, me], edge)
        spread_scales(1)

        @pl.loop(0, pairs)
        def _(c):
            wait_bytes(raw.at[0], k_recv.at[c])
            start(handover_far(1, c))
            keep(1, c, edge)

            @pl.when(c < pairs - 1)
            def _():
                wait_bytes(qbuf.at[0, 1], q_recv.at[0, c + 1])
                forward_query(c + 1).start()

            wait_bytes(qbuf.at[0, pl.ds(2, 2)], q_recv.at[1, c])
            dequantize_keys(c)
            far_sum, far_out_stat[c] = partial(c, 2)
            for j in range(2):
                far_out[c, j] = far_sum[j * half:(j + 1) * half].astype(bf16)
            start(sums(c))

            @pl.when(c == 1)
            def _():
                start(handover_far(0, c))

            near_sum, side_stat[c] = partial(c, 0)
            for j in range(2):
                side_sum[c, j] = near_sum[j * half:(j + 1) * half]

            @pl.when(c >= 1)
            def _():
                merge(c - 1)

        for c in range(2, pairs):
            start(handover(0, c, far_edge, 1))
        for c in range(2, pairs):
            start(handover(0, c, across, 1))
        for place in (across, far_edge):
            await_scales(place)
        merge(pairs - 1)
        wait_bytes(sbuf.at[0, 0], s_send.at[0])
        wait_bytes(sbuf.at[0], s_send.at[1])
        for flow in (1, 2):
            wait_bytes(qbuf.at[:, 0], q_send.at[flow])
        wait_bytes(meter, far_send.at[0])
        wait_bytes(result, r_send.at[0])
        wait_bytes(qbuf.at[:, 0], f_send.at[0])
        for slot in range(2):
            wait_bytes(qbuf.at[:, pl.ds(0, 2)], f_send.at[1 + slot])
        for place in (across, far_edge):
            wait_bytes(qbuf.at[:, 0], f_recv.at[place])


def _emit_kernel(att_ref, cache_ref, crope_ref, cscale_ref, att_out, cache_out, crope_out, cscale_out, sem):
    copies = []
    for c in range(cache_ref.shape[0]):
        copies.append(pltpu.make_async_copy(cache_ref.at[c], cache_out.at[c], sem.at[len(copies)]))
    for src, dst in ((att_ref, att_out), (crope_ref, crope_out), (cscale_ref, cscale_out)):
        copies.append(pltpu.make_async_copy(src, dst, sem.at[len(copies)]))
    for copy in copies:
        copy.start()
    for copy in copies:
        copy.wait()


def emit(values):
    return pl.pallas_call(
        _emit_kernel,
        out_shape=[jax.ShapeDtypeStruct(v.shape, v.dtype) for v in values],
        in_specs=[pl.BlockSpec(memory_space=pl.ANY)] * 4,
        out_specs=[pl.BlockSpec(memory_space=pl.ANY)] * 4,
        scratch_shapes=[pltpu.SemaphoreType.DMA((values[1].shape[0] + 3,))],
        compiler_params=pltpu.CompilerParams(vmem_limit_bytes=1 << 20),
    )(*values)


def per_device_line(
    latent_codes, latent_scales, rope_keys, lengths, query_latent, query_rope, new_latent, new_rope
):
    layers, requests, span, width = latent_codes.shape
    pairs, rows = layers * requests, span // 4
    rope, blocks = rope_keys.shape[-1], latent_scales.shape[-1]
    tokens, heads = query_latent.shape[2:4]
    half = tokens * heads
    tile_rows = -(-pairs * blocks // 16) * 16
    hbm_spec = pl.BlockSpec(memory_space=pltpu.HBM)
    vmem_spec = pl.BlockSpec(memory_space=pltpu.VMEM)
    dma = pltpu.SemaphoreType.DMA
    bf16, f32 = jnp.bfloat16, jnp.float32
    att, cache, crope, cscale = pl.pallas_call(
        _hub_kernel,
        out_shape=(
            pltpu.VMEM((pairs, half, width), bf16),
            pltpu.VMEM((pairs, span, width), bf16),
            pltpu.VMEM((pairs, rope, span), bf16),
            pltpu.VMEM((pairs, blocks, span), bf16),
        ),
        in_specs=[hbm_spec] * 8,
        out_specs=(vmem_spec,) * 4,
        scratch_shapes=[
            pltpu.SMEM(lengths.shape, lengths.dtype),
            pltpu.VMEM((span, span), bf16),
            pltpu.VMEM((2, pairs, 4, rows, width), bf16),
            pltpu.VMEM((2, pairs, 4, rope, rows), bf16),
            pltpu.VMEM((2, 4, tile_rows, rows), bf16),
            pltpu.VMEM((4, tile_rows, rows), bf16),
            pltpu.VMEM((2, pairs, 8, span), f32),
            pltpu.VMEM((pairs, span + rope, width), bf16),
            pltpu.VMEM((pairs, blocks, span), bf16),
            pltpu.VMEM((pairs, half, rope), bf16),
            pltpu.VMEM((pairs, 4, half + half * rope // width, width), bf16),
            pltpu.VMEM((pairs, 128, width), bf16),
            pltpu.VMEM((pairs, 128, rope), bf16),
            pltpu.VMEM((pairs, tokens, width), bf16),
            pltpu.VMEM((pairs, tokens, rope), bf16),
            pltpu.VMEM((2 * span, width), bf16),
            pltpu.VMEM((pairs, half, width), bf16),
            pltpu.VMEM((pairs, 2, half, width), f32),
            pltpu.VMEM((pairs, 4, 128), f32),
            pltpu.VMEM((pairs, 2, half, width), bf16),
            pltpu.VMEM((pairs, 4, 128), f32),
            pltpu.VMEM((pairs, 2, half, width), bf16),
            pltpu.VMEM((pairs, 4, 128), f32),
            pltpu.VMEM((pairs, half * width // 128 + 4, 128), f32),
            dma((1,)), dma((6,)), dma((3,)), dma((2, pairs)), dma((1,)), dma((pairs,)),
            dma((3,)), dma((4,)), dma((2,)), dma((5,)), dma((1,)), dma((pairs,)), dma((1,)), dma((1,)),
            pltpu.SemaphoreType.REGULAR, pltpu.SemaphoreType.REGULAR,
        ],
        compiler_params=pltpu.CompilerParams(
            collective_id=0, has_side_effects=True, vmem_limit_bytes=56 << 20
        ),
    )(
        lengths, latent_codes.reshape(pairs, span, width),
        rope_keys.transpose(0, 1, 3, 2).reshape(pairs, rope, span),
        latent_scales.transpose(0, 1, 3, 2).reshape(pairs, blocks, span),
        query_latent.reshape(pairs, half, width), query_rope.reshape(pairs, half, rope),
        new_latent.reshape(pairs, tokens, width), new_rope.reshape(pairs, tokens, rope),
    )

    att, cache, crope, cscale = emit((att, cache, crope, cscale))

    def as_cache(values):
        flipped = values.reshape(layers, requests, values.shape[1], span).transpose(0, 1, 3, 2)
        return flipped.reshape(layers, requests, span, 1, values.shape[1])

    return (
        att.reshape(query_latent.shape),
        cache.reshape(layers, requests, span, 1, width),
        as_cache(cscale),
        as_cache(crope),
    )


def solution(mesh):
    placed = (
        P(None, ("group", "req", "sub"), "seq", None),
        P(None, ("group", "req", "sub"), "seq", None),
        P(None, ("group", "req", "sub"), "seq", None),
        P(("group", "req", "sub")),
        P(None, ("group", "req", "sub"), None, "seq", None),
        P(None, ("group", "req", "sub"), None, "seq", None),
        P(None, ("group", "req", "sub"), None, None),
        P(None, ("group", "req", "sub"), None, None),
    )
    return jax.shard_map(
        per_device_line if mesh.shape["seq"] == 4 else per_device,
        mesh=mesh,
        in_specs=placed,
        out_specs=(
            P(None, ("group", "req", "sub"), None, "seq", None),
            P(None, ("group", "req", "sub"), None, "seq", None),
            P(None, ("group", "req", "sub"), None, "seq", None),
            P(None, ("group", "req", "sub"), None, "seq", None),
        ),
        check_vma=False,
    )
```

```python
import jax
import jax.numpy as jnp
from jax import lax
from jax.experimental import pallas as pl
from jax.experimental.pallas import tpu as pltpu
from jax.sharding import PartitionSpec as P

softmax_gain = 192.0 ** (-0.5)
masked_score = -1e30


def dequantize(code_values, scale_values):
    blocks = scale_values.shape[-1]
    latent_width = code_values.shape[-1]
    shaped = code_values.astype(jnp.float32).reshape(
        code_values.shape[:-1] + (blocks, latent_width // blocks)
    )
    scaled = shaped * scale_values.astype(jnp.float32)[..., None]
    return scaled.reshape(code_values.shape).astype(jnp.bfloat16)


def shard_partial(
    lat_query, rope_query, key_rows, rope_rows, usable, new_keys, new_rope_rows, holds_new
):
    tokens_new, head_count, latent_width = lat_query.shape
    query_rows = lat_query.reshape(tokens_new * head_count, latent_width)
    query_pos = rope_query.reshape(tokens_new * head_count, rope_query.shape[-1])
    scores = jnp.dot(query_rows, key_rows.T, preferred_element_type=jnp.float32)
    scores = (
        scores + jnp.dot(query_pos, rope_rows.T, preferred_element_type=jnp.float32)
    ) * softmax_gain
    fresh_scores = jnp.dot(query_rows, new_keys.T, preferred_element_type=jnp.float32)
    fresh_scores = (
        fresh_scores + jnp.dot(query_pos, new_rope_rows.T, preferred_element_type=jnp.float32)
    ) * softmax_gain
    token_of_row = jnp.arange(tokens_new * head_count, dtype=jnp.int32) // head_count
    causal = (jnp.arange(tokens_new, dtype=jnp.int32)[None, :] <= token_of_row[:, None]) & holds_new
    scores = jnp.where(usable[None, :], scores, masked_score)
    fresh_scores = jnp.where(causal, fresh_scores, masked_score)
    group_peak = jnp.maximum(jnp.max(scores, 1), jnp.max(fresh_scores, 1)).astype(jnp.bfloat16)
    peak_float = group_peak.astype(jnp.float32)[:, None]
    weights = jnp.where(usable[None, :], jnp.exp(scores - peak_float), 0.0).astype(jnp.bfloat16)
    fresh_weights = jnp.where(causal, jnp.exp(fresh_scores - peak_float), 0.0).astype(jnp.bfloat16)
    group_total = jnp.sum(weights.astype(jnp.float32), 1) + jnp.sum(
        fresh_weights.astype(jnp.float32), 1
    )
    group_sum = jnp.dot(weights, key_rows, preferred_element_type=jnp.float32)
    group_sum = group_sum + jnp.dot(fresh_weights, new_keys, preferred_element_type=jnp.float32)
    return (
        group_sum.astype(jnp.bfloat16).reshape(tokens_new, head_count, latent_width),
        group_peak.reshape(tokens_new, head_count),
        group_total.astype(jnp.bfloat16).reshape(tokens_new, head_count),
    )


def merge_groups(pieces):
    group_sum, group_peak, group_total = pieces
    peak_float = group_peak.astype(jnp.float32)
    overall = jnp.max(peak_float, 0)
    factor = jnp.exp(peak_float - overall)
    numerator = jnp.sum(factor[..., None] * group_sum.astype(jnp.float32), 0)
    denominator = jnp.sum(factor * group_total.astype(jnp.float32), 0)
    return (numerator / denominator[..., None]).astype(jnp.bfloat16)


def per_device(
    latent_codes, latent_scales, rope_keys, lengths, query_latent, query_rope, new_latent, new_rope
):
    shard_count = lax.axis_size("seq")
    seq_index = lax.axis_index("seq")
    layer_count, request_count, span, latent_width = latent_codes.shape
    lat_query, rope_query = (
        lax.all_gather(query_latent, "seq", axis=3, tiled=True),
        lax.all_gather(query_rope, "seq", axis=3, tiled=True),
    )

    def regroup_rows(values):
        return values.reshape(
            values.shape[0], values.shape[1], span // shard_count, shard_count, values.shape[-1]
        )

    codes_moved, scales_moved, rope_moved = (
        lax.all_to_all(regroup_rows(latent_codes), "seq", split_axis=3, concat_axis=2, tiled=True),
        lax.all_to_all(regroup_rows(latent_scales), "seq", split_axis=3, concat_axis=2, tiled=True),
        lax.all_to_all(regroup_rows(rope_keys), "seq", split_axis=3, concat_axis=2, tiled=True),
    )
    offsets = jnp.arange(span, dtype=jnp.int32)
    key_rows = dequantize(latent_codes, latent_scales)
    positions = seq_index * span + offsets
    usable = positions[None, :] < lengths[:, None]
    holds_new = seq_index == 0
    per_request = jax.vmap(shard_partial, in_axes=(0, 0, 0, 0, 0, 0, 0, None))
    per_layer = jax.vmap(per_request, in_axes=(0, 0, 0, 0, None, 0, 0, None))
    group_sum, group_peak, group_total = per_layer(
        lat_query, rope_query, key_rows, rope_keys, usable, new_latent, new_rope, holds_new
    )
    attended = merge_groups(
        (
            lax.all_to_all(group_sum[None], "seq", split_axis=4, concat_axis=0, tiled=True),
            lax.all_to_all(group_peak[None], "seq", split_axis=4, concat_axis=0, tiled=True),
            lax.all_to_all(group_total[None], "seq", split_axis=4, concat_axis=0, tiled=True),
        )
    )
    return (attended, codes_moved, scales_moved, rope_moved)


def _hub_kernel(
    len_ref, codes_ref, rope_ref, scale_ref, q_ref, qr_ref, new_ref, newr_ref,
    att_ref, cache_ref, crope_ref, cscale_ref,
    lengths, perm, kbuf, abuf, sbuf, scale_in, scale_rows, raw, raws, rawq, qbuf, nkbuf, nrbuf,
    new_rows, newr_rows, keys, result, side_sum, side_stat, far_out, far_out_stat, far_in, far_in_stat,
    meter, load_sem, misc_sem, q_send, q_recv, k_send, k_recv, f_send, f_recv, s_send, s_recv,
    far_send, far_recv, r_send, r_recv, edge_in, far_edge_in,
):
    pairs, span, width = codes_ref.shape
    groups = 4
    rows = span // groups
    half = q_ref.shape[1]
    rope = qr_ref.shape[2]
    blocks = scale_ref.shape[1]
    fresh = new_ref.shape[1]
    heads = half // fresh
    fold = half * rope // width
    me = lax.axis_index("seq")
    is_hub = (me == 1) | (me == 2)
    is_edge = jnp.logical_not(is_hub)
    hub = 1 + me // 2
    edge = me // 2 * 3
    across = 3 - hub
    far_edge = 3 - edge
    f32, bf16 = jnp.float32, jnp.bfloat16

    def start(copies):
        for copy in copies:
            copy.start()

    def remote(src, dst, send, recv, target):
        return pltpu.make_async_remote_copy(
            src_ref=src, dst_ref=dst, send_sem=send, recv_sem=recv,
            device_id={"seq": target}, device_id_type=pl.DeviceIdType.MESH,
        )

    def greet(target):
        pl.semaphore_signal(
            pltpu.get_barrier_semaphore(), inc=1, device_id={"seq": target},
            device_id_type=pl.DeviceIdType.MESH,
        )

    def tell(sem, target):
        pl.semaphore_signal(sem, inc=1, device_id={"seq": target}, device_id_type=pl.DeviceIdType.MESH)

    def wait_bytes(ref, sem):
        pltpu.make_async_copy(ref, ref, sem).wait()

    def load(c):
        return (
            pltpu.make_async_copy(codes_ref.at[c], raw.at[c, pl.ds(0, span)], load_sem.at[0]),
            pltpu.make_async_copy(rope_ref.at[c], raw.at[c, pl.ds(span, rope)], load_sem.at[0]),
        )

    load_scales = pltpu.make_async_copy(scale_ref, raws, misc_sem.at[0])
    load_rotary = pltpu.make_async_copy(qr_ref, rawq, misc_sem.at[1])
    load_query = pltpu.make_async_copy(q_ref, qbuf.at[:, 0, pl.ds(0, half)], misc_sem.at[2])
    load_new = (
        pltpu.make_async_copy(new_ref, new_rows, misc_sem.at[3]),
        pltpu.make_async_copy(newr_ref, newr_rows, misc_sem.at[4]),
    )
    load_lengths = pltpu.make_async_copy(len_ref, lengths, misc_sem.at[5])

    def query_latent(c, flow, dst, target):
        return remote(q_ref.at[c], qbuf.at[c, dst, pl.ds(0, half)],
                      q_send.at[flow], q_recv.at[flow, c], target)

    def query_rotary(c, flow, dst, target):
        return remote(qbuf.at[c, 0, pl.ds(half, fold)], qbuf.at[c, dst, pl.ds(half, fold)],
                      q_send.at[flow], q_recv.at[flow, c], target)

    def forward_query(c):
        return remote(qbuf.at[c, 1], qbuf.at[c, 3], q_send.at[2], q_recv.at[1, c], across)

    def shard(c):
        return (
            remote(abuf.at[0, c], abuf.at[1, c], k_send.at[0], k_recv.at[c], hub),
            remote(kbuf.at[0, c], kbuf.at[1, c], k_send.at[0], k_recv.at[c], hub),
        )

    shard_scales = remote(sbuf.at[0], sbuf.at[1], s_send.at[0], s_recv.at[groups], hub)

    def place_of(slot):
        return hub if slot == 0 else edge

    def handover(slot, c, target, send):
        place = place_of(slot)
        spot = pl.multiple_of(place * rows, rows)
        return (
            remote(kbuf.at[slot, c, target], cache_ref.at[c, pl.ds(spot, rows)],
                   f_send.at[send], f_recv.at[place], target),
            remote(abuf.at[slot, c, target], crope_ref.at[c, :, pl.ds(spot, rows)],
                   f_send.at[send], f_recv.at[place], target),
        )

    def handover_far(slot, c):
        return handover(slot, c, far_edge, 1 + slot) + handover(slot, c, across, 1 + slot)

    def handover_scales(slot, target, send):
        return remote(sbuf.at[slot, target], scale_in.at[place_of(slot)],
                      s_send.at[send], s_recv.at[place_of(slot)], target)

    def keep_scales(tile, place):
        values = tile.astype(f32)
        for c in range(pairs):
            cscale_ref[c, :, pl.ds(pl.multiple_of(place * rows, rows), rows)] = (
                values[c * blocks:(c + 1) * blocks].astype(bf16)
            )

    def await_scales(place):
        wait_bytes(scale_in.at[place], s_recv.at[place])
        keep_scales(scale_in[place], place)

    def keep(slot, c, place):
        spot = pl.multiple_of(place * rows, rows)
        cache_ref[c, pl.ds(spot, rows), :] = kbuf[slot, c, me]
        crope_ref[c, :, pl.ds(spot, rows)] = abuf[slot, c, me]

    def sums(c):
        return (
            remote(far_out.at[c], far_in.at[c], far_send.at[0], far_recv.at[c], across),
            remote(far_out_stat.at[c], far_in_stat.at[c], far_send.at[0], far_recv.at[c], across),
        )

    def edge_result(c):
        return remote(result.at[c], att_ref.at[c], r_send.at[0], r_recv.at[0], edge)

    @pl.when(is_hub)
    def _():
        greet(across)
        greet(edge)

    load_rotary.start()

    @pl.when(is_hub)
    def _():
        pl.semaphore_wait(pltpu.get_barrier_semaphore(), 1)
        for c in range(pairs):
            query_latent(c, 1, 2, across).start()
        load_query.start()
        start(load_new)

    @pl.when(is_edge)
    def _():
        pl.semaphore_wait(pltpu.get_barrier_semaphore(), 1)
        tell(edge_in, hub)
        query_latent(0, 0, 1, hub).start()

    load_scales.start()
    for c in range(pairs):
        start(load(c))
    load_lengths.start()
    load_rotary.wait()
    for c in range(pairs):
        qbuf[c, 0, half:half + fold, :] = jnp.concatenate(
            [rawq[c, i * fold:(i + 1) * fold, :] for i in range(half // fold)], axis=1
        )

    @pl.when(is_hub)
    def _():
        for c in range(pairs):
            query_rotary(c, 1, 2, across).start()

    @pl.when(is_edge)
    def _():
        query_rotary(0, 0, 1, hub).start()

    line = lax.broadcasted_iota(jnp.int32, (span, span), 0)
    column = lax.broadcasted_iota(jnp.int32, (span, span), 1)
    perm[...] = jnp.where(column == (line % rows) * groups + line // rows, 1.0, 0.0).astype(bf16)
    dims = (((1,), (1,)), ((), ()))

    tile_rows = sbuf.shape[2]
    load_scales.wait()
    load_lengths.wait()
    wait_bytes(raw, load_sem.at[0])
    stacked = [raws[c].astype(f32) for c in range(pairs)]
    if tile_rows > pairs * blocks:
        stacked.append(jnp.zeros((tile_rows - pairs * blocks, span), f32))
    stacked = jnp.concatenate(stacked, axis=0).astype(bf16)
    sorted_scales = lax.dot_general(stacked, perm[...], dims, preferred_element_type=f32)
    for k in range(groups):
        sbuf[0, k] = sorted_scales[:, k * rows:(k + 1) * rows].astype(bf16)
    keep_scales(sbuf[0, me], me)

    def spread_scales(slot):
        scale_rows[slot] = jnp.zeros(scale_rows.shape[1:], f32)
        for k in range(groups):
            values = sbuf[slot, k].astype(f32)
            for c in range(pairs):
                scale_rows[slot, c, 0:blocks, k * rows:(k + 1) * rows] = (
                    values[c * blocks:(c + 1) * blocks]
                )

    def prepare(c):
        sorted_codes = jnp.dot(perm[...], raw[c, 0:span], preferred_element_type=f32)
        for k in range(groups):
            kbuf[0, c, k] = sorted_codes[k * rows:(k + 1) * rows].astype(bf16)
        sorted_rope = lax.dot_general(raw[c, span:span + rope], perm[...], dims, preferred_element_type=f32)
        for k in range(groups):
            abuf[0, c, k] = sorted_rope[:, k * rows:(k + 1) * rows].astype(bf16)

    def stats_of(m, d):
        lane = lax.broadcasted_iota(jnp.int32, (half, 128), 1)
        return jnp.where(
            lane < 2, jnp.where(lane == 0, m[:half], d[:half]), jnp.where(lane == 2, m[half:], d[half:])
        ).T[0:4]

    def columns_of(stat, j):
        return stat[:, 2 * j:2 * j + 1], stat[:, 2 * j + 1:2 * j + 2]

    def dequantize_keys(c):
        for slot in range(2):
            scales = scale_rows[slot, c].T
            for k in range(groups):
                for b in range(blocks):
                    lanes = slice(b * (width // blocks), (b + 1) * (width // blocks))
                    keys[slot * span + k * rows:slot * span + (k + 1) * rows, lanes] = (
                        kbuf[slot, c, k, :, lanes].astype(f32)
                        * scales[k * rows:(k + 1) * rows, b:b + 1]
                    ).astype(bf16)

    def partial(c, first):
        q = qbuf[c, first:first + 2, 0:half, :].reshape(2 * half, width)
        qr = jnp.concatenate(
            [
                qbuf[c, first + j, half:half + fold, i * rope:(i + 1) * rope]
                for j in range(2) for i in range(half // fold)
            ],
            axis=0,
        )
        ropes = jnp.concatenate(
            [abuf[slot, c, k] for slot in range(2) for k in range(groups)], axis=1
        )
        s = lax.dot_general(q, keys[...], dims, preferred_element_type=f32)
        s = (s + jnp.dot(qr, ropes, preferred_element_type=f32)) * softmax_gain
        column = lax.broadcasted_iota(jnp.int32, (1, 2 * span), 1)
        local = column % span
        position = jnp.where(column < span, hub, edge) * span + local % rows * groups + local // rows
        s = jnp.where(position < lengths[c % lengths.shape[0]], s, masked_score)
        m = jnp.max(s, axis=1, keepdims=True)
        if first == 0:
            t = lax.dot_general(q, nkbuf[c], dims, preferred_element_type=f32)
            t = (t + lax.dot_general(qr, nrbuf[c], dims, preferred_element_type=f32)) * softmax_gain
            token = lax.broadcasted_iota(jnp.int32, t.shape, 0) % half // heads
            t = jnp.where(lax.broadcasted_iota(jnp.int32, t.shape, 1) <= token, t, masked_score)
            m = jnp.maximum(m, jnp.max(t, axis=1, keepdims=True))
        w = jnp.exp(s - m).astype(bf16)
        d = jnp.sum(w.astype(f32), axis=1, keepdims=True)
        n = jnp.dot(w, keys[...], preferred_element_type=f32)
        if first == 0:
            v = jnp.exp(t - m).astype(bf16)
            d = d + jnp.sum(v.astype(f32), axis=1, keepdims=True)
            n = n + jnp.dot(v, nkbuf[c], preferred_element_type=f32)
        return n, stats_of(m, d)

    def merge(c):
        wait_bytes(meter.at[c], far_recv.at[c])
        pad = jnp.zeros((4, 128), f32)
        side = jnp.concatenate([side_stat[c], pad], axis=0).T
        far = jnp.concatenate([far_in_stat[c], pad], axis=0).T
        for j in (1, 0):
            m0, d0 = columns_of(side, j)
            m1, d1 = columns_of(far, j)
            m = jnp.maximum(m0, m1)
            f0, f1 = jnp.exp(m0 - m), jnp.exp(m1 - m)
            numerator = f0 * side_sum[c, j] + f1 * far_in[c, j].astype(f32)
            merged = (numerator / (f0 * d0 + f1 * d1)).astype(bf16)
            if j == 1:
                result[c] = merged
                edge_result(c).start()
            else:
                att_ref[c] = merged

    @pl.when(is_edge)
    def _():
        shard_scales.start()

        @pl.loop(0, pairs)
        def _(c):
            prepare(c)

            @pl.when(c >= 1)
            def _():
                wait_bytes(raw.at[0], k_send.at[0])
                start((query_latent(c, 0, 1, hub), query_rotary(c, 0, 1, hub)))

            start(shard(c))
            keep(0, c, me)

        wait_bytes(raw.at[0], k_send.at[0])
        shard_scales.wait_send()
        wait_bytes(qbuf.at[:, 0], q_send.at[0])
        for place in (hub, across, far_edge):
            await_scales(place)
        for place in (hub, across, far_edge):
            wait_bytes(qbuf.at[:, 0], f_recv.at[place])
        wait_bytes(att_ref, r_recv.at[0])

    @pl.when(is_hub)
    def _():
        pl.semaphore_wait(edge_in, 1)
        tell(far_edge_in, across)
        handover_scales(0, edge, 0).start()

        @pl.loop(0, pairs)
        def _(c):
            prepare(c)
            start(handover(0, c, edge, 0))
            keep(0, c, me)

        pl.semaphore_wait(far_edge_in, 1)
        for target in (across, far_edge):
            handover_scales(0, target, 1).start()
        wait_bytes(qbuf.at[0, 1], q_recv.at[0, 0])
        forward_query(0).start()
        start(handover_far(0, 0))
        for copy in load_new:
            copy.wait()
        nkbuf[...] = jnp.zeros(nkbuf.shape, bf16)
        nrbuf[...] = jnp.zeros(nrbuf.shape, bf16)
        for c in range(pairs):
            nkbuf[c, 0:fresh, :] = new_rows[c]
            nrbuf[c, 0:fresh, :] = newr_rows[c]
        load_query.wait()
        spread_scales(0)
        shard_scales.wait_recv()
        for target in (across, far_edge):
            handover_scales(1, target, 1).start()
        keep_scales(sbuf[1, me], edge)
        spread_scales(1)

        @pl.loop(0, pairs)
        def _(c):
            wait_bytes(raw.at[0], k_recv.at[c])
            start(handover_far(1, c))
            keep(1, c, edge)

            @pl.when(c < pairs - 1)
            def _():
                wait_bytes(qbuf.at[0, 1], q_recv.at[0, c + 1])
                forward_query(c + 1).start()

            wait_bytes(qbuf.at[0, pl.ds(2, 2)], q_recv.at[1, c])
            dequantize_keys(c)
            far_sum, far_out_stat[c] = partial(c, 2)
            for j in range(2):
                far_out[c, j] = far_sum[j * half:(j + 1) * half].astype(bf16)
            start(sums(c))

            @pl.when(c == 1)
            def _():
                start(handover_far(0, c))

            near_sum, side_stat[c] = partial(c, 0)
            for j in range(2):
                side_sum[c, j] = near_sum[j * half:(j + 1) * half]

            @pl.when(c >= 1)
            def _():
                merge(c - 1)

        for c in range(2, pairs):
            start(handover(0, c, far_edge, 1))
        for c in range(2, pairs):
            start(handover(0, c, across, 1))
        for place in (across, far_edge):
            await_scales(place)
        merge(pairs - 1)
        wait_bytes(sbuf.at[0, 0], s_send.at[0])
        wait_bytes(sbuf.at[0], s_send.at[1])
        for flow in (1, 2):
            wait_bytes(qbuf.at[:, 0], q_send.at[flow])
        wait_bytes(meter, far_send.at[0])
        wait_bytes(result, r_send.at[0])
        wait_bytes(qbuf.at[:, 0], f_send.at[0])
        for slot in range(2):
            wait_bytes(qbuf.at[:, pl.ds(0, 2)], f_send.at[1 + slot])
        for place in (across, far_edge):
            wait_bytes(qbuf.at[:, 0], f_recv.at[place])


def _emit_kernel(att_ref, cache_ref, crope_ref, cscale_ref, att_out, cache_out, crope_out, cscale_out, sem):
    copies = []
    for c in range(cache_ref.shape[0]):
        copies.append(pltpu.make_async_copy(cache_ref.at[c], cache_out.at[c], sem.at[0]))
    for src, dst in ((att_ref, att_out), (crope_ref, crope_out), (cscale_ref, cscale_out)):
        copies.append(pltpu.make_async_copy(src, dst, sem.at[len(copies) - cache_ref.shape[0] + 1]))
    for copy in copies:
        copy.start()
    pltpu.make_async_copy(cache_ref, cache_out, sem.at[0]).wait()
    for copy in copies[cache_ref.shape[0]:]:
        copy.wait()


def emit(values):
    return pl.pallas_call(
        _emit_kernel,
        out_shape=[jax.ShapeDtypeStruct(v.shape, v.dtype) for v in values],
        in_specs=[pl.BlockSpec(memory_space=pl.ANY)] * 4,
        out_specs=[pl.BlockSpec(memory_space=pl.ANY)] * 4,
        scratch_shapes=[pltpu.SemaphoreType.DMA((4,))],
        compiler_params=pltpu.CompilerParams(vmem_limit_bytes=1 << 20),
    )(*values)


def per_device_line(
    latent_codes, latent_scales, rope_keys, lengths, query_latent, query_rope, new_latent, new_rope
):
    layers, requests, span, width = latent_codes.shape
    pairs, rows = layers * requests, span // 4
    rope, blocks = rope_keys.shape[-1], latent_scales.shape[-1]
    tokens, heads = query_latent.shape[2:4]
    half = tokens * heads
    tile_rows = -(-pairs * blocks // 16) * 16
    hbm_spec = pl.BlockSpec(memory_space=pltpu.HBM)
    vmem_spec = pl.BlockSpec(memory_space=pltpu.VMEM)
    dma = pltpu.SemaphoreType.DMA
    bf16, f32 = jnp.bfloat16, jnp.float32
    att, cache, crope, cscale = pl.pallas_call(
        _hub_kernel,
        out_shape=(
            pltpu.VMEM((pairs, half, width), bf16),
            pltpu.VMEM((pairs, span, width), bf16),
            pltpu.VMEM((pairs, rope, span), bf16),
            pltpu.VMEM((pairs, blocks, span), bf16),
        ),
        in_specs=[hbm_spec] * 8,
        out_specs=(vmem_spec,) * 4,
        scratch_shapes=[
            pltpu.SMEM(lengths.shape, lengths.dtype),
            pltpu.VMEM((span, span), bf16),
            pltpu.VMEM((2, pairs, 4, rows, width), bf16),
            pltpu.VMEM((2, pairs, 4, rope, rows), bf16),
            pltpu.VMEM((2, 4, tile_rows, rows), bf16),
            pltpu.VMEM((4, tile_rows, rows), bf16),
            pltpu.VMEM((2, pairs, 8, span), f32),
            pltpu.VMEM((pairs, span + rope, width), bf16),
            pltpu.VMEM((pairs, blocks, span), bf16),
            pltpu.VMEM((pairs, half, rope), bf16),
            pltpu.VMEM((pairs, 4, half + half * rope // width, width), bf16),
            pltpu.VMEM((pairs, 128, width), bf16),
            pltpu.VMEM((pairs, 128, rope), bf16),
            pltpu.VMEM((pairs, tokens, width), bf16),
            pltpu.VMEM((pairs, tokens, rope), bf16),
            pltpu.VMEM((2 * span, width), bf16),
            pltpu.VMEM((pairs, half, width), bf16),
            pltpu.VMEM((pairs, 2, half, width), f32),
            pltpu.VMEM((pairs, 4, 128), f32),
            pltpu.VMEM((pairs, 2, half, width), bf16),
            pltpu.VMEM((pairs, 4, 128), f32),
            pltpu.VMEM((pairs, 2, half, width), bf16),
            pltpu.VMEM((pairs, 4, 128), f32),
            pltpu.VMEM((pairs, half * width // 128 + 4, 128), f32),
            dma((1,)), dma((6,)), dma((3,)), dma((2, pairs)), dma((1,)), dma((pairs,)),
            dma((3,)), dma((4,)), dma((2,)), dma((5,)), dma((1,)), dma((pairs,)), dma((1,)), dma((1,)),
            pltpu.SemaphoreType.REGULAR, pltpu.SemaphoreType.REGULAR,
        ],
        compiler_params=pltpu.CompilerParams(
            collective_id=0, has_side_effects=True, vmem_limit_bytes=56 << 20
        ),
    )(
        lengths, latent_codes.reshape(pairs, span, width),
        rope_keys.transpose(0, 1, 3, 2).reshape(pairs, rope, span),
        latent_scales.transpose(0, 1, 3, 2).reshape(pairs, blocks, span),
        query_latent.reshape(pairs, half, width), query_rope.reshape(pairs, half, rope),
        new_latent.reshape(pairs, tokens, width), new_rope.reshape(pairs, tokens, rope),
    )

    att, cache, crope, cscale = emit((att, cache, crope, cscale))

    def as_cache(values):
        flipped = values.reshape(layers, requests, values.shape[1], span).transpose(0, 1, 3, 2)
        return flipped.reshape(layers, requests, span, 1, values.shape[1])

    return (
        att.reshape(query_latent.shape),
        cache.reshape(layers, requests, span, 1, width),
        as_cache(cscale),
        as_cache(crope),
    )


def solution(mesh):
    placed = (
        P(None, ("group", "req", "sub"), "seq", None),
        P(None, ("group", "req", "sub"), "seq", None),
        P(None, ("group", "req", "sub"), "seq", None),
        P(("group", "req", "sub")),
        P(None, ("group", "req", "sub"), None, "seq", None),
        P(None, ("group", "req", "sub"), None, "seq", None),
        P(None, ("group", "req", "sub"), None, None),
        P(None, ("group", "req", "sub"), None, None),
    )
    return jax.shard_map(
        per_device_line if mesh.shape["seq"] == 4 else per_device,
        mesh=mesh,
        in_specs=placed,
        out_specs=(
            P(None, ("group", "req", "sub"), None, "seq", None),
            P(None, ("group", "req", "sub"), None, "seq", None),
            P(None, ("group", "req", "sub"), None, "seq", None),
            P(None, ("group", "req", "sub"), None, "seq", None),
        ),
        check_vma=False,
    )
```

```python
import jax
import jax.numpy as jnp
from jax import lax
from jax.experimental import pallas as pl
from jax.experimental.pallas import tpu as pltpu
from jax.sharding import PartitionSpec as P

softmax_gain = 192.0 ** (-0.5)
masked_score = -1e30


def dequantize(code_values, scale_values):
    blocks = scale_values.shape[-1]
    latent_width = code_values.shape[-1]
    shaped = code_values.astype(jnp.float32).reshape(
        code_values.shape[:-1] + (blocks, latent_width // blocks)
    )
    scaled = shaped * scale_values.astype(jnp.float32)[..., None]
    return scaled.reshape(code_values.shape).astype(jnp.bfloat16)


def shard_partial(
    lat_query, rope_query, key_rows, rope_rows, usable, new_keys, new_rope_rows, holds_new
):
    tokens_new, head_count, latent_width = lat_query.shape
    query_rows = lat_query.reshape(tokens_new * head_count, latent_width)
    query_pos = rope_query.reshape(tokens_new * head_count, rope_query.shape[-1])
    scores = jnp.dot(query_rows, key_rows.T, preferred_element_type=jnp.float32)
    scores = (
        scores + jnp.dot(query_pos, rope_rows.T, preferred_element_type=jnp.float32)
    ) * softmax_gain
    fresh_scores = jnp.dot(query_rows, new_keys.T, preferred_element_type=jnp.float32)
    fresh_scores = (
        fresh_scores + jnp.dot(query_pos, new_rope_rows.T, preferred_element_type=jnp.float32)
    ) * softmax_gain
    token_of_row = jnp.arange(tokens_new * head_count, dtype=jnp.int32) // head_count
    causal = (jnp.arange(tokens_new, dtype=jnp.int32)[None, :] <= token_of_row[:, None]) & holds_new
    scores = jnp.where(usable[None, :], scores, masked_score)
    fresh_scores = jnp.where(causal, fresh_scores, masked_score)
    group_peak = jnp.maximum(jnp.max(scores, 1), jnp.max(fresh_scores, 1)).astype(jnp.bfloat16)
    peak_float = group_peak.astype(jnp.float32)[:, None]
    weights = jnp.where(usable[None, :], jnp.exp(scores - peak_float), 0.0).astype(jnp.bfloat16)
    fresh_weights = jnp.where(causal, jnp.exp(fresh_scores - peak_float), 0.0).astype(jnp.bfloat16)
    group_total = jnp.sum(weights.astype(jnp.float32), 1) + jnp.sum(
        fresh_weights.astype(jnp.float32), 1
    )
    group_sum = jnp.dot(weights, key_rows, preferred_element_type=jnp.float32)
    group_sum = group_sum + jnp.dot(fresh_weights, new_keys, preferred_element_type=jnp.float32)
    return (
        group_sum.astype(jnp.bfloat16).reshape(tokens_new, head_count, latent_width),
        group_peak.reshape(tokens_new, head_count),
        group_total.astype(jnp.bfloat16).reshape(tokens_new, head_count),
    )


def merge_groups(pieces):
    group_sum, group_peak, group_total = pieces
    peak_float = group_peak.astype(jnp.float32)
    overall = jnp.max(peak_float, 0)
    factor = jnp.exp(peak_float - overall)
    numerator = jnp.sum(factor[..., None] * group_sum.astype(jnp.float32), 0)
    denominator = jnp.sum(factor * group_total.astype(jnp.float32), 0)
    return (numerator / denominator[..., None]).astype(jnp.bfloat16)


def per_device(
    latent_codes, latent_scales, rope_keys, lengths, query_latent, query_rope, new_latent, new_rope
):
    shard_count = lax.axis_size("seq")
    seq_index = lax.axis_index("seq")
    layer_count, request_count, span, latent_width = latent_codes.shape
    lat_query, rope_query = (
        lax.all_gather(query_latent, "seq", axis=3, tiled=True),
        lax.all_gather(query_rope, "seq", axis=3, tiled=True),
    )

    def regroup_rows(values):
        return values.reshape(
            values.shape[0], values.shape[1], span // shard_count, shard_count, values.shape[-1]
        )

    codes_moved, scales_moved, rope_moved = (
        lax.all_to_all(regroup_rows(latent_codes), "seq", split_axis=3, concat_axis=2, tiled=True),
        lax.all_to_all(regroup_rows(latent_scales), "seq", split_axis=3, concat_axis=2, tiled=True),
        lax.all_to_all(regroup_rows(rope_keys), "seq", split_axis=3, concat_axis=2, tiled=True),
    )
    offsets = jnp.arange(span, dtype=jnp.int32)
    key_rows = dequantize(latent_codes, latent_scales)
    positions = seq_index * span + offsets
    usable = positions[None, :] < lengths[:, None]
    holds_new = seq_index == 0
    per_request = jax.vmap(shard_partial, in_axes=(0, 0, 0, 0, 0, 0, 0, None))
    per_layer = jax.vmap(per_request, in_axes=(0, 0, 0, 0, None, 0, 0, None))
    group_sum, group_peak, group_total = per_layer(
        lat_query, rope_query, key_rows, rope_keys, usable, new_latent, new_rope, holds_new
    )
    attended = merge_groups(
        (
            lax.all_to_all(group_sum[None], "seq", split_axis=4, concat_axis=0, tiled=True),
            lax.all_to_all(group_peak[None], "seq", split_axis=4, concat_axis=0, tiled=True),
            lax.all_to_all(group_total[None], "seq", split_axis=4, concat_axis=0, tiled=True),
        )
    )
    return (attended, codes_moved, scales_moved, rope_moved)


def _hub_kernel(
    len_ref, codes_ref, rope_ref, scale_ref, q_ref, qr_ref, new_ref, newr_ref,
    att_ref, cache_ref, crope_ref, cscale_ref,
    lengths, perm, kbuf, abuf, sbuf, scale_in, scale_rows, raw, raws, rawq, qbuf, nkbuf, nrbuf,
    new_rows, newr_rows, keys, result, side_sum, side_stat, far_out, far_out_stat, far_in, far_in_stat,
    meter, load_sem, misc_sem, q_send, q_recv, k_send, k_recv, f_send, f_recv, s_send, s_recv,
    far_send, far_recv, r_send, r_recv, edge_in, far_edge_in,
):
    pairs, span, width = codes_ref.shape
    groups = 4
    rows = span // groups
    half = q_ref.shape[1]
    rope = qr_ref.shape[2]
    blocks = scale_ref.shape[1]
    fresh = new_ref.shape[1]
    heads = half // fresh
    fold = half * rope // width
    me = lax.axis_index("seq")
    is_hub = (me == 1) | (me == 2)
    is_edge = jnp.logical_not(is_hub)
    hub = 1 + me // 2
    edge = me // 2 * 3
    across = 3 - hub
    far_edge = 3 - edge
    f32, bf16 = jnp.float32, jnp.bfloat16

    def start(copies):
        for copy in copies:
            copy.start()

    def remote(src, dst, send, recv, target):
        return pltpu.make_async_remote_copy(
            src_ref=src, dst_ref=dst, send_sem=send, recv_sem=recv,
            device_id={"seq": target}, device_id_type=pl.DeviceIdType.MESH,
        )

    def greet(target):
        pl.semaphore_signal(
            pltpu.get_barrier_semaphore(), inc=1, device_id={"seq": target},
            device_id_type=pl.DeviceIdType.MESH,
        )

    def tell(sem, target):
        pl.semaphore_signal(sem, inc=1, device_id={"seq": target}, device_id_type=pl.DeviceIdType.MESH)

    def wait_bytes(ref, sem):
        pltpu.make_async_copy(ref, ref, sem).wait()

    def load(c):
        return (
            pltpu.make_async_copy(codes_ref.at[c], raw.at[c, pl.ds(0, span)], load_sem.at[0]),
            pltpu.make_async_copy(rope_ref.at[c], raw.at[c, pl.ds(span, rope)], load_sem.at[0]),
        )

    load_scales = pltpu.make_async_copy(scale_ref, raws, misc_sem.at[0])
    load_rotary = pltpu.make_async_copy(qr_ref, rawq, misc_sem.at[1])
    load_query = pltpu.make_async_copy(q_ref, qbuf.at[:, 0, pl.ds(0, half)], misc_sem.at[2])
    load_new = (
        pltpu.make_async_copy(new_ref, new_rows, misc_sem.at[3]),
        pltpu.make_async_copy(newr_ref, newr_rows, misc_sem.at[4]),
    )
    load_lengths = pltpu.make_async_copy(len_ref, lengths, misc_sem.at[5])

    def query_latent(c, flow, dst, target):
        return remote(q_ref.at[c], qbuf.at[c, dst, pl.ds(0, half)],
                      q_send.at[flow], q_recv.at[flow, c], target)

    def query_rotary(c, flow, dst, target):
        return remote(qbuf.at[c, 0, pl.ds(half, fold)], qbuf.at[c, dst, pl.ds(half, fold)],
                      q_send.at[flow], q_recv.at[flow, c], target)

    def forward_query(c):
        return remote(qbuf.at[c, 1], qbuf.at[c, 3], q_send.at[2], q_recv.at[1, c], across)

    def shard(c):
        return (
            remote(abuf.at[0, c], abuf.at[1, c], k_send.at[0], k_recv.at[c], hub),
            remote(kbuf.at[0, c], kbuf.at[1, c], k_send.at[0], k_recv.at[c], hub),
        )

    shard_scales = remote(sbuf.at[0], sbuf.at[1], s_send.at[0], s_recv.at[groups], hub)

    def place_of(slot):
        return hub if slot == 0 else edge

    def handover(slot, c, target, send):
        place = place_of(slot)
        spot = pl.multiple_of(place * rows, rows)
        return (
            remote(kbuf.at[slot, c, target], cache_ref.at[c, pl.ds(spot, rows)],
                   f_send.at[send], f_recv.at[place], target),
            remote(abuf.at[slot, c, target], crope_ref.at[c, :, pl.ds(spot, rows)],
                   f_send.at[send], f_recv.at[place], target),
        )

    def handover_far(slot, c):
        return handover(slot, c, far_edge, 1 + slot) + handover(slot, c, across, 1 + slot)

    def handover_scales(slot, target, send):
        return remote(sbuf.at[slot, target], scale_in.at[place_of(slot)],
                      s_send.at[send], s_recv.at[place_of(slot)], target)

    def keep_scales(tile, place):
        values = tile.astype(f32)
        for c in range(pairs):
            cscale_ref[c, :, pl.ds(pl.multiple_of(place * rows, rows), rows)] = (
                values[c * blocks:(c + 1) * blocks].astype(bf16)
            )

    def await_scales(place):
        wait_bytes(scale_in.at[place], s_recv.at[place])
        keep_scales(scale_in[place], place)

    def keep(slot, c, place):
        spot = pl.multiple_of(place * rows, rows)
        cache_ref[c, pl.ds(spot, rows), :] = kbuf[slot, c, me]
        crope_ref[c, :, pl.ds(spot, rows)] = abuf[slot, c, me]

    def sums(c):
        return (
            remote(far_out.at[c], far_in.at[c], far_send.at[0], far_recv.at[c], across),
            remote(far_out_stat.at[c], far_in_stat.at[c], far_send.at[0], far_recv.at[c], across),
        )

    def edge_result(c):
        return remote(result.at[c], att_ref.at[c], r_send.at[0], r_recv.at[0], edge)

    @pl.when(is_hub)
    def _():
        greet(across)
        greet(edge)

    load_rotary.start()

    @pl.when(is_hub)
    def _():
        pl.semaphore_wait(pltpu.get_barrier_semaphore(), 1)
        for c in range(pairs):
            query_latent(c, 1, 2, across).start()
        load_query.start()
        start(load_new)

    @pl.when(is_edge)
    def _():
        pl.semaphore_wait(pltpu.get_barrier_semaphore(), 1)
        tell(edge_in, hub)
        query_latent(0, 0, 1, hub).start()

    load_scales.start()
    for c in range(pairs):
        start(load(c))
    load_lengths.start()
    load_rotary.wait()
    for c in range(pairs):
        qbuf[c, 0, half:half + fold, :] = jnp.concatenate(
            [rawq[c, i * fold:(i + 1) * fold, :] for i in range(half // fold)], axis=1
        )

    @pl.when(is_hub)
    def _():
        for c in range(pairs):
            query_rotary(c, 1, 2, across).start()

    @pl.when(is_edge)
    def _():
        query_rotary(0, 0, 1, hub).start()

    line = lax.broadcasted_iota(jnp.int32, (span, span), 0)
    column = lax.broadcasted_iota(jnp.int32, (span, span), 1)
    perm[...] = jnp.where(column == (line % rows) * groups + line // rows, 1.0, 0.0).astype(bf16)
    dims = (((1,), (1,)), ((), ()))

    tile_rows = sbuf.shape[2]
    load_scales.wait()
    load_lengths.wait()
    wait_bytes(raw, load_sem.at[0])
    stacked = [raws[c].astype(f32) for c in range(pairs)]
    if tile_rows > pairs * blocks:
        stacked.append(jnp.zeros((tile_rows - pairs * blocks, span), f32))
    stacked = jnp.concatenate(stacked, axis=0).astype(bf16)
    sorted_scales = lax.dot_general(stacked, perm[...], dims, preferred_element_type=f32)
    for k in range(groups):
        sbuf[0, k] = sorted_scales[:, k * rows:(k + 1) * rows].astype(bf16)
    keep_scales(sbuf[0, me], me)

    def spread_scales(slot):
        scale_rows[slot] = jnp.zeros(scale_rows.shape[1:], f32)
        for k in range(groups):
            values = sbuf[slot, k].astype(f32)
            for c in range(pairs):
                scale_rows[slot, c, 0:blocks, k * rows:(k + 1) * rows] = (
                    values[c * blocks:(c + 1) * blocks]
                )

    def prepare(c):
        sorted_codes = jnp.dot(perm[...], raw[c, 0:span], preferred_element_type=f32)
        for k in range(groups):
            kbuf[0, c, k] = sorted_codes[k * rows:(k + 1) * rows].astype(bf16)
        sorted_rope = lax.dot_general(raw[c, span:span + rope], perm[...], dims, preferred_element_type=f32)
        for k in range(groups):
            abuf[0, c, k] = sorted_rope[:, k * rows:(k + 1) * rows].astype(bf16)

    def stats_of(m, d):
        lane = lax.broadcasted_iota(jnp.int32, (half, 128), 1)
        return jnp.where(
            lane < 2, jnp.where(lane == 0, m[:half], d[:half]), jnp.where(lane == 2, m[half:], d[half:])
        ).T[0:4]

    def columns_of(stat, j):
        return stat[:, 2 * j:2 * j + 1], stat[:, 2 * j + 1:2 * j + 2]

    def dequantize_keys(c):
        for slot in range(2):
            scales = scale_rows[slot, c].T
            for k in range(groups):
                for b in range(blocks):
                    lanes = slice(b * (width // blocks), (b + 1) * (width // blocks))
                    keys[slot * span + k * rows:slot * span + (k + 1) * rows, lanes] = (
                        kbuf[slot, c, k, :, lanes].astype(f32)
                        * scales[k * rows:(k + 1) * rows, b:b + 1]
                    ).astype(bf16)

    def partial(c, first):
        q = qbuf[c, first:first + 2, 0:half, :].reshape(2 * half, width)
        qr = jnp.concatenate(
            [
                qbuf[c, first + j, half:half + fold, i * rope:(i + 1) * rope]
                for j in range(2) for i in range(half // fold)
            ],
            axis=0,
        )
        ropes = jnp.concatenate(
            [abuf[slot, c, k] for slot in range(2) for k in range(groups)], axis=1
        )
        s = lax.dot_general(q, keys[...], dims, preferred_element_type=f32)
        s = (s + jnp.dot(qr, ropes, preferred_element_type=f32)) * softmax_gain
        column = lax.broadcasted_iota(jnp.int32, (1, 2 * span), 1)
        local = column % span
        position = jnp.where(column < span, hub, edge) * span + local % rows * groups + local // rows
        s = jnp.where(position < lengths[c % lengths.shape[0]], s, masked_score)
        m = jnp.max(s, axis=1, keepdims=True)
        if first == 0:
            t = lax.dot_general(q, nkbuf[c], dims, preferred_element_type=f32)
            t = (t + lax.dot_general(qr, nrbuf[c], dims, preferred_element_type=f32)) * softmax_gain
            token = lax.broadcasted_iota(jnp.int32, t.shape, 0) % half // heads
            t = jnp.where(lax.broadcasted_iota(jnp.int32, t.shape, 1) <= token, t, masked_score)
            m = jnp.maximum(m, jnp.max(t, axis=1, keepdims=True))
        w = jnp.exp(s - m).astype(bf16)
        d = jnp.sum(w.astype(f32), axis=1, keepdims=True)
        n = jnp.dot(w, keys[...], preferred_element_type=f32)
        if first == 0:
            v = jnp.exp(t - m).astype(bf16)
            d = d + jnp.sum(v.astype(f32), axis=1, keepdims=True)
            n = n + jnp.dot(v, nkbuf[c], preferred_element_type=f32)
        return n, stats_of(m, d)

    def merge(c):
        wait_bytes(meter.at[c], far_recv.at[c])
        pad = jnp.zeros((4, 128), f32)
        side = jnp.concatenate([side_stat[c], pad], axis=0).T
        far = jnp.concatenate([far_in_stat[c], pad], axis=0).T
        for j in (1, 0):
            m0, d0 = columns_of(side, j)
            m1, d1 = columns_of(far, j)
            m = jnp.maximum(m0, m1)
            f0, f1 = jnp.exp(m0 - m), jnp.exp(m1 - m)
            numerator = f0 * side_sum[c, j] + f1 * far_in[c, j].astype(f32)
            merged = (numerator / (f0 * d0 + f1 * d1)).astype(bf16)
            if j == 1:
                result[c] = merged
                edge_result(c).start()
            else:
                att_ref[c] = merged

    @pl.when(is_edge)
    def _():
        shard_scales.start()

        @pl.loop(0, pairs)
        def _(c):
            prepare(c)

            @pl.when(c >= 1)
            def _():
                wait_bytes(raw.at[0], k_send.at[0])
                start((query_latent(c, 0, 1, hub), query_rotary(c, 0, 1, hub)))

            start(shard(c))
            keep(0, c, me)

        wait_bytes(raw.at[0], k_send.at[0])
        shard_scales.wait_send()
        wait_bytes(qbuf.at[:, 0], q_send.at[0])
        for place in (hub, across, far_edge):
            await_scales(place)
        for place in (hub, across, far_edge):
            wait_bytes(qbuf.at[:, 0], f_recv.at[place])
        wait_bytes(att_ref, r_recv.at[0])

    @pl.when(is_hub)
    def _():
        pl.semaphore_wait(edge_in, 1)
        tell(far_edge_in, across)
        handover_scales(0, edge, 0).start()

        @pl.loop(0, pairs)
        def _(c):
            prepare(c)
            start(handover(0, c, edge, 0))
            keep(0, c, me)

        pl.semaphore_wait(far_edge_in, 1)
        for target in (across, far_edge):
            handover_scales(0, target, 1).start()
        wait_bytes(qbuf.at[0, 1], q_recv.at[0, 0])
        forward_query(0).start()
        start(handover_far(0, 0))
        for copy in load_new:
            copy.wait()
        nkbuf[...] = jnp.zeros(nkbuf.shape, bf16)
        nrbuf[...] = jnp.zeros(nrbuf.shape, bf16)
        for c in range(pairs):
            nkbuf[c, 0:fresh, :] = new_rows[c]
            nrbuf[c, 0:fresh, :] = newr_rows[c]
        load_query.wait()
        spread_scales(0)
        shard_scales.wait_recv()
        for target in (across, far_edge):
            handover_scales(1, target, 1).start()
        keep_scales(sbuf[1, me], edge)
        spread_scales(1)

        @pl.loop(0, pairs)
        def _(c):
            wait_bytes(raw.at[0], k_recv.at[c])
            start(handover(1, c, far_edge, 2))
            keep(1, c, edge)

            @pl.when(c < pairs - 1)
            def _():
                wait_bytes(qbuf.at[0, 1], q_recv.at[0, c + 1])
                forward_query(c + 1).start()

            wait_bytes(qbuf.at[0, pl.ds(2, 2)], q_recv.at[1, c])
            dequantize_keys(c)
            far_sum, far_out_stat[c] = partial(c, 2)
            for j in range(2):
                far_out[c, j] = far_sum[j * half:(j + 1) * half].astype(bf16)
            start(sums(c))

            @pl.when(c == 1)
            def _():
                start(handover_far(0, c))

            start(handover(1, c, across, 2))
            near_sum, side_stat[c] = partial(c, 0)
            for j in range(2):
                side_sum[c, j] = near_sum[j * half:(j + 1) * half]

            @pl.when(c >= 1)
            def _():
                merge(c - 1)

        for c in range(2, pairs):
            start(handover(0, c, far_edge, 1))
        for c in range(2, pairs):
            start(handover(0, c, across, 1))
        for place in (across, far_edge):
            await_scales(place)
        merge(pairs - 1)
        wait_bytes(sbuf.at[0, 0], s_send.at[0])
        wait_bytes(sbuf.at[0], s_send.at[1])
        for flow in (1, 2):
            wait_bytes(qbuf.at[:, 0], q_send.at[flow])
        wait_bytes(meter, far_send.at[0])
        wait_bytes(result, r_send.at[0])
        wait_bytes(qbuf.at[:, 0], f_send.at[0])
        for slot in range(2):
            wait_bytes(qbuf.at[:, pl.ds(0, 2)], f_send.at[1 + slot])
        for place in (across, far_edge):
            wait_bytes(qbuf.at[:, 0], f_recv.at[place])


def _emit_kernel(att_ref, cache_ref, crope_ref, cscale_ref, att_out, cache_out, crope_out, cscale_out, sem):
    copies = []
    for c in range(cache_ref.shape[0]):
        copies.append(pltpu.make_async_copy(cache_ref.at[c], cache_out.at[c], sem.at[len(copies)]))
    for src, dst in ((att_ref, att_out), (crope_ref, crope_out), (cscale_ref, cscale_out)):
        copies.append(pltpu.make_async_copy(src, dst, sem.at[len(copies)]))
    for copy in copies:
        copy.start()
    for copy in copies:
        copy.wait()


def emit(values):
    return pl.pallas_call(
        _emit_kernel,
        out_shape=[jax.ShapeDtypeStruct(v.shape, v.dtype) for v in values],
        in_specs=[pl.BlockSpec(memory_space=pl.ANY)] * 4,
        out_specs=[pl.BlockSpec(memory_space=pl.ANY)] * 4,
        scratch_shapes=[pltpu.SemaphoreType.DMA((values[1].shape[0] + 3,))],
        compiler_params=pltpu.CompilerParams(vmem_limit_bytes=1 << 20),
    )(*values)


def per_device_line(
    latent_codes, latent_scales, rope_keys, lengths, query_latent, query_rope, new_latent, new_rope
):
    layers, requests, span, width = latent_codes.shape
    pairs, rows = layers * requests, span // 4
    rope, blocks = rope_keys.shape[-1], latent_scales.shape[-1]
    tokens, heads = query_latent.shape[2:4]
    half = tokens * heads
    tile_rows = -(-pairs * blocks // 16) * 16
    hbm_spec = pl.BlockSpec(memory_space=pltpu.HBM)
    vmem_spec = pl.BlockSpec(memory_space=pltpu.VMEM)
    dma = pltpu.SemaphoreType.DMA
    bf16, f32 = jnp.bfloat16, jnp.float32
    att, cache, crope, cscale = pl.pallas_call(
        _hub_kernel,
        out_shape=(
            pltpu.VMEM((pairs, half, width), bf16),
            pltpu.VMEM((pairs, span, width), bf16),
            pltpu.VMEM((pairs, rope, span), bf16),
            pltpu.VMEM((pairs, blocks, span), bf16),
        ),
        in_specs=[hbm_spec] * 8,
        out_specs=(vmem_spec,) * 4,
        scratch_shapes=[
            pltpu.SMEM(lengths.shape, lengths.dtype),
            pltpu.VMEM((span, span), bf16),
            pltpu.VMEM((2, pairs, 4, rows, width), bf16),
            pltpu.VMEM((2, pairs, 4, rope, rows), bf16),
            pltpu.VMEM((2, 4, tile_rows, rows), bf16),
            pltpu.VMEM((4, tile_rows, rows), bf16),
            pltpu.VMEM((2, pairs, 8, span), f32),
            pltpu.VMEM((pairs, span + rope, width), bf16),
            pltpu.VMEM((pairs, blocks, span), bf16),
            pltpu.VMEM((pairs, half, rope), bf16),
            pltpu.VMEM((pairs, 4, half + half * rope // width, width), bf16),
            pltpu.VMEM((pairs, 128, width), bf16),
            pltpu.VMEM((pairs, 128, rope), bf16),
            pltpu.VMEM((pairs, tokens, width), bf16),
            pltpu.VMEM((pairs, tokens, rope), bf16),
            pltpu.VMEM((2 * span, width), bf16),
            pltpu.VMEM((pairs, half, width), bf16),
            pltpu.VMEM((pairs, 2, half, width), f32),
            pltpu.VMEM((pairs, 4, 128), f32),
            pltpu.VMEM((pairs, 2, half, width), bf16),
            pltpu.VMEM((pairs, 4, 128), f32),
            pltpu.VMEM((pairs, 2, half, width), bf16),
            pltpu.VMEM((pairs, 4, 128), f32),
            pltpu.VMEM((pairs, half * width // 128 + 4, 128), f32),
            dma((1,)), dma((6,)), dma((3,)), dma((2, pairs)), dma((1,)), dma((pairs,)),
            dma((3,)), dma((4,)), dma((2,)), dma((5,)), dma((1,)), dma((pairs,)), dma((1,)), dma((1,)),
            pltpu.SemaphoreType.REGULAR, pltpu.SemaphoreType.REGULAR,
        ],
        compiler_params=pltpu.CompilerParams(
            collective_id=0, has_side_effects=True, vmem_limit_bytes=56 << 20
        ),
    )(
        lengths, latent_codes.reshape(pairs, span, width),
        rope_keys.transpose(0, 1, 3, 2).reshape(pairs, rope, span),
        latent_scales.transpose(0, 1, 3, 2).reshape(pairs, blocks, span),
        query_latent.reshape(pairs, half, width), query_rope.reshape(pairs, half, rope),
        new_latent.reshape(pairs, tokens, width), new_rope.reshape(pairs, tokens, rope),
    )

    att, cache, crope, cscale = emit((att, cache, crope, cscale))

    def as_cache(values):
        flipped = values.reshape(layers, requests, values.shape[1], span).transpose(0, 1, 3, 2)
        return flipped.reshape(layers, requests, span, 1, values.shape[1])

    return (
        att.reshape(query_latent.shape),
        cache.reshape(layers, requests, span, 1, width),
        as_cache(cscale),
        as_cache(crope),
    )


def solution(mesh):
    placed = (
        P(None, ("group", "req", "sub"), "seq", None),
        P(None, ("group", "req", "sub"), "seq", None),
        P(None, ("group", "req", "sub"), "seq", None),
        P(("group", "req", "sub")),
        P(None, ("group", "req", "sub"), None, "seq", None),
        P(None, ("group", "req", "sub"), None, "seq", None),
        P(None, ("group", "req", "sub"), None, None),
        P(None, ("group", "req", "sub"), None, None),
    )
    return jax.shard_map(
        per_device_line if mesh.shape["seq"] == 4 else per_device,
        mesh=mesh,
        in_specs=placed,
        out_specs=(
            P(None, ("group", "req", "sub"), None, "seq", None),
            P(None, ("group", "req", "sub"), None, "seq", None),
            P(None, ("group", "req", "sub"), None, "seq", None),
            P(None, ("group", "req", "sub"), None, "seq", None),
        ),
        check_vma=False,
    )
```
